32 devices in a mesh: dp: 16 (over z, y, core), pair: 2 (over x).
Axes of the slice: x: 2, y: 2, z: 4, core: 2. Of those that a mesh axis runs over, the one named last changes fastest.
Arguments:
- latents: bfloat16 [64, 256, 768], P(('dp', 'pair')), may hold values from -6 to 6
- conditioning: bfloat16 [64, 768], P(('dp', 'pair')), may hold values from -6 to 6
- cotangent: bfloat16 [64, 256, 768], P(('dp', 'pair')), may hold values from -6 to 6
- adaln_weight: bfloat16 [2, 768, 4608], P(None, ('dp', 'pair')), may hold values from -0.21875 to 0.21875
- adaln_bias: bfloat16 [2, 4608], P(None, ('dp', 'pair')), may hold values from -3 to 3
- qkv_weight: bfloat16 [2, 768, 2304], P(None, ('dp', 'pair')), may hold values from -0.21875 to 0.21875
- query_bias: bfloat16 [2, 768], P(None, ('dp', 'pair')), may hold values from -3 to 3
- value_bias: bfloat16 [2, 768], P(None, ('dp', 'pair')), may hold values from -3 to 3
- proj_weight: bfloat16 [2, 768, 768], P(None, ('dp', 'pair')), may hold values from -0.875 to 0.875
- proj_bias: bfloat16 [2, 768], P(None, ('dp', 'pair')), may hold values from -3 to 3
- expand_weight: bfloat16 [2, 768, 3072], P(None, ('dp', 'pair')), may hold values from -0.21875 to 0.21875
- expand_bias: bfloat16 [2, 3072], P(None, ('dp', 'pair')), may hold values from -3 to 3
- reduce_weight: bfloat16 [2, 3072, 768], P(None, ('dp', 'pair')), may hold values from -0.109375 to 0.109375
- reduce_bias: bfloat16 [2, 768], P(None, ('dp', 'pair')), may hold values from -3 to 3
Outputs:
- outputs: bfloat16 [64, 256, 768], P(('dp', 'pair'))
- grad_latents: float32 [64, 256, 768], P(('dp', 'pair'))
- grad_conditioning: float32 [64, 768], P(('dp', 'pair'))
- grad_adaln_weight: float32 [2, 768, 4608], P(None, ('dp', 'pair'))
- grad_adaln_bias: float32 [2, 4608], P(None, ('dp', 'pair'))
- grad_qkv_weight: float32 [2, 768, 2304], P(None, ('dp', 'pair'))
- grad_query_bias: float32 [2, 768], P(None, ('dp', 'pair'))
- grad_value_bias: float32 [2, 768], P(None, ('dp', 'pair'))
- grad_proj_weight: float32 [2, 768, 768], P(None, ('dp', 'pair'))
- grad_proj_bias: float32 [2, 768], P(None, ('dp', 'pair'))
- grad_expand_weight: float32 [2, 768, 3072], P(None, ('dp', 'pair'))
- grad_expand_bias: float32 [2, 3072], P(None, ('dp', 'pair'))
- grad_reduce_weight: float32 [2, 3072, 768], P(None, ('dp', 'pair'))
- grad_reduce_bias: float32 [2, 768], P(None, ('dp', 'pair'))
The draws below stay inside these ranges and needn't reach their ends.
All inputs are finite; a program needn't handle non-finite values.
Results may differ from the reference program's by a relative error of at most 0.025.
The reference program's roundings to bfloat16 on the way count: a program that leaves them out, or rounds other values in their place, can miss the bound.
Values may be sent and summed in bfloat16 or wider, within the bound.
A program may use at most 256 MiB of HBM per device.

```python
import math
import jax
import jax.numpy as jnp
from jax import lax

D = 768
HEADS = 12
HEAD = 64
FF = 3072
SEQ = 256
LAYERS = 2
LATENTS = 64


def spiked(drawn, stream_key, source, target, blocks, factor):
    def block_of(axis_at):
        return (jnp.arange(drawn.shape[axis_at]) // (drawn.shape[axis_at] // blocks)).reshape((-1,) + (1,) * (drawn.ndim - 1 - axis_at))

    one_side = jax.random.permutation(stream_key, blocks)[block_of(target)]
    other_side = (block_of(target) + blocks // 2) % blocks
    return jnp.where((block_of(source) == one_side) | (block_of(source) == other_side), factor * drawn, drawn)


def block_levels(stream_key, shape, shards, low, high):
    gain = 1.0
    for position, blocks in shards:
        heights = jax.random.uniform(jax.random.fold_in(jax.random.fold_in(stream_key, 6), position), (blocks,), jnp.float32, low / len(shards), high / len(shards))
        gain = gain * jnp.repeat(jnp.exp(heights), shape[position] // blocks).reshape((-1,) + (1,) * (len(shape) - 1 - position))
    return gain


def noise(key, extent, scale, limit, cuts=(), dtype=jnp.bfloat16):
    values = jax.random.normal(key, extent, jnp.float32) * scale
    if len(cuts) > 0:
        values = block_levels(key, extent, cuts, -0.22, 0.18) * values
    return jnp.clip(values, min=-limit, max=limit).astype(dtype)


def noise_with(rng, extent, deviation, reach, shards, heavy, held_as=jnp.bfloat16):
    array = deviation * jax.random.normal(rng, extent, jnp.float32)
    if shards:
        array = array * block_levels(rng, extent, shards, -0.22, 0.18)
    return jnp.clip(spiked(array, jax.random.fold_in(rng, 3), *heavy), -reach, reach).astype(held_as)


def setup_inputs(seed: int = 0) -> dict:
    seeds = jax.random.split(jax.random.key(seed), 15)
    return {
        "latents": noise(seeds[0], (LATENTS, SEQ, D), 1.0, 6.0, ((0, 32),)),
        "conditioning": noise(seeds[1], (LATENTS, D), 1.0, 6.0, ((0, 32),)),
        "cotangent": noise_with(seeds[2], (LATENTS, SEQ, D), 1.0, 6.0, ((0, 32),), (0, 2, 32, 2.75)),
        "adaln_weight": noise(seeds[3], (LAYERS, D, 6 * D), D ** -0.5, 0.21875, ((1, 32),)),
        "adaln_bias": noise(seeds[4], (LAYERS, 6 * D), 0.5, 3.0, ((1, 32),)),
        "qkv_weight": noise(seeds[5], (LAYERS, D, 3 * D), D ** -0.5, 0.21875, ((1, 32),)),
        "query_bias": noise(seeds[6], (LAYERS, D), 0.5, 3.0, ((1, 32),)),
        "value_bias": noise(seeds[7], (LAYERS, D), 0.5, 3.0, ((1, 32),)),
        "proj_weight": noise(seeds[8], (LAYERS, D, D), (D // 16) ** -0.5, 0.875, ((1, 32),)),
        "proj_bias": noise(seeds[9], (LAYERS, D), 0.5, 3.0, ((1, 32),)),
        "expand_weight": noise(seeds[10], (LAYERS, D, FF), D ** -0.5, 0.21875, ((1, 32),)),
        "expand_bias": noise(seeds[11], (LAYERS, FF), 0.5, 3.0, ((1, 32),)),
        "reduce_weight": noise(seeds[12], (LAYERS, FF, D), FF ** -0.5, 0.109375, ((1, 32),)),
        "reduce_bias": noise(seeds[13], (LAYERS, D), 0.5, 3.0, ((1, 32),)),
    }


PRECISE = lax.Precision.HIGHEST
EPSILON = 1e-06

@jax.custom_vjp
def low(v):
    return lax.optimization_barrier(v.astype(jnp.bfloat16)).astype(jnp.float32)

@jax.custom_vjp
def low_back(v):
    return v

def low_keep(v):
    return (low(v), None)

def low_pass(kept, grad):
    return (grad,)

def back_keep(v):
    return (v, None)

def back_low(kept, grad):
    return (low(grad),)
low.defvjp(low_keep, low_pass)
low_back.defvjp(back_keep, back_low)

def layer_norm(values):
    centre = values - lax.optimization_barrier(jnp.mean(values, axis=-1, keepdims=True))
    spread = lax.optimization_barrier(jnp.mean(centre * centre, axis=-1, keepdims=True))
    return centre * lax.rsqrt(spread + EPSILON)

def matmul(left, right):
    return jnp.dot(left, right, precision=PRECISE, preferred_element_type=jnp.float32)

def diffusion_transformer_block(residual_state, condition_vector, parameters):
    adaln_weight, adaln_bias, qkv_weight, query_bias, value_bias, proj_weight, proj_bias, expand_weight, expand_bias, reduce_weight, reduce_bias = parameters
    groups, length, width = residual_state.shape
    silu_low = low(jax.nn.silu(condition_vector))
    modulation = low_back(matmul(silu_low, adaln_weight) + adaln_bias)
    pieces = [piece[:, None, :] for piece in jnp.split(modulation, 6, axis=-1)]
    shift_attn, scale_attn, gate_attn, shift_mlp, scale_mlp, gate_mlp = pieces
    normed_in = low(layer_norm(residual_state) * (1.0 + scale_attn) + shift_attn)
    qkv_bias = jnp.concatenate([query_bias, jnp.zeros_like(query_bias), value_bias])
    qkv_rows = low(low_back(matmul(normed_in, qkv_weight) + qkv_bias))
    qkv_rows = qkv_rows.reshape(groups, length, 3, HEADS, HEAD)
    scores = low_back(jnp.einsum('gqhe,gkhe->ghqk', qkv_rows[:, :, 0], qkv_rows[:, :, 1], precision=PRECISE) * HEAD ** (-0.5))
    top_score = lax.optimization_barrier(jnp.max(scores, axis=-1, keepdims=True))
    weights_exp = jnp.exp(scores - top_score)
    probs = weights_exp / lax.optimization_barrier(jnp.sum(weights_exp, axis=-1, keepdims=True))
    attended = jnp.einsum('ghqk,gkhe->gqhe', low(probs), qkv_rows[:, :, 2], precision=PRECISE)
    attended = low(low_back(attended.reshape(groups, length, width)))
    attn_out = low_back(matmul(attended, proj_weight) + proj_bias)
    middle = residual_state + gate_attn * attn_out
    normed_mid = low(layer_norm(middle) * (1.0 + scale_mlp) + shift_mlp)
    pre_act = low_back(matmul(normed_mid, expand_weight) + expand_bias)
    activated = low(jax.nn.gelu(pre_act, approximate=True))
    mlp_out = low_back(matmul(activated, reduce_weight) + reduce_bias)
    return middle + gate_mlp * mlp_out

def group_forward(parameters, latent_group, condition_group):
    residual_state = latent_group
    for layer_number in range(LAYERS):
        residual_state = diffusion_transformer_block(residual_state, condition_group, tuple((weight_matrix[layer_number] for weight_matrix in parameters)))
    return residual_state

def whole_forward(latent_all, cond_all, parameters):
    group_size = math.gcd(LATENTS, max(1, 4096 // SEQ))
    group_count = LATENTS // group_size
    latent_groups = latent_all.reshape(group_count, group_size, SEQ, D)
    cond_groups = cond_all.reshape(group_count, group_size, D)
    checked = jax.checkpoint(group_forward)

    def step_fn(carry, inputs):
        return (carry, checked(parameters, inputs[0], inputs[1]))
    _, results = lax.scan(step_fn, jnp.int32(0), (latent_groups, cond_groups))
    return results.reshape(LATENTS, SEQ, D)

def reference(latents, conditioning, cotangent, adaln_weight, adaln_bias, qkv_weight, query_bias, value_bias, proj_weight, proj_bias, expand_weight, expand_bias, reduce_weight, reduce_bias):
    parameters = (adaln_weight.astype(jnp.float32), adaln_bias.astype(jnp.float32), qkv_weight.astype(jnp.float32), query_bias.astype(jnp.float32), value_bias.astype(jnp.float32), proj_weight.astype(jnp.float32), proj_bias.astype(jnp.float32), expand_weight.astype(jnp.float32), expand_bias.astype(jnp.float32), reduce_weight.astype(jnp.float32), reduce_bias.astype(jnp.float32))
    outputs, pull = jax.vjp(whole_forward, latents.astype(jnp.float32), conditioning.astype(jnp.float32), parameters)
    grad_latents, grad_conditioning, grads = pull(cotangent.astype(jnp.float32))
    return (outputs.astype(jnp.bfloat16), grad_latents, grad_conditioning, grads[0], grads[1], grads[2], grads[3], grads[4], grads[5], grads[6], grads[7], grads[8], grads[9], grads[10])
```

```python
import functools

import jax
import jax.numpy as jnp
from jax import lax
from jax.experimental import pallas as pl
from jax.experimental.pallas import tpu as pltpu
from jax.sharding import PartitionSpec as P

HEADS = 12
HEAD = 64
LAYERS = 2


EPSILON = 1e-06


def layer_norm(values):
    centre = values - jnp.mean(values, axis=-1, keepdims=True)
    spread = jnp.mean(centre * centre, axis=-1, keepdims=True)
    return centre * lax.rsqrt(spread + EPSILON)


def modulate(residual_state, shift, scale):
    return layer_norm(residual_state) * (1.0 + scale[:, None, :]) + shift[:, None, :]


def gelu_tanh(values):
    return jax.nn.gelu(values, approximate=True)


AXES = ("dp", "pair")
LANES = 128
GRAD_DTYPE = jnp.bfloat16


MESH_ID = pl.DeviceIdType.MESH
BIAS_TILE = (16, 128)
CHUNK = 384
VMEM_LIMIT = 60 * 1024 * 1024


class Place:
    def __init__(self):
        self.line = lax.axis_size("dp") // 4
        spot = lax.axis_index("dp")
        self.z, self.y, self.c = spot // 4, (spot // 2) % 2, spot % 2
        self.x = lax.axis_index("pair")

    def device(self, z=None, y=None, c=None, x=None):
        z = self.z if z is None else z
        y = self.y if y is None else y
        c = self.c if c is None else c
        x = self.x if x is None else x
        return ((z * 2 + y) * 2 + c, x)

    def partner(self, axis):
        return self.device(**{axis: 1 - getattr(self, axis)})

    def greet(self):
        barrier = pltpu.get_barrier_semaphore()
        for axis in ("y", "c", "x"):
            pl.semaphore_signal(
                barrier, inc=1, device_id=self.partner(axis), device_id_type=MESH_ID
            )

        @pl.when(self.z > 0)
        def _():
            pl.semaphore_signal(
                barrier, inc=1, device_id=self.device(z=self.z - 1), device_id_type=MESH_ID
            )

        @pl.when(self.z < self.line - 1)
        def _():
            pl.semaphore_signal(
                barrier, inc=1, device_id=self.device(z=self.z + 1), device_id_type=MESH_ID
            )

        ends = (self.z > 0).astype(jnp.int32) + (self.z < self.line - 1).astype(jnp.int32)
        pl.semaphore_wait(barrier, 3 + ends)


def remote(src, dst, send, recv, device):
    return pltpu.make_async_remote_copy(
        src_ref=src,
        dst_ref=dst,
        send_sem=send,
        recv_sem=recv,
        device_id=device,
        device_id_type=MESH_ID,
    )


def gather_kernel(members, *refs):
    count = len(members)
    input_count = len(refs) - 9 - count
    ins, outs = refs[:input_count], refs[input_count : input_count + count]
    (local, zs, as_, bs, cs, zr, ar, br, cr) = refs[input_count + count :]
    place = Place()
    line, z, y, c, x = place.line, place.z, place.y, place.c, place.x
    place.greet()

    def source(k):
        number, layer, _ = members[k]
        return ins[number] if layer is None else ins[number].at[layer]

    def at(k, zz, flip_a=False):
        first = members[k][2]
        yy = 1 - y if flip_a and first == "y" else y
        xx = 1 - x if flip_a and first == "x" else x
        return outs[k].at[zz, yy, c, xx]

    def axes(k):
        first = members[k][2]
        return first, "x" if first == "y" else "y"

    def z_copy(k, src, zz, up):
        to = place.device(z=z + 1 if up else z - 1)
        return remote(src, at(k, zz), zs.at[k, 0 if up else 1, zz], zr.at[k, zz], to)

    def a_copy(k, src, zz):
        return remote(src, at(k, zz), as_.at[k], ar.at[k, zz], place.partner(axes(k)[0]))

    def b_copy(k, src, zz, flip_a):
        return remote(src, at(k, zz, flip_a), bs.at[k], br.at[k], place.partner(axes(k)[1]))

    def c_copy(k, src, dst):
        return remote(src, dst, cs.at[k], cr.at[k], place.partner("c"))

    def spread(k, src, zz):
        a_copy(k, src, zz).start()
        b_copy(k, src, zz, False).start()
        c_copy(k, src, at(k, zz)).start()

    def line_step(k, d):
        if d == 0:
            src = source(k)

            @pl.when(z < line - 1)
            def _():
                z_copy(k, src, z, True).start()

            @pl.when(z > 0)
            def _():
                z_copy(k, src, z, False).start()

            spread(k, src, z)
            pltpu.make_async_copy(src, at(k, z), local.at[k]).start()
            return

        @pl.when(z >= d)
        def _():
            zz = z - d
            z_copy(k, at(k, zz), zz, True).wait_recv()

            @pl.when(z < line - 1)
            def _():
                z_copy(k, at(k, zz), zz, True).start()

            spread(k, at(k, zz), zz)

        @pl.when(z + d < line)
        def _():
            zz = z + d
            z_copy(k, at(k, zz), zz, False).wait_recv()

            @pl.when(z > 0)
            def _():
                z_copy(k, at(k, zz), zz, False).start()

            spread(k, at(k, zz), zz)

    def a_step(k, d):
        def pass_on(zz):
            block = at(k, zz, True)
            a_copy(k, block, zz).wait_recv()
            b_copy(k, block, zz, True).start()
            c_copy(k, block, block).start()

        if d == 0:
            pass_on(z)
            return

        @pl.when(z >= d)
        def _():
            pass_on(z - d)

        @pl.when(z + d < line)
        def _():
            pass_on(z + d)

    def b_slice(k, mine):
        if members[k][2] == "y":
            return outs[k].at[:, :, c, x if mine else 1 - x]
        return outs[k].at[:, y if mine else 1 - y, c]

    def b_step(k):
        theirs = b_slice(k, False)
        remote(theirs, theirs, bs.at[k], br.at[k], place.partner(axes(k)[1])).wait_recv()
        c_copy(k, theirs, theirs).start()

    for wave in range(count + line + 2):
        for k in range(count):
            step = wave - k
            if 0 <= step < line:
                line_step(k, step)
            if 1 <= step < line + 1:
                a_step(k, step - 1)
            if step == line + 2:
                b_step(k)

    for k in range(count):
        pltpu.make_async_copy(source(k), at(k, z), local.at[k]).wait()
        theirs = outs[k].at[:, :, 1 - c]
        own = outs[k].at[:, :, c]
        c_copy(k, theirs, theirs).wait_recv()
        c_copy(k, own, own).wait_send()
        column = outs[k].at[:, y, c, x]
        remote(column, column, as_.at[k], br.at[k], place.partner("c")).wait_send()
        mine = b_slice(k, True)
        remote(mine, mine, bs.at[k], br.at[k], place.partner("c")).wait_send()
        for zz in range(line):

            @pl.when((z < line - 1) & (zz <= z))
            def _():
                z_copy(k, at(k, zz), zz, True).wait_send()

            @pl.when((z > 0) & (zz >= z))
            def _():
                z_copy(k, at(k, zz), zz, False).wait_send()


def gather_weights(mesh_shape, shards, bias_block, layer):
    dp_size, pair_size = mesh_shape
    line = dp_size // 4
    members = []
    outs = []
    operands = list(shards)
    if bias_block is not None:
        members.append((len(shards), None, "y"))
        outs.append(bias_block)
        operands.append(bias_block)
    for number, shard in enumerate(shards):
        members.append((number, layer, "y" if (number + layer) % 2 == 0 else "x"))
        outs.append(shard[layer])
    count = len(members)
    shapes = [
        jax.ShapeDtypeStruct((line, 2, 2, pair_size) + out.shape, out.dtype) for out in outs
    ]
    dma = pltpu.SemaphoreType.DMA
    full = pl.pallas_call(
        functools.partial(gather_kernel, members),
        out_shape=shapes,
        in_specs=[pl.BlockSpec(memory_space=pl.ANY)] * len(operands),
        out_specs=[pl.BlockSpec(memory_space=pl.ANY)] * count,
        scratch_shapes=[
            dma((count,)),
            dma((count, 2, line)),
            dma((count,)),
            dma((count,)),
            dma((count,)),
            dma((count, line)),
            dma((count, line)),
            dma((count,)),
            dma((count,)),
        ],
        compiler_params=pltpu.CompilerParams(collective_id=layer, has_side_effects=True),
        cost_estimate=pl.CostEstimate(flops=0, bytes_accessed=200_000_000, transcendentals=0),
        name="gather_weights_%d" % layer,
    )(*operands)
    weights = [weight.reshape(-1, weight.shape[-1]) for weight in full[-len(shards) :]]
    biases = None if bias_block is None else full[0].reshape(dp_size * pair_size, -1)
    return weights, biases


def reduce_kernel(firsts, pair_count, *refs):
    count = len(firsts)
    pairs = [(refs[2 * k], refs[2 * k + 1]) for k in range(pair_count)]
    at = 2 * pair_count
    given = list(refs[at : at + count - pair_count])
    at += len(given)
    outs = refs[at : at + count]
    at += count
    full = list(refs[at : at + pair_count]) + given
    at += pair_count
    from_c, from_b, from_a, from_low, from_high = [
        refs[at + count * j : at + count * (j + 1)] for j in range(5)
    ]
    at += 5 * count
    c_send, c_recv, b_send, b_recv, a_send, a_recv, up_send, up_recv, down_send, down_recv = refs[
        at:
    ]
    place = Place()
    line, z, y, c, x = place.line, place.z, place.y, place.c, place.x
    half = line // 2
    place.greet()

    def axes(k):
        return firsts[k], "x" if firsts[k] == "y" else "y"

    def add(total_ref, total_at, more_ref, more_at):
        total_ref[total_at] = (
            total_ref[total_at].astype(jnp.float32) + more_ref[more_at].astype(jnp.float32)
        ).astype(total_ref.dtype)

    def c_copy(k, h):
        zs = pl.ds(h * half, half)
        return remote(
            full[k].at[zs, :, 1 - c],
            from_c[k].at[zs],
            c_send.at[k, h],
            c_recv.at[k, h],
            place.partner("c"),
        )

    def b_copy(k, h):
        zs = pl.ds(h * half, half)
        src = from_c[k].at[zs, :, 1 - x] if firsts[k] == "x" else from_c[k].at[zs, 1 - y]
        return remote(
            src, from_b[k].at[zs], b_send.at[k, h], b_recv.at[k, h], place.partner(axes(k)[0])
        )

    def a_copy(k, h):
        zs = pl.ds(h * half, half)
        other = 1 - getattr(place, axes(k)[1])
        return remote(
            from_b[k].at[zs, other],
            from_a[k].at[zs],
            a_send.at[k, h],
            a_recv.at[k, h],
            place.partner(axes(k)[1]),
        )

    def up_copy(k, t, src):
        return remote(
            src, from_low[k].at[t], up_send.at[k, t], up_recv.at[k, t], place.device(z=z + 1)
        )

    def down_copy(k, t, src):
        return remote(
            src, from_high[k].at[t], down_send.at[k, t], down_recv.at[k, t], place.device(z=z - 1)
        )

    def compute(k, h):
        if k < pair_count:
            left, right = pairs[k]
            rows = full[k].shape[4]
            height = full[k].shape[0] * 8 * rows // 2
            blocks = CHUNK // rows
            wide = right.shape[1]
            for chunk in range(height // CHUNK):
                base = h * half * 8 + chunk * blocks

                def tile(j, carry, chunk=chunk, base=base):
                    columns = pl.ds(pl.multiple_of(j * 768, 768), 768)
                    product = lax.dot_general(
                        left[:, h * height + chunk * CHUNK : h * height + (chunk + 1) * CHUNK],
                        right[:, columns],
                        (((0,), (0,)), ((), ())),
                        preferred_element_type=jnp.float32,
                    )
                    for block in range(blocks):
                        n = base + block
                        full[k][n // 8, (n // 4) % 2, (n // 2) % 2, n % 2, :, columns] = product[
                            block * rows : (block + 1) * rows
                        ].astype(jnp.bfloat16)
                    return carry

                lax.fori_loop(0, wide // 768, tile, 0)
        c_copy(k, h).start()

    def after_c(k, h):
        c_copy(k, h).wait_recv()

        def sweep(other):
            def one(i, carry):
                zz, side = h * half + i // 2, i % 2
                yy, xx = (side, other) if firsts[k] == "x" else (other, side)
                add(from_c[k], (zz, yy, xx), full[k], (zz, yy, c, xx))
                return carry

            lax.fori_loop(0, half * 2, one, 0)

        mine = getattr(place, axes(k)[0])
        sweep(1 - mine)
        b_copy(k, h).start()
        sweep(mine)

    def after_b(k, h):
        b_copy(k, h).wait_recv()

        def sweep(side):
            def one(i, carry):
                zz = h * half + i
                yy, xx = (side, x) if firsts[k] == "x" else (y, side)
                add(from_b[k], (zz, side), from_c[k], (zz, yy, xx))
                return carry

            lax.fori_loop(0, half, one, 0)

        mine = getattr(place, axes(k)[1])
        sweep(1 - mine)
        a_copy(k, h).start()
        sweep(mine)

    def after_a(k, h):
        a_copy(k, h).wait_recv()
        mine = getattr(place, axes(k)[1])

        def one(i, carry):
            zz = h * half + i
            add(from_a[k], (zz,), from_b[k], (zz, mine))
            return carry

        lax.fori_loop(0, half, one, 0)

    def hop(k, h, step):
        for t in reversed(range(h * half, (h + 1) * half)):

            @pl.when((z == step) & (z < t))
            def _():
                if step == 0:
                    up_copy(k, t, from_a[k].at[t]).start()
                else:
                    up_copy(k, t, from_low[k].at[t]).wait_recv()
                    add(from_low[k], (t,), from_a[k], (t,))
                    up_copy(k, t, from_low[k].at[t]).start()

        for t in range(h * half, (h + 1) * half):

            @pl.when((z == line - 1 - step) & (z > t))
            def _():
                if step == 0:
                    down_copy(k, t, from_a[k].at[t]).start()
                else:
                    down_copy(k, t, from_high[k].at[t]).wait_recv()
                    add(from_high[k], (t,), from_a[k], (t,))
                    down_copy(k, t, from_high[k].at[t]).start()

    def finish(k, h):
        for t in range(h * half, (h + 1) * half):

            @pl.when(z == t)
            def _():
                total = from_a[k][t].astype(jnp.float32)
                if t > 0:
                    up_copy(k, t, from_low[k].at[t]).wait_recv()
                    total = total + from_low[k][t].astype(jnp.float32)
                if t < line - 1:
                    down_copy(k, t, from_high[k].at[t]).wait_recv()
                    total = total + from_high[k][t].astype(jnp.float32)
                outs[k][...] = total

    def settle(k, h):
        c_copy(k, h).wait_send()
        b_copy(k, h).wait_send()
        a_copy(k, h).wait_send()
        for t in range(h * half, (h + 1) * half):

            @pl.when(z < t)
            def _():
                up_copy(k, t, from_a[k].at[t]).wait_send()

            @pl.when(z > t)
            def _():
                down_copy(k, t, from_a[k].at[t]).wait_send()

    units = [(k, h) for h in range(2) for k in range(count)]
    stages = [compute, after_c, after_b, after_a]
    stages += [functools.partial(hop, step=step) for step in range(line)]
    stages += [finish]
    for wave in range(len(units) + len(stages) - 1):
        for number, (k, h) in enumerate(units):
            step = wave - number
            if 0 <= step < len(stages):
                stages[step](k, h)
    for k, h in units:
        settle(k, h)


def reduce_grads(mesh_shape, pairs, bias_rows, number):
    dp_size, pair_size = mesh_shape
    shard_count = dp_size * pair_size
    line = dp_size // 4
    lead = (line, 2, 2, pair_size)
    low = jnp.bfloat16
    operands = [side for pair in pairs for side in pair]
    shapes = [(left.shape[1] // shard_count, right.shape[1]) for left, right in pairs]
    scratch = [pltpu.VMEM(lead + shape, low) for shape in shapes]
    if bias_rows is not None:
        operands.append(bias_rows.reshape(lead + BIAS_TILE))
        shapes.append(BIAS_TILE)
    count = len(shapes)
    firsts = ["x" if (k + number) % 2 == 0 else "y" for k in range(count)]
    for space in ((line, 2, 2), (line, 2), (line,), (line,), (line,)):
        scratch += [pltpu.VMEM(space + shape, low) for shape in shapes]
    dma = pltpu.SemaphoreType.DMA
    scratch += [dma((count, 2))] * 6 + [dma((count, line))] * 4
    vmem = pl.BlockSpec(memory_space=pltpu.VMEM)
    return pl.pallas_call(
        functools.partial(reduce_kernel, firsts, len(pairs)),
        out_shape=[jax.ShapeDtypeStruct(shape, jnp.float32) for shape in shapes],
        in_specs=[vmem] * len(operands),
        out_specs=[vmem] * count,
        scratch_shapes=scratch,
        compiler_params=pltpu.CompilerParams(
            collective_id=LAYERS + number, has_side_effects=True, vmem_limit_bytes=VMEM_LIMIT
        ),
        cost_estimate=pl.CostEstimate(flops=0, bytes_accessed=150_000_000, transcendentals=0),
        name="reduce_grads_%d" % number,
    )(*operands)


def spread(values):
    count = lax.axis_size(AXES)
    copies = jnp.broadcast_to(values[None], (count,) + values.shape)
    copies = lax.all_to_all(copies, AXES, split_axis=0, concat_axis=0, tiled=True)
    return copies.reshape((-1,) + values.shape[1:])


def plain_gather(shards, bias_block, layer):
    weights = [lax.all_gather(shard[layer], AXES, axis=0, tiled=True) for shard in shards]
    if bias_block is None:
        return weights, None
    return weights, lax.all_gather(bias_block.reshape(1, -1), AXES, axis=0, tiled=True)


def plain_reduce(pairs, bias_rows, number):
    grads = []
    for left, right in pairs:
        product = jnp.einsum("tk,tn->kn", left, right, preferred_element_type=jnp.float32)
        grads.append(product.astype(GRAD_DTYPE))
    if bias_rows is not None:
        grads.append(bias_rows)
    return [
        lax.psum_scatter(grad, AXES, scatter_dimension=0, tiled=True).astype(jnp.float32)
        for grad in grads
    ]


def forward_layer(residual_state, modulation, gathered):
    (
        qkv_weight,
        query_bias,
        value_bias,
        proj_weight,
        proj_bias,
        expand_weight,
        expand_bias,
        reduce_weight,
        reduce_bias,
    ) = gathered
    latent_count, seq_len, model_width = residual_state.shape
    inv_root = HEAD ** (-0.5)
    shift_attn, scale_attn, gate_attn, shift_mlp, scale_mlp, gate_mlp = jnp.split(
        modulation, 6, axis=-1
    )
    normed_in = modulate(residual_state, shift_attn, scale_attn).astype(jnp.bfloat16)
    qkv_bias = jnp.concatenate([query_bias, jnp.zeros_like(query_bias), value_bias]).astype(
        jnp.float32
    )
    qkv_rows = (
        jnp.dot(normed_in, qkv_weight, preferred_element_type=jnp.float32) + qkv_bias
    ).astype(jnp.bfloat16)
    qkv_rows = qkv_rows.reshape(latent_count, seq_len, 3, HEADS, HEAD)
    scores = (
        jnp.einsum(
            "bqhe,bkhe->bhqk",
            qkv_rows[:, :, 0],
            qkv_rows[:, :, 1],
            preferred_element_type=jnp.float32,
        )
        * inv_root
    )
    top_score = jnp.max(scores, axis=-1, keepdims=True)
    weights_exp = jnp.exp(scores - top_score)
    total_exp = jnp.sum(weights_exp, axis=-1, keepdims=True)
    probs = weights_exp / total_exp
    log_total = top_score + jnp.log(total_exp)
    attended = jnp.einsum(
        "bhqk,bkhe->bqhe",
        probs.astype(jnp.bfloat16),
        qkv_rows[:, :, 2],
        preferred_element_type=jnp.float32,
    )
    attended = attended.astype(jnp.bfloat16).reshape(latent_count, seq_len, model_width)
    attn_out = jnp.dot(
        attended, proj_weight, preferred_element_type=jnp.float32
    ) + proj_bias.astype(jnp.float32)
    middle = residual_state + gate_attn[:, None, :] * attn_out
    normed_mid = modulate(middle, shift_mlp, scale_mlp).astype(jnp.bfloat16)
    pre_act = jnp.dot(
        normed_mid, expand_weight, preferred_element_type=jnp.float32
    ) + expand_bias.astype(jnp.float32)
    activated = gelu_tanh(pre_act).astype(jnp.bfloat16)
    mlp_out = jnp.dot(
        activated, reduce_weight, preferred_element_type=jnp.float32
    ) + reduce_bias.astype(jnp.float32)
    result = middle + gate_mlp[:, None, :] * mlp_out
    stored = (
        residual_state,
        modulation,
        normed_in,
        qkv_rows,
        log_total,
        attended,
        attn_out,
        middle,
        normed_mid,
        pre_act,
        activated,
        mlp_out,
    )
    return (result, stored)


def backward_layer(upstream, gathered, stored):
    (
        qkv_weight,
        query_bias,
        value_bias,
        proj_weight,
        proj_bias,
        expand_weight,
        expand_bias,
        reduce_weight,
        reduce_bias,
    ) = gathered
    (
        residual_state,
        modulation,
        normed_in,
        qkv_rows,
        log_total,
        attended,
        attn_out,
        middle,
        normed_mid,
        pre_act,
        activated,
        mlp_out,
    ) = stored
    latent_count, seq_len, model_width = residual_state.shape
    inv_root = HEAD ** (-0.5)
    shift_attn, scale_attn, gate_attn, shift_mlp, scale_mlp, gate_mlp = jnp.split(
        modulation, 6, axis=-1
    )
    d_mlp = (gate_mlp[:, None, :] * upstream).astype(jnp.bfloat16)
    d_gate_mlp = jnp.sum(upstream * mlp_out, axis=1)
    g_reduce_b = jnp.sum(d_mlp, axis=(0, 1), dtype=jnp.float32)
    d_act = jnp.einsum("bsd,fd->bsf", d_mlp, reduce_weight, preferred_element_type=jnp.float32)
    _, pull_gelu = jax.vjp(gelu_tanh, pre_act)
    d_pre = pull_gelu(d_act)[0].astype(jnp.bfloat16)
    g_expand_b = jnp.sum(d_pre, axis=(0, 1), dtype=jnp.float32)
    d_normed_mid = jnp.einsum(
        "bsf,df->bsd", d_pre, expand_weight, preferred_element_type=jnp.float32
    )
    _, pull_mid = jax.vjp(modulate, middle, shift_mlp, scale_mlp)
    d_middle, d_shift_mlp, d_scale_mlp = pull_mid(d_normed_mid)
    d_middle = d_middle + upstream
    d_attn = (gate_attn[:, None, :] * d_middle).astype(jnp.bfloat16)
    d_gate_attn = jnp.sum(d_middle * attn_out, axis=1)
    g_proj_b = jnp.sum(d_attn, axis=(0, 1), dtype=jnp.float32)
    d_attended = jnp.einsum("bse,de->bsd", d_attn, proj_weight, preferred_element_type=jnp.float32)
    d_attended = d_attended.astype(jnp.bfloat16).reshape(latent_count, seq_len, HEADS, HEAD)
    queries = qkv_rows[:, :, 0]
    key_rows = qkv_rows[:, :, 1]
    value_rows = qkv_rows[:, :, 2]
    scores = (
        jnp.einsum("bqhe,bkhe->bhqk", queries, key_rows, preferred_element_type=jnp.float32)
        * inv_root
    )
    probs = jnp.exp(scores - log_total)
    d_probs = jnp.einsum(
        "bqhe,bkhe->bhqk", d_attended, value_rows, preferred_element_type=jnp.float32
    )
    d_scores = (probs * (d_probs - jnp.sum(probs * d_probs, axis=-1, keepdims=True))).astype(
        jnp.bfloat16
    )
    d_values = jnp.einsum(
        "bhqk,bqhe->bkhe",
        probs.astype(jnp.bfloat16),
        d_attended,
        preferred_element_type=jnp.float32,
    )
    d_queries = (
        jnp.einsum("bhqk,bkhe->bqhe", d_scores, key_rows, preferred_element_type=jnp.float32)
        * inv_root
    )
    d_keys = (
        jnp.einsum("bhqk,bqhe->bkhe", d_scores, queries, preferred_element_type=jnp.float32)
        * inv_root
    )
    d_qkv = jnp.stack([d_queries, d_keys, d_values], axis=2).astype(jnp.bfloat16)
    d_qkv = d_qkv.reshape(latent_count, seq_len, 3 * model_width)
    g_query_b = jnp.sum(d_qkv[:, :, :model_width], axis=(0, 1), dtype=jnp.float32)
    g_value_b = jnp.sum(d_qkv[:, :, 2 * model_width :], axis=(0, 1), dtype=jnp.float32)
    d_normed_in = jnp.einsum("bsf,df->bsd", d_qkv, qkv_weight, preferred_element_type=jnp.float32)
    _, pull_in = jax.vjp(modulate, residual_state, shift_attn, scale_attn)
    d_stream, d_shift_attn, d_scale_attn = pull_in(d_normed_in)
    d_stream = d_stream + d_middle
    d_modulation = jnp.concatenate(
        [d_shift_attn, d_scale_attn, d_gate_attn, d_shift_mlp, d_scale_mlp, d_gate_mlp], axis=-1
    ).astype(jnp.bfloat16)
    pairs = (
        (normed_in, d_qkv),
        (attended, d_attn),
        (normed_mid, d_pre),
        (activated, d_mlp),
    )
    pairs = [[side.reshape(-1, side.shape[-1]) for side in pair] for pair in pairs]
    return (d_stream, d_modulation, pairs, (g_query_b, g_value_b, g_proj_b, g_expand_b, g_reduce_b))


def on_device(
    latents,
    conditioning,
    cotangent,
    adaln_weight,
    adaln_bias,
    qkv_weight,
    query_bias,
    value_bias,
    proj_weight,
    proj_bias,
    expand_weight,
    expand_bias,
    reduce_weight,
    reduce_bias,
):
    shard_count = lax.axis_size(AXES)
    mesh_shape = (lax.axis_size("dp"), lax.axis_size("pair"))
    rows = qkv_weight.shape[1]
    in_kernels = rows % 8 == 0 and CHUNK % rows == 0
    here = lax.axis_index(AXES)
    stream = latents.astype(jnp.float32)
    cond_part = conditioning.astype(jnp.float32)
    silu_low = jax.nn.silu(spread(conditioning).astype(jnp.float32)).astype(jnp.bfloat16)
    silu_mine = lax.dynamic_slice_in_dim(silu_low, here * rows, rows, axis=1)
    adaln_columns = lax.all_to_all(adaln_weight, AXES, split_axis=2, concat_axis=1, tiled=True)
    modulation = jnp.einsum(
        "bd,ldf->lbf", silu_low, adaln_columns, preferred_element_type=jnp.float32
    ) + adaln_bias.astype(jnp.float32)[:, None]
    modulation = lax.all_to_all(modulation, AXES, split_axis=1, concat_axis=2, tiled=True)
    shards = (qkv_weight, proj_weight, expand_weight, reduce_weight)
    bias_members = (query_bias, value_bias, proj_bias, expand_bias, reduce_bias)
    bias_sizes = [member.shape[1] for member in bias_members]
    room = BIAS_TILE[0] * BIAS_TILE[1]
    bias_row = jnp.concatenate(bias_members, axis=1).reshape(-1)
    bias_row = jnp.pad(bias_row, (0, room - bias_row.shape[0])).reshape(BIAS_TILE)
    weights = []
    for layer in range(LAYERS):
        block = bias_row if layer == 0 else None
        if in_kernels:
            found = gather_weights(mesh_shape, shards, block, layer)
        else:
            found = plain_gather(shards, block, layer)
        weights.append(found[0])
        if layer == 0:
            bias_rows = found[1]
    gathered = []
    at = 0
    for layer in range(LAYERS):
        biases = []
        for size in bias_sizes:
            biases.append(bias_rows[:, at : at + size].reshape(-1))
            at += size
        query_b, value_b, proj_b, expand_b, reduce_b = biases
        qkv_w, proj_w, expand_w, reduce_w = weights[layer]
        gathered.append(
            (qkv_w, query_b, value_b, proj_w, proj_b, expand_w, expand_b, reduce_w, reduce_b)
        )
    stored = [None] * LAYERS
    for layer in range(LAYERS):
        stream, stored[layer] = forward_layer(stream, modulation[layer], gathered[layer])
    outputs = stream.astype(jnp.bfloat16)
    upstream = cotangent.astype(jnp.float32)
    summed = [None] * LAYERS
    d_mods = [None] * LAYERS
    reduce = functools.partial(reduce_grads, mesh_shape) if in_kernels else plain_reduce
    calls = 0
    for layer in reversed(range(LAYERS)):
        upstream, d_modulation, pairs, bias_grads = backward_layer(
            upstream, gathered[layer], stored[layer]
        )
        d_mods[layer] = spread(d_modulation)
        flat = jnp.concatenate([grad.reshape(shard_count, -1) for grad in bias_grads], axis=1)
        flat = jnp.pad(flat, ((0, 0), (0, room - flat.shape[1]))).astype(GRAD_DTYPE)
        if layer > 0:
            summed[layer] = reduce(pairs, flat, number=calls)
            calls += 1
        else:
            late = reduce(pairs[2:], None, number=calls)
            held = lax.optimization_barrier((pairs[:2], flat, d_mods))
            early_pairs, flat, d_mods = held
            early = reduce(early_pairs, flat, number=calls + 1)
            summed[layer] = list(early[:2]) + list(late) + [early[2]]
    g_adaln_w = []
    g_adaln_b = []
    d_silu = 0.0
    adaln_size = adaln_bias.shape[1]
    for layer in range(LAYERS):
        part = d_mods[layer]
        g_adaln_w.append(
            jnp.einsum("bd,bf->df", silu_mine, part, preferred_element_type=jnp.float32)
        )
        mine = lax.dynamic_slice_in_dim(part, here * adaln_size, adaln_size, axis=1)
        g_adaln_b.append(jnp.sum(mine, axis=0, dtype=jnp.float32))
        d_silu = d_silu + jnp.einsum(
            "bf,df->bd", part, adaln_weight[layer], preferred_element_type=jnp.float32
        )
    d_silu = lax.all_to_all(d_silu, AXES, split_axis=0, concat_axis=1, tiled=True)
    _, pull_silu = jax.vjp(jax.nn.silu, cond_part)
    grad_conditioning = pull_silu(d_silu)[0]
    small = [[] for _ in bias_sizes]
    for layer in range(LAYERS):
        flat = summed[layer][4].reshape(-1)
        at = 0
        for number, size in enumerate(bias_sizes):
            small[number].append(flat[at : at + size])
            at += size
    large = [[summed[layer][member] for layer in range(LAYERS)] for member in range(4)]
    stacked = [
        g_adaln_w,
        g_adaln_b,
        large[0],
        small[0],
        small[1],
        large[1],
        small[2],
        large[2],
        small[3],
        large[3],
        small[4],
    ]
    stacked = [jnp.stack(member) for member in stacked]
    return tuple([outputs, upstream, grad_conditioning] + stacked)


def solution(mesh):
    in_specs = (
        P(("dp", "pair"), None, None),
        P(("dp", "pair"), None),
        P(("dp", "pair"), None, None),
        P(None, ("dp", "pair"), None),
        P(None, ("dp", "pair")),
        P(None, ("dp", "pair"), None),
        P(None, ("dp", "pair")),
        P(None, ("dp", "pair")),
        P(None, ("dp", "pair"), None),
        P(None, ("dp", "pair")),
        P(None, ("dp", "pair"), None),
        P(None, ("dp", "pair")),
        P(None, ("dp", "pair"), None),
        P(None, ("dp", "pair")),
    )
    out_specs = (
        P(("dp", "pair"), None, None),
        P(("dp", "pair"), None, None),
        P(("dp", "pair"), None),
        P(None, ("dp", "pair"), None),
        P(None, ("dp", "pair")),
        P(None, ("dp", "pair"), None),
        P(None, ("dp", "pair")),
        P(None, ("dp", "pair")),
        P(None, ("dp", "pair"), None),
        P(None, ("dp", "pair")),
        P(None, ("dp", "pair"), None),
        P(None, ("dp", "pair")),
        P(None, ("dp", "pair"), None),
        P(None, ("dp", "pair")),
    )
    return jax.shard_map(
        on_device, mesh=mesh, in_specs=in_specs, out_specs=out_specs, check_vma=False
    )
```

```python
import functools

import jax
import jax.numpy as jnp
from jax import lax
from jax.experimental import pallas as pl
from jax.experimental.pallas import tpu as pltpu
from jax.sharding import PartitionSpec as P

HEADS = 12
HEAD = 64
LAYERS = 2


EPSILON = 1e-06


def layer_norm(values):
    centre = values - jnp.mean(values, axis=-1, keepdims=True)
    spread = jnp.mean(centre * centre, axis=-1, keepdims=True)
    return centre * lax.rsqrt(spread + EPSILON)


def modulate(residual_state, shift, scale):
    return layer_norm(residual_state) * (1.0 + scale[:, None, :]) + shift[:, None, :]


def gelu_tanh(values):
    return jax.nn.gelu(values, approximate=True)


AXES = ("dp", "pair")
LANES = 128
GRAD_DTYPE = jnp.bfloat16


MESH_ID = pl.DeviceIdType.MESH
BIAS_TILE = (16, 128)
CHUNK = 384
SIDE_LAG = 1
CORNER_LAG = 2
OFFSETS = (0, 1, 2, 3, 4)
ORDER = (1, 3, 2, 0, 4)
VMEM_LIMIT = 60 * 1024 * 1024


class Place:
    def __init__(self):
        self.line = lax.axis_size("dp") // 4
        spot = lax.axis_index("dp")
        self.z, self.y, self.c = spot // 4, (spot // 2) % 2, spot % 2
        self.x = lax.axis_index("pair")

    def device(self, z=None, y=None, c=None, x=None):
        z = self.z if z is None else z
        y = self.y if y is None else y
        c = self.c if c is None else c
        x = self.x if x is None else x
        return ((z * 2 + y) * 2 + c, x)

    def partner(self, axis):
        return self.device(**{axis: 1 - getattr(self, axis)})

    def greet(self):
        barrier = pltpu.get_barrier_semaphore()
        for axis in ("y", "c", "x"):
            pl.semaphore_signal(
                barrier, inc=1, device_id=self.partner(axis), device_id_type=MESH_ID
            )

        @pl.when(self.z > 0)
        def _():
            pl.semaphore_signal(
                barrier, inc=1, device_id=self.device(z=self.z - 1), device_id_type=MESH_ID
            )

        @pl.when(self.z < self.line - 1)
        def _():
            pl.semaphore_signal(
                barrier, inc=1, device_id=self.device(z=self.z + 1), device_id_type=MESH_ID
            )

        ends = (self.z > 0).astype(jnp.int32) + (self.z < self.line - 1).astype(jnp.int32)
        pl.semaphore_wait(barrier, 3 + ends)


def remote(src, dst, send, recv, device):
    return pltpu.make_async_remote_copy(
        src_ref=src,
        dst_ref=dst,
        send_sem=send,
        recv_sem=recv,
        device_id=device,
        device_id_type=MESH_ID,
    )


def gather_kernel(members, *refs):
    count = len(members)
    input_count = len(refs) - 9 - count
    ins, outs = refs[:input_count], refs[input_count : input_count + count]
    (local, zs, as_, bs, cs, zr, ar, br, cr) = refs[input_count + count :]
    place = Place()
    line, z, y, c, x = place.line, place.z, place.y, place.c, place.x
    place.greet()

    def source(k):
        number, layer = members[k]
        return ins[number] if layer is None else ins[number].at[layer]

    def at(k, zz, flip_y=False, flip_x=False):
        return outs[k].at[zz, 1 - y if flip_y else y, c, 1 - x if flip_x else x]

    def z_copy(k, src, zz, up):
        to = place.device(z=z + 1 if up else z - 1)
        return remote(src, at(k, zz), zs.at[k, 0 if up else 1, zz], zr.at[k, zz], to)

    def y_copy(k, src, dst, step, zz):
        return remote(src, dst, as_.at[k, step], ar.at[k, step, zz], place.partner("y"))

    def x_copy(k, src, dst, step, zz):
        return remote(src, dst, bs.at[k, step], br.at[k, step, zz], place.partner("x"))

    def c_copy(k, src, dst):
        return remote(src, dst, cs.at[k], cr.at[k], place.partner("c"))

    def spread(k, src, zz):
        dst = at(k, zz)
        y_copy(k, src, dst, 0, zz).start()
        x_copy(k, src, dst, 0, zz).start()
        c_copy(k, src, dst).start()

    def line_step(k, d):
        if d == 0:
            src = source(k)

            @pl.when(z < line - 1)
            def _():
                z_copy(k, src, z, True).start()

            @pl.when(z > 0)
            def _():
                z_copy(k, src, z, False).start()

            spread(k, src, z)
            pltpu.make_async_copy(src, at(k, z), local.at[k]).start()
            return

        @pl.when(z >= d)
        def _():
            zz = z - d
            z_copy(k, at(k, zz), zz, True).wait_recv()

            @pl.when(z < line - 1)
            def _():
                z_copy(k, at(k, zz), zz, True).start()

            spread(k, at(k, zz), zz)

        @pl.when(z + d < line)
        def _():
            zz = z + d
            z_copy(k, at(k, zz), zz, False).wait_recv()

            @pl.when(z > 0)
            def _():
                z_copy(k, at(k, zz), zz, False).start()

            spread(k, at(k, zz), zz)

    def at_distance(d, use):
        if d == 0:
            use(z)
            return

        @pl.when(z >= d)
        def _():
            use(z - d)

        @pl.when(z + d < line)
        def _():
            use(z + d)

    def y_first(zz):
        return zz % 2 == 0

    def side_step(k, d):
        def use(zz):
            over_y, over_x = at(k, zz, flip_y=True), at(k, zz, flip_x=True)
            y_copy(k, over_y, over_y, 0, zz).wait_recv()

            @pl.when(y_first(zz))
            def _():
                x_copy(k, over_y, over_y, 1, zz).start()

            c_copy(k, over_y, over_y).start()
            x_copy(k, over_x, over_x, 0, zz).wait_recv()

            @pl.when(jnp.logical_not(y_first(zz)))
            def _():
                y_copy(k, over_x, over_x, 1, zz).start()

            c_copy(k, over_x, over_x).start()

        at_distance(d, use)

    def corner_step(k, d):
        def use(zz):
            corner = at(k, zz, flip_y=True, flip_x=True)

            @pl.when(y_first(zz))
            def _():
                x_copy(k, corner, corner, 1, zz).wait_recv()

            @pl.when(jnp.logical_not(y_first(zz)))
            def _():
                y_copy(k, corner, corner, 1, zz).wait_recv()

            c_copy(k, corner, corner).start()

        at_distance(d, use)

    for wave in range(count + line + CORNER_LAG):
        for k in range(count):
            step = wave - k
            if 0 <= step < line:
                line_step(k, step)
            if 0 <= step - SIDE_LAG < line:
                side_step(k, step - SIDE_LAG)
            if 0 <= step - CORNER_LAG < line:
                corner_step(k, step - CORNER_LAG)

    for k in range(count):
        pltpu.make_async_copy(source(k), at(k, z), local.at[k]).wait()
        theirs = outs[k].at[:, :, 1 - c]
        own = outs[k].at[:, :, c]
        c_copy(k, theirs, theirs).wait_recv()
        c_copy(k, own, own).wait_send()
        column = outs[k].at[:, y, c, x]
        y_copy(k, column, column, 0, 0).wait_send()
        x_copy(k, column, column, 0, 0).wait_send()
        part = outs[k].at[pl.ds(0, line // 2), y, c, x]
        y_copy(k, part, part, 1, 0).wait_send()
        x_copy(k, part, part, 1, 0).wait_send()
        for zz in range(line):

            @pl.when((z < line - 1) & (zz <= z))
            def _():
                z_copy(k, at(k, zz), zz, True).wait_send()

            @pl.when((z > 0) & (zz >= z))
            def _():
                z_copy(k, at(k, zz), zz, False).wait_send()


def gather_weights(mesh_shape, shards, bias_block, layer):
    dp_size, pair_size = mesh_shape
    line = dp_size // 4
    members = []
    outs = []
    operands = list(shards)
    if bias_block is not None:
        members.append((len(shards), None))
        outs.append(bias_block)
        operands.append(bias_block)
    for number, shard in enumerate(shards):
        members.append((number, layer))
        outs.append(shard[layer])
    count = len(members)
    shapes = [
        jax.ShapeDtypeStruct((line, 2, 2, pair_size) + out.shape, out.dtype) for out in outs
    ]
    dma = pltpu.SemaphoreType.DMA
    full = pl.pallas_call(
        functools.partial(gather_kernel, members),
        out_shape=shapes,
        in_specs=[pl.BlockSpec(memory_space=pl.ANY)] * len(operands),
        out_specs=[pl.BlockSpec(memory_space=pl.ANY)] * count,
        scratch_shapes=[
            dma((count,)),
            dma((count, 2, line)),
            dma((count, 2)),
            dma((count, 2)),
            dma((count,)),
            dma((count, line)),
            dma((count, 2, line)),
            dma((count, 2, line)),
            dma((count,)),
        ],
        compiler_params=pltpu.CompilerParams(collective_id=layer, has_side_effects=True),
        cost_estimate=pl.CostEstimate(flops=0, bytes_accessed=200_000_000, transcendentals=0),
        name="gather_weights_%d" % layer,
    )(*operands)
    weights = [weight.reshape(-1, weight.shape[-1]) for weight in full[-len(shards) :]]
    biases = None if bias_block is None else full[0].reshape(dp_size * pair_size, -1)
    return weights, biases


def reduce_kernel(count, pair_count, *refs):
    pairs = [(refs[2 * k], refs[2 * k + 1]) for k in range(pair_count)]
    at = 2 * pair_count
    given = list(refs[at : at + count - pair_count])
    at += len(given)
    outs = refs[at : at + count]
    at += count
    full = list(refs[at : at + pair_count]) + given
    at += pair_count
    from_c, from_b, from_a, from_low, from_high = [
        refs[at + count * j : at + count * (j + 1)] for j in range(5)
    ]
    at += 5 * count
    c_send, c_recv, b_send, b_recv, a_send, a_recv, up_send, up_recv, down_send, down_recv = refs[
        at:
    ]
    place = Place()
    line, z, y, c, x = place.line, place.z, place.y, place.c, place.x
    half = line // 2
    place.greet()

    def axes(zz):
        return ("x", "y") if zz % 2 == 0 else ("y", "x")

    def add(total_ref, total_at, more_ref, more_at):
        total_ref[total_at] = (
            total_ref[total_at].astype(jnp.float32) + more_ref[more_at].astype(jnp.float32)
        ).astype(total_ref.dtype)

    def c_copy(k, zz):
        return remote(
            full[k].at[zz, :, 1 - c],
            from_c[k].at[zz],
            c_send.at[k, zz],
            c_recv.at[k, zz],
            place.partner("c"),
        )

    def b_copy(k, zz):
        first = axes(zz)[0]
        src = from_c[k].at[zz, :, 1 - x] if first == "x" else from_c[k].at[zz, 1 - y]
        return remote(
            src, from_b[k].at[zz], b_send.at[k, zz], b_recv.at[k, zz], place.partner(first)
        )

    def a_copy(k, zz):
        second = axes(zz)[1]
        other = 1 - getattr(place, second)
        return remote(
            from_b[k].at[zz, other],
            from_a[k].at[zz],
            a_send.at[k, zz],
            a_recv.at[k, zz],
            place.partner(second),
        )

    def up_copy(k, t, src):
        return remote(
            src, from_low[k].at[t], up_send.at[k, t], up_recv.at[k, t], place.device(z=z + 1)
        )

    def down_copy(k, t, src):
        return remote(
            src, from_high[k].at[t], down_send.at[k, t], down_recv.at[k, t], place.device(z=z - 1)
        )

    def zs_of(h):
        return range(h * half, (h + 1) * half)

    def compute(k, h):
        if k < pair_count:
            left, right = pairs[k]
            rows = full[k].shape[4]
            height = full[k].shape[0] * 8 * rows // 2
            blocks = CHUNK // rows
            wide = right.shape[1]
            for chunk in range(height // CHUNK):
                base = h * half * 8 + chunk * blocks

                def tile(j, carry, chunk=chunk, base=base):
                    columns = pl.ds(pl.multiple_of(j * 768, 768), 768)
                    product = lax.dot_general(
                        left[:, h * height + chunk * CHUNK : h * height + (chunk + 1) * CHUNK],
                        right[:, columns],
                        (((0,), (0,)), ((), ())),
                        preferred_element_type=jnp.float32,
                    )
                    for block in range(blocks):
                        n = base + block
                        full[k][n // 8, (n // 4) % 2, (n // 2) % 2, n % 2, :, columns] = product[
                            block * rows : (block + 1) * rows
                        ].astype(jnp.bfloat16)
                    return carry

                lax.fori_loop(0, wide // 768, tile, 0)
        for zz in zs_of(h):
            c_copy(k, zz).start()

    def after_c(k, h):
        def sweep(zz, other):
            for side in range(2):
                yy, xx = (side, other) if axes(zz)[0] == "x" else (other, side)
                add(from_c[k], (zz, yy, xx), full[k], (zz, yy, c, xx))

        for zz in zs_of(h):
            mine = getattr(place, axes(zz)[0])
            c_copy(k, zz).wait_recv()
            sweep(zz, 1 - mine)
            b_copy(k, zz).start()
        for zz in zs_of(h):
            sweep(zz, getattr(place, axes(zz)[0]))

    def after_b(k, h):
        def sweep(zz, side):
            yy, xx = (side, x) if axes(zz)[0] == "x" else (y, side)
            add(from_b[k], (zz, side), from_c[k], (zz, yy, xx))

        for zz in zs_of(h):
            mine = getattr(place, axes(zz)[1])
            b_copy(k, zz).wait_recv()
            sweep(zz, 1 - mine)
            a_copy(k, zz).start()
        for zz in zs_of(h):
            sweep(zz, getattr(place, axes(zz)[1]))

    def after_a(k, h):
        for zz in zs_of(h):
            a_copy(k, zz).wait_recv()
            add(from_a[k], (zz,), from_b[k], (zz, getattr(place, axes(zz)[1])))

    def hop(k, h, step):
        for t in reversed(range(h * half, (h + 1) * half)):

            @pl.when((z == step) & (z < t))
            def _():
                if step == 0:
                    up_copy(k, t, from_a[k].at[t]).start()
                else:
                    up_copy(k, t, from_low[k].at[t]).wait_recv()
                    add(from_low[k], (t,), from_a[k], (t,))
                    up_copy(k, t, from_low[k].at[t]).start()

        for t in range(h * half, (h + 1) * half):

            @pl.when((z == line - 1 - step) & (z > t))
            def _():
                if step == 0:
                    down_copy(k, t, from_a[k].at[t]).start()
                else:
                    down_copy(k, t, from_high[k].at[t]).wait_recv()
                    add(from_high[k], (t,), from_a[k], (t,))
                    down_copy(k, t, from_high[k].at[t]).start()

    def finish(k, h):
        for t in range(h * half, (h + 1) * half):

            @pl.when(z == t)
            def _():
                total = from_a[k][t].astype(jnp.float32)
                if t > 0:
                    up_copy(k, t, from_low[k].at[t]).wait_recv()
                    total = total + from_low[k][t].astype(jnp.float32)
                if t < line - 1:
                    down_copy(k, t, from_high[k].at[t]).wait_recv()
                    total = total + from_high[k][t].astype(jnp.float32)
                outs[k][...] = total

    def settle(k, h):
        for t in zs_of(h):
            c_copy(k, t).wait_send()
            b_copy(k, t).wait_send()
            a_copy(k, t).wait_send()

            @pl.when(z < t)
            def _():
                up_copy(k, t, from_a[k].at[t]).wait_send()

            @pl.when(z > t)
            def _():
                down_copy(k, t, from_a[k].at[t]).wait_send()

    units = [(k, h) for k in ORDER if k < count for h in range(2)]
    stages = [compute, after_c, after_b, after_a]
    stages += [functools.partial(hop, step=step) for step in range(line)]
    stages += [finish]
    offsets = list(OFFSETS) + [OFFSETS[-1] + 1 + step for step in range(line)]
    for wave in range(len(units) + offsets[-1]):
        for number, (k, h) in enumerate(units):
            if wave - number in offsets:
                stages[offsets.index(wave - number)](k, h)
    for k, h in units:
        settle(k, h)


def reduce_grads(mesh_shape, pairs, bias_rows, number):
    dp_size, pair_size = mesh_shape
    shard_count = dp_size * pair_size
    line = dp_size // 4
    lead = (line, 2, 2, pair_size)
    low = jnp.bfloat16
    operands = [side for pair in pairs for side in pair]
    shapes = [(left.shape[1] // shard_count, right.shape[1]) for left, right in pairs]
    scratch = [pltpu.VMEM(lead + shape, low) for shape in shapes]
    if bias_rows is not None:
        operands.append(bias_rows.reshape(lead + BIAS_TILE))
        shapes.append(BIAS_TILE)
    count = len(shapes)
    for space in ((line, 2, 2), (line, 2), (line,), (line,), (line,)):
        scratch += [pltpu.VMEM(space + shape, low) for shape in shapes]
    dma = pltpu.SemaphoreType.DMA
    scratch += [dma((count, line))] * 10
    vmem = pl.BlockSpec(memory_space=pltpu.VMEM)
    return pl.pallas_call(
        functools.partial(reduce_kernel, count, len(pairs)),
        out_shape=[jax.ShapeDtypeStruct(shape, jnp.float32) for shape in shapes],
        in_specs=[vmem] * len(operands),
        out_specs=[vmem] * count,
        scratch_shapes=scratch,
        compiler_params=pltpu.CompilerParams(
            collective_id=LAYERS + number, has_side_effects=True, vmem_limit_bytes=VMEM_LIMIT
        ),
        cost_estimate=pl.CostEstimate(flops=0, bytes_accessed=150_000_000, transcendentals=0),
        name="reduce_grads_%d" % number,
    )(*operands)


def spread(values):
    count = lax.axis_size(AXES)
    copies = jnp.broadcast_to(values[None], (count,) + values.shape)
    copies = lax.all_to_all(copies, AXES, split_axis=0, concat_axis=0, tiled=True)
    return copies.reshape((-1,) + values.shape[1:])


def plain_gather(shards, bias_block, layer):
    weights = [lax.all_gather(shard[layer], AXES, axis=0, tiled=True) for shard in shards]
    if bias_block is None:
        return weights, None
    return weights, lax.all_gather(bias_block.reshape(1, -1), AXES, axis=0, tiled=True)


def plain_reduce(pairs, bias_rows, number):
    grads = []
    for left, right in pairs:
        product = jnp.einsum("tk,tn->kn", left, right, preferred_element_type=jnp.float32)
        grads.append(product.astype(GRAD_DTYPE))
    if bias_rows is not None:
        grads.append(bias_rows)
    return [
        lax.psum_scatter(grad, AXES, scatter_dimension=0, tiled=True).astype(jnp.float32)
        for grad in grads
    ]


def forward_layer(residual_state, modulation, gathered):
    (
        qkv_weight,
        query_bias,
        value_bias,
        proj_weight,
        proj_bias,
        expand_weight,
        expand_bias,
        reduce_weight,
        reduce_bias,
    ) = gathered
    latent_count, seq_len, model_width = residual_state.shape
    inv_root = HEAD ** (-0.5)
    shift_attn, scale_attn, gate_attn, shift_mlp, scale_mlp, gate_mlp = jnp.split(
        modulation, 6, axis=-1
    )
    normed_in = modulate(residual_state, shift_attn, scale_attn).astype(jnp.bfloat16)
    qkv_bias = jnp.concatenate([query_bias, jnp.zeros_like(query_bias), value_bias]).astype(
        jnp.float32
    )
    qkv_rows = (
        jnp.dot(normed_in, qkv_weight, preferred_element_type=jnp.float32) + qkv_bias
    ).astype(jnp.bfloat16)
    qkv_rows = qkv_rows.reshape(latent_count, seq_len, 3, HEADS, HEAD)
    scores = (
        jnp.einsum(
            "bqhe,bkhe->bhqk",
            qkv_rows[:, :, 0],
            qkv_rows[:, :, 1],
            preferred_element_type=jnp.float32,
        )
        * inv_root
    )
    top_score = jnp.max(scores, axis=-1, keepdims=True)
    weights_exp = jnp.exp(scores - top_score)
    total_exp = jnp.sum(weights_exp, axis=-1, keepdims=True)
    probs = weights_exp / total_exp
    log_total = top_score + jnp.log(total_exp)
    attended = jnp.einsum(
        "bhqk,bkhe->bqhe",
        probs.astype(jnp.bfloat16),
        qkv_rows[:, :, 2],
        preferred_element_type=jnp.float32,
    )
    attended = attended.astype(jnp.bfloat16).reshape(latent_count, seq_len, model_width)
    attn_out = jnp.dot(
        attended, proj_weight, preferred_element_type=jnp.float32
    ) + proj_bias.astype(jnp.float32)
    middle = residual_state + gate_attn[:, None, :] * attn_out
    normed_mid = modulate(middle, shift_mlp, scale_mlp).astype(jnp.bfloat16)
    pre_act = jnp.dot(
        normed_mid, expand_weight, preferred_element_type=jnp.float32
    ) + expand_bias.astype(jnp.float32)
    activated = gelu_tanh(pre_act).astype(jnp.bfloat16)
    mlp_out = jnp.dot(
        activated, reduce_weight, preferred_element_type=jnp.float32
    ) + reduce_bias.astype(jnp.float32)
    result = middle + gate_mlp[:, None, :] * mlp_out
    stored = (
        residual_state,
        modulation,
        normed_in,
        qkv_rows,
        log_total,
        attended,
        attn_out,
        middle,
        normed_mid,
        pre_act,
        activated,
        mlp_out,
    )
    return (result, stored)


def backward_layer(upstream, gathered, stored):
    (
        qkv_weight,
        query_bias,
        value_bias,
        proj_weight,
        proj_bias,
        expand_weight,
        expand_bias,
        reduce_weight,
        reduce_bias,
    ) = gathered
    (
        residual_state,
        modulation,
        normed_in,
        qkv_rows,
        log_total,
        attended,
        attn_out,
        middle,
        normed_mid,
        pre_act,
        activated,
        mlp_out,
    ) = stored
    latent_count, seq_len, model_width = residual_state.shape
    inv_root = HEAD ** (-0.5)
    shift_attn, scale_attn, gate_attn, shift_mlp, scale_mlp, gate_mlp = jnp.split(
        modulation, 6, axis=-1
    )
    d_mlp = (gate_mlp[:, None, :] * upstream).astype(jnp.bfloat16)
    d_gate_mlp = jnp.sum(upstream * mlp_out, axis=1)
    g_reduce_b = jnp.sum(d_mlp, axis=(0, 1), dtype=jnp.float32)
    d_act = jnp.einsum("bsd,fd->bsf", d_mlp, reduce_weight, preferred_element_type=jnp.float32)
    _, pull_gelu = jax.vjp(gelu_tanh, pre_act)
    d_pre = pull_gelu(d_act)[0].astype(jnp.bfloat16)
    g_expand_b = jnp.sum(d_pre, axis=(0, 1), dtype=jnp.float32)
    d_normed_mid = jnp.einsum(
        "bsf,df->bsd", d_pre, expand_weight, preferred_element_type=jnp.float32
    )
    _, pull_mid = jax.vjp(modulate, middle, shift_mlp, scale_mlp)
    d_middle, d_shift_mlp, d_scale_mlp = pull_mid(d_normed_mid)
    d_middle = d_middle + upstream
    d_attn = (gate_attn[:, None, :] * d_middle).astype(jnp.bfloat16)
    d_gate_attn = jnp.sum(d_middle * attn_out, axis=1)
    g_proj_b = jnp.sum(d_attn, axis=(0, 1), dtype=jnp.float32)
    d_attended = jnp.einsum("bse,de->bsd", d_attn, proj_weight, preferred_element_type=jnp.float32)
    d_attended = d_attended.astype(jnp.bfloat16).reshape(latent_count, seq_len, HEADS, HEAD)
    queries = qkv_rows[:, :, 0]
    key_rows = qkv_rows[:, :, 1]
    value_rows = qkv_rows[:, :, 2]
    scores = (
        jnp.einsum("bqhe,bkhe->bhqk", queries, key_rows, preferred_element_type=jnp.float32)
        * inv_root
    )
    probs = jnp.exp(scores - log_total)
    d_probs = jnp.einsum(
        "bqhe,bkhe->bhqk", d_attended, value_rows, preferred_element_type=jnp.float32
    )
    d_scores = (probs * (d_probs - jnp.sum(probs * d_probs, axis=-1, keepdims=True))).astype(
        jnp.bfloat16
    )
    d_values = jnp.einsum(
        "bhqk,bqhe->bkhe",
        probs.astype(jnp.bfloat16),
        d_attended,
        preferred_element_type=jnp.float32,
    )
    d_queries = (
        jnp.einsum("bhqk,bkhe->bqhe", d_scores, key_rows, preferred_element_type=jnp.float32)
        * inv_root
    )
    d_keys = (
        jnp.einsum("bhqk,bqhe->bkhe", d_scores, queries, preferred_element_type=jnp.float32)
        * inv_root
    )
    d_qkv = jnp.stack([d_queries, d_keys, d_values], axis=2).astype(jnp.bfloat16)
    d_qkv = d_qkv.reshape(latent_count, seq_len, 3 * model_width)
    g_query_b = jnp.sum(d_qkv[:, :, :model_width], axis=(0, 1), dtype=jnp.float32)
    g_value_b = jnp.sum(d_qkv[:, :, 2 * model_width :], axis=(0, 1), dtype=jnp.float32)
    d_normed_in = jnp.einsum("bsf,df->bsd", d_qkv, qkv_weight, preferred_element_type=jnp.float32)
    _, pull_in = jax.vjp(modulate, residual_state, shift_attn, scale_attn)
    d_stream, d_shift_attn, d_scale_attn = pull_in(d_normed_in)
    d_stream = d_stream + d_middle
    d_modulation = jnp.concatenate(
        [d_shift_attn, d_scale_attn, d_gate_attn, d_shift_mlp, d_scale_mlp, d_gate_mlp], axis=-1
    ).astype(jnp.bfloat16)
    pairs = (
        (normed_in, d_qkv),
        (attended, d_attn),
        (normed_mid, d_pre),
        (activated, d_mlp),
    )
    pairs = [[side.reshape(-1, side.shape[-1]) for side in pair] for pair in pairs]
    return (d_stream, d_modulation, pairs, (g_query_b, g_value_b, g_proj_b, g_expand_b, g_reduce_b))


def on_device(
    latents,
    conditioning,
    cotangent,
    adaln_weight,
    adaln_bias,
    qkv_weight,
    query_bias,
    value_bias,
    proj_weight,
    proj_bias,
    expand_weight,
    expand_bias,
    reduce_weight,
    reduce_bias,
):
    shard_count = lax.axis_size(AXES)
    mesh_shape = (lax.axis_size("dp"), lax.axis_size("pair"))
    rows = qkv_weight.shape[1]
    in_kernels = rows % 8 == 0 and CHUNK % rows == 0
    here = lax.axis_index(AXES)
    stream = latents.astype(jnp.float32)
    cond_part = conditioning.astype(jnp.float32)
    adaln_size = adaln_bias.shape[1]
    adaln_columns = adaln_weight.reshape(LAYERS * rows, shard_count, adaln_size)
    adaln_columns = adaln_columns.transpose(1, 0, 2)
    own = conditioning.reshape(-1)
    more = -(-own.shape[0] // (8 * adaln_size)) * 8
    own = jnp.pad(own, (0, more * adaln_size - own.shape[0])).reshape(1, more, adaln_size)
    own = jnp.broadcast_to(own, (shard_count, more, adaln_size))
    adaln_columns = jnp.concatenate([adaln_columns, own], axis=1)
    adaln_columns = lax.all_to_all(adaln_columns, AXES, split_axis=0, concat_axis=0, tiled=True)
    conditioning_all = adaln_columns[:, LAYERS * rows :].reshape(shard_count, -1)
    conditioning_all = conditioning_all[:, : conditioning.size].reshape(-1, conditioning.shape[1])
    silu_low = jax.nn.silu(conditioning_all.astype(jnp.float32)).astype(jnp.bfloat16)
    silu_mine = lax.dynamic_slice_in_dim(silu_low, here * rows, rows, axis=1)
    modulation = []
    for layer in range(LAYERS):
        columns = adaln_columns[:, layer * rows : (layer + 1) * rows].reshape(-1, adaln_size)
        modulation.append(
            jnp.dot(silu_low, columns, preferred_element_type=jnp.float32)
            + adaln_bias[layer].astype(jnp.float32)
        )
    modulation = jnp.stack(modulation)
    modulation = lax.all_to_all(modulation, AXES, split_axis=1, concat_axis=2, tiled=True)
    shards = (qkv_weight, proj_weight, expand_weight, reduce_weight)
    bias_members = (query_bias, value_bias, proj_bias, expand_bias, reduce_bias)
    bias_sizes = [member.shape[1] for member in bias_members]
    room = BIAS_TILE[0] * BIAS_TILE[1]
    bias_row = jnp.concatenate(bias_members, axis=1).reshape(-1)
    bias_row = jnp.pad(bias_row, (0, room - bias_row.shape[0])).reshape(BIAS_TILE)
    weights = []
    for layer in range(LAYERS):
        block = bias_row if layer == 0 else None
        if in_kernels:
            found = gather_weights(mesh_shape, shards, block, layer)
        else:
            found = plain_gather(shards, block, layer)
        weights.append(found[0])
        if layer == 0:
            bias_rows = found[1]
    gathered = []
    at = 0
    for layer in range(LAYERS):
        biases = []
        for size in bias_sizes:
            biases.append(bias_rows[:, at : at + size].reshape(-1))
            at += size
        query_b, value_b, proj_b, expand_b, reduce_b = biases
        qkv_w, proj_w, expand_w, reduce_w = weights[layer]
        gathered.append(
            (qkv_w, query_b, value_b, proj_w, proj_b, expand_w, expand_b, reduce_w, reduce_b)
        )
    stored = [None] * LAYERS
    for layer in range(LAYERS):
        stream, stored[layer] = forward_layer(stream, modulation[layer], gathered[layer])
    outputs = stream.astype(jnp.bfloat16)
    upstream = cotangent.astype(jnp.float32)
    d_mods = [None] * LAYERS
    terms = [None] * LAYERS
    reduce = functools.partial(reduce_grads, mesh_shape) if in_kernels else plain_reduce
    for layer in reversed(range(LAYERS)):
        upstream, d_mods[layer], pairs, bias_grads = backward_layer(
            upstream, gathered[layer], stored[layer]
        )
        flat = jnp.concatenate([grad.reshape(shard_count, -1) for grad in bias_grads], axis=1)
        flat = jnp.pad(flat, ((0, 0), (0, room - flat.shape[1]))).astype(GRAD_DTYPE)
        terms[layer] = (pairs, flat)
    terms[1], d_modulation = lax.optimization_barrier((terms[1], jnp.stack(d_mods)))
    d_mods = spread(d_modulation.transpose(1, 0, 2))
    summed = [None, reduce(*terms[1], number=0)]
    d_mods, summed[1] = lax.optimization_barrier((d_mods, summed[1]))
    g_adaln_w = []
    g_adaln_b = []
    d_silu = 0.0
    for layer in range(LAYERS):
        part = d_mods[:, layer]
        g_adaln_w.append(
            jnp.einsum("bd,bf->df", silu_mine, part, preferred_element_type=jnp.float32)
        )
        mine = lax.dynamic_slice_in_dim(part, here * adaln_size, adaln_size, axis=1)
        g_adaln_b.append(jnp.sum(mine, axis=0, dtype=jnp.float32))
        d_silu = d_silu + jnp.einsum(
            "bf,df->bd", part, adaln_weight[layer], preferred_element_type=jnp.float32
        )
    terms[0], d_silu = lax.optimization_barrier((terms[0], d_silu))
    summed[0] = reduce(*terms[0], number=1)
    d_silu = lax.all_to_all(d_silu, AXES, split_axis=0, concat_axis=1, tiled=True)
    _, pull_silu = jax.vjp(jax.nn.silu, cond_part)
    grad_conditioning = pull_silu(d_silu)[0]
    small = [[] for _ in bias_sizes]
    for layer in range(LAYERS):
        flat = summed[layer][4].reshape(-1)
        at = 0
        for number, size in enumerate(bias_sizes):
            small[number].append(flat[at : at + size])
            at += size
    large = [[summed[layer][member] for layer in range(LAYERS)] for member in range(4)]
    stacked = [
        g_adaln_w,
        g_adaln_b,
        large[0],
        small[0],
        small[1],
        large[1],
        small[2],
        large[2],
        small[3],
        large[3],
        small[4],
    ]
    stacked = [jnp.stack(member) for member in stacked]
    return tuple([outputs, upstream, grad_conditioning] + stacked)


def solution(mesh):
    in_specs = (
        P(("dp", "pair"), None, None),
        P(("dp", "pair"), None),
        P(("dp", "pair"), None, None),
        P(None, ("dp", "pair"), None),
        P(None, ("dp", "pair")),
        P(None, ("dp", "pair"), None),
        P(None, ("dp", "pair")),
        P(None, ("dp", "pair")),
        P(None, ("dp", "pair"), None),
        P(None, ("dp", "pair")),
        P(None, ("dp", "pair"), None),
        P(None, ("dp", "pair")),
        P(None, ("dp", "pair"), None),
        P(None, ("dp", "pair")),
    )
    out_specs = (
        P(("dp", "pair"), None, None),
        P(("dp", "pair"), None, None),
        P(("dp", "pair"), None),
        P(None, ("dp", "pair"), None),
        P(None, ("dp", "pair")),
        P(None, ("dp", "pair"), None),
        P(None, ("dp", "pair")),
        P(None, ("dp", "pair")),
        P(None, ("dp", "pair"), None),
        P(None, ("dp", "pair")),
        P(None, ("dp", "pair"), None),
        P(None, ("dp", "pair")),
        P(None, ("dp", "pair"), None),
        P(None, ("dp", "pair")),
    )
    return jax.shard_map(
        on_device, mesh=mesh, in_specs=in_specs, out_specs=out_specs, check_vma=False
    )
```

```python
import functools

import jax
import jax.numpy as jnp
from jax import lax
from jax.experimental import pallas as pl
from jax.experimental.pallas import tpu as pltpu
from jax.sharding import PartitionSpec as P

HEADS = 12
HEAD = 64
LAYERS = 2


EPSILON = 1e-06


def gelu_tanh(values):
    return jax.nn.gelu(values, approximate=True)


AXES = ("dp", "pair")
LANES = 128
GRAD_DTYPE = jnp.bfloat16


MESH_ID = pl.DeviceIdType.MESH
BIAS_TILE = (16, 128)
CHUNK = 384
SIDE_LAG = 1
CORNER_LAG = 2
OFFSETS = (0, 1, 2, 3, 4)
ORDER = (1, 3, 2, 0, 4)
VMEM_LIMIT = 60 * 1024 * 1024


class Place:
    def __init__(self):
        self.line = lax.axis_size("dp") // 4
        spot = lax.axis_index("dp")
        self.z, self.y, self.c = spot // 4, (spot // 2) % 2, spot % 2
        self.x = lax.axis_index("pair")

    def device(self, z=None, y=None, c=None, x=None):
        z = self.z if z is None else z
        y = self.y if y is None else y
        c = self.c if c is None else c
        x = self.x if x is None else x
        return ((z * 2 + y) * 2 + c, x)

    def partner(self, axis):
        return self.device(**{axis: 1 - getattr(self, axis)})

    def greet(self):
        barrier = pltpu.get_barrier_semaphore()
        for axis in ("y", "c", "x"):
            pl.semaphore_signal(
                barrier, inc=1, device_id=self.partner(axis), device_id_type=MESH_ID
            )

        @pl.when(self.z > 0)
        def _():
            pl.semaphore_signal(
                barrier, inc=1, device_id=self.device(z=self.z - 1), device_id_type=MESH_ID
            )

        @pl.when(self.z < self.line - 1)
        def _():
            pl.semaphore_signal(
                barrier, inc=1, device_id=self.device(z=self.z + 1), device_id_type=MESH_ID
            )

        ends = (self.z > 0).astype(jnp.int32) + (self.z < self.line - 1).astype(jnp.int32)
        pl.semaphore_wait(barrier, 3 + ends)


def remote(src, dst, send, recv, device):
    return pltpu.make_async_remote_copy(
        src_ref=src,
        dst_ref=dst,
        send_sem=send,
        recv_sem=recv,
        device_id=device,
        device_id_type=MESH_ID,
    )


def gather_kernel(members, *refs):
    count = len(members)
    input_count = len(refs) - 9 - count
    ins, outs = refs[:input_count], refs[input_count : input_count + count]
    (local, zs, as_, bs, cs, zr, ar, br, cr) = refs[input_count + count :]
    place = Place()
    line, z, y, c, x = place.line, place.z, place.y, place.c, place.x
    place.greet()

    def source(k):
        number, layer = members[k]
        return ins[number] if layer is None else ins[number].at[layer]

    def at(k, zz, flip_y=False, flip_x=False):
        return outs[k].at[zz, 1 - y if flip_y else y, c, 1 - x if flip_x else x]

    def z_copy(k, src, zz, up):
        to = place.device(z=z + 1 if up else z - 1)
        return remote(src, at(k, zz), zs.at[k, 0 if up else 1, zz], zr.at[k, zz], to)

    def y_copy(k, src, dst, step, zz):
        return remote(src, dst, as_.at[k, step], ar.at[k, step, zz], place.partner("y"))

    def x_copy(k, src, dst, step, zz):
        return remote(src, dst, bs.at[k, step], br.at[k, step, zz], place.partner("x"))

    def c_copy(k, src, dst):
        return remote(src, dst, cs.at[k], cr.at[k], place.partner("c"))

    def spread(k, src, zz):
        dst = at(k, zz)
        y_copy(k, src, dst, 0, zz).start()
        x_copy(k, src, dst, 0, zz).start()
        c_copy(k, src, dst).start()

    def line_step(k, d):
        if d == 0:
            src = source(k)

            @pl.when(z < line - 1)
            def _():
                z_copy(k, src, z, True).start()

            @pl.when(z > 0)
            def _():
                z_copy(k, src, z, False).start()

            spread(k, src, z)
            pltpu.make_async_copy(src, at(k, z), local.at[k]).start()
            return

        @pl.when(z >= d)
        def _():
            zz = z - d
            z_copy(k, at(k, zz), zz, True).wait_recv()

            @pl.when(z < line - 1)
            def _():
                z_copy(k, at(k, zz), zz, True).start()

            spread(k, at(k, zz), zz)

        @pl.when(z + d < line)
        def _():
            zz = z + d
            z_copy(k, at(k, zz), zz, False).wait_recv()

            @pl.when(z > 0)
            def _():
                z_copy(k, at(k, zz), zz, False).start()

            spread(k, at(k, zz), zz)

    def at_distance(d, use):
        if d == 0:
            use(z)
            return

        @pl.when(z >= d)
        def _():
            use(z - d)

        @pl.when(z + d < line)
        def _():
            use(z + d)

    def y_first(zz):
        return zz % 2 == 0

    def side_step(k, d):
        def use(zz):
            over_y, over_x = at(k, zz, flip_y=True), at(k, zz, flip_x=True)
            y_copy(k, over_y, over_y, 0, zz).wait_recv()

            @pl.when(y_first(zz))
            def _():
                x_copy(k, over_y, over_y, 1, zz).start()

            c_copy(k, over_y, over_y).start()
            x_copy(k, over_x, over_x, 0, zz).wait_recv()

            @pl.when(jnp.logical_not(y_first(zz)))
            def _():
                y_copy(k, over_x, over_x, 1, zz).start()

            c_copy(k, over_x, over_x).start()

        at_distance(d, use)

    def corner_step(k, d):
        def use(zz):
            corner = at(k, zz, flip_y=True, flip_x=True)

            @pl.when(y_first(zz))
            def _():
                x_copy(k, corner, corner, 1, zz).wait_recv()

            @pl.when(jnp.logical_not(y_first(zz)))
            def _():
                y_copy(k, corner, corner, 1, zz).wait_recv()

            c_copy(k, corner, corner).start()

        at_distance(d, use)

    for wave in range(count + line + CORNER_LAG):
        for k in range(count):
            step = wave - k
            if 0 <= step < line:
                line_step(k, step)
            if 0 <= step - SIDE_LAG < line:
                side_step(k, step - SIDE_LAG)
            if 0 <= step - CORNER_LAG < line:
                corner_step(k, step - CORNER_LAG)

    for k in range(count):
        pltpu.make_async_copy(source(k), at(k, z), local.at[k]).wait()
        theirs = outs[k].at[:, :, 1 - c]
        own = outs[k].at[:, :, c]
        c_copy(k, theirs, theirs).wait_recv()
        c_copy(k, own, own).wait_send()
        column = outs[k].at[:, y, c, x]
        y_copy(k, column, column, 0, 0).wait_send()
        x_copy(k, column, column, 0, 0).wait_send()
        part = outs[k].at[pl.ds(0, line // 2), y, c, x]
        y_copy(k, part, part, 1, 0).wait_send()
        x_copy(k, part, part, 1, 0).wait_send()
        for zz in range(line):

            @pl.when((z < line - 1) & (zz <= z))
            def _():
                z_copy(k, at(k, zz), zz, True).wait_send()

            @pl.when((z > 0) & (zz >= z))
            def _():
                z_copy(k, at(k, zz), zz, False).wait_send()


def gather_weights(mesh_shape, shards, bias_block, layer):
    dp_size, pair_size = mesh_shape
    line = dp_size // 4
    members = []
    outs = []
    operands = list(shards)
    if bias_block is not None:
        members.append((len(shards), None))
        outs.append(bias_block)
        operands.append(bias_block)
    for number, shard in enumerate(shards):
        members.append((number, layer))
        outs.append(shard[layer])
    count = len(members)
    shapes = [
        jax.ShapeDtypeStruct((line, 2, 2, pair_size) + out.shape, out.dtype) for out in outs
    ]
    dma = pltpu.SemaphoreType.DMA
    full = pl.pallas_call(
        functools.partial(gather_kernel, members),
        out_shape=shapes,
        in_specs=[pl.BlockSpec(memory_space=pl.ANY)] * len(operands),
        out_specs=[pl.BlockSpec(memory_space=pl.ANY)] * count,
        scratch_shapes=[
            dma((count,)),
            dma((count, 2, line)),
            dma((count, 2)),
            dma((count, 2)),
            dma((count,)),
            dma((count, line)),
            dma((count, 2, line)),
            dma((count, 2, line)),
            dma((count,)),
        ],
        compiler_params=pltpu.CompilerParams(collective_id=layer, has_side_effects=True),
        cost_estimate=pl.CostEstimate(flops=0, bytes_accessed=200_000_000, transcendentals=0),
        name="gather_weights_%d" % layer,
    )(*operands)
    weights = [weight.reshape(-1, weight.shape[-1]) for weight in full[-len(shards) :]]
    biases = None if bias_block is None else full[0].reshape(dp_size * pair_size, -1)
    return weights, biases


def reduce_kernel(count, pair_count, *refs):
    pairs = [(refs[2 * k], refs[2 * k + 1]) for k in range(pair_count)]
    at = 2 * pair_count
    given = list(refs[at : at + count - pair_count])
    at += len(given)
    outs = refs[at : at + count]
    at += count
    full = list(refs[at : at + pair_count]) + given
    at += pair_count
    from_c, from_b, from_a, from_low, from_high = [
        refs[at + count * j : at + count * (j + 1)] for j in range(5)
    ]
    at += 5 * count
    c_send, c_recv, b_send, b_recv, a_send, a_recv, up_send, up_recv, down_send, down_recv = refs[
        at:
    ]
    place = Place()
    line, z, y, c, x = place.line, place.z, place.y, place.c, place.x
    half = line // 2
    place.greet()

    def axes(zz):
        return ("x", "y") if zz % 2 == 0 else ("y", "x")

    def add(total_ref, total_at, more_ref, more_at):
        total_ref[total_at] = (
            total_ref[total_at].astype(jnp.float32) + more_ref[more_at].astype(jnp.float32)
        ).astype(total_ref.dtype)

    def c_copy(k, zz):
        return remote(
            full[k].at[zz, :, 1 - c],
            from_c[k].at[zz],
            c_send.at[k, zz],
            c_recv.at[k, zz],
            place.partner("c"),
        )

    def b_copy(k, zz):
        first = axes(zz)[0]
        src = from_c[k].at[zz, :, 1 - x] if first == "x" else from_c[k].at[zz, 1 - y]
        return remote(
            src, from_b[k].at[zz], b_send.at[k, zz], b_recv.at[k, zz], place.partner(first)
        )

    def a_copy(k, zz):
        second = axes(zz)[1]
        other = 1 - getattr(place, second)
        return remote(
            from_b[k].at[zz, other],
            from_a[k].at[zz],
            a_send.at[k, zz],
            a_recv.at[k, zz],
            place.partner(second),
        )

    def up_copy(k, t, src):
        return remote(
            src, from_low[k].at[t], up_send.at[k, t], up_recv.at[k, t], place.device(z=z + 1)
        )

    def down_copy(k, t, src):
        return remote(
            src, from_high[k].at[t], down_send.at[k, t], down_recv.at[k, t], place.device(z=z - 1)
        )

    def zs_of(h):
        return range(h * half, (h + 1) * half)

    def compute(k, h):
        if k < pair_count:
            left, right = pairs[k]
            rows = full[k].shape[4]
            height = full[k].shape[0] * 8 * rows // 2
            blocks = CHUNK // rows
            wide = right.shape[1]
            for chunk in range(height // CHUNK):
                base = h * half * 8 + chunk * blocks

                def tile(j, carry, chunk=chunk, base=base):
                    columns = pl.ds(pl.multiple_of(j * 768, 768), 768)
                    product = lax.dot_general(
                        left[:, h * height + chunk * CHUNK : h * height + (chunk + 1) * CHUNK],
                        right[:, columns],
                        (((0,), (0,)), ((), ())),
                        preferred_element_type=jnp.float32,
                    )
                    for block in range(blocks):
                        n = base + block
                        full[k][n // 8, (n // 4) % 2, (n // 2) % 2, n % 2, :, columns] = product[
                            block * rows : (block + 1) * rows
                        ].astype(jnp.bfloat16)
                    return carry

                lax.fori_loop(0, wide // 768, tile, 0)
        for zz in zs_of(h):
            c_copy(k, zz).start()

    def after_c(k, h):
        def sweep(zz, other):
            for side in range(2):
                yy, xx = (side, other) if axes(zz)[0] == "x" else (other, side)
                add(from_c[k], (zz, yy, xx), full[k], (zz, yy, c, xx))

        for zz in zs_of(h):
            mine = getattr(place, axes(zz)[0])
            c_copy(k, zz).wait_recv()
            sweep(zz, 1 - mine)
            b_copy(k, zz).start()
        for zz in zs_of(h):
            sweep(zz, getattr(place, axes(zz)[0]))

    def after_b(k, h):
        def sweep(zz, side):
            yy, xx = (side, x) if axes(zz)[0] == "x" else (y, side)
            add(from_b[k], (zz, side), from_c[k], (zz, yy, xx))

        for zz in zs_of(h):
            mine = getattr(place, axes(zz)[1])
            b_copy(k, zz).wait_recv()
            sweep(zz, 1 - mine)
            a_copy(k, zz).start()
        for zz in zs_of(h):
            sweep(zz, getattr(place, axes(zz)[1]))

    def after_a(k, h):
        for zz in zs_of(h):
            a_copy(k, zz).wait_recv()
            add(from_a[k], (zz,), from_b[k], (zz, getattr(place, axes(zz)[1])))

    def hop(k, h, step):
        for t in reversed(range(h * half, (h + 1) * half)):

            @pl.when((z == step) & (z < t))
            def _():
                if step == 0:
                    up_copy(k, t, from_a[k].at[t]).start()
                else:
                    up_copy(k, t, from_low[k].at[t]).wait_recv()
                    add(from_low[k], (t,), from_a[k], (t,))
                    up_copy(k, t, from_low[k].at[t]).start()

        for t in range(h * half, (h + 1) * half):

            @pl.when((z == line - 1 - step) & (z > t))
            def _():
                if step == 0:
                    down_copy(k, t, from_a[k].at[t]).start()
                else:
                    down_copy(k, t, from_high[k].at[t]).wait_recv()
                    add(from_high[k], (t,), from_a[k], (t,))
                    down_copy(k, t, from_high[k].at[t]).start()

    def finish(k, h):
        for t in range(h * half, (h + 1) * half):

            @pl.when(z == t)
            def _():
                total = from_a[k][t].astype(jnp.float32)
                if t > 0:
                    up_copy(k, t, from_low[k].at[t]).wait_recv()
                    total = total + from_low[k][t].astype(jnp.float32)
                if t < line - 1:
                    down_copy(k, t, from_high[k].at[t]).wait_recv()
                    total = total + from_high[k][t].astype(jnp.float32)
                outs[k][...] = total

    def settle(k, h):
        for t in zs_of(h):
            c_copy(k, t).wait_send()
            b_copy(k, t).wait_send()
            a_copy(k, t).wait_send()

            @pl.when(z < t)
            def _():
                up_copy(k, t, from_a[k].at[t]).wait_send()

            @pl.when(z > t)
            def _():
                down_copy(k, t, from_a[k].at[t]).wait_send()

    units = [(k, h) for k in ORDER if k < count for h in range(2)]
    stages = [compute, after_c, after_b, after_a]
    stages += [functools.partial(hop, step=step) for step in range(line)]
    stages += [finish]
    offsets = list(OFFSETS) + [OFFSETS[-1] + 1 + step for step in range(line)]
    for wave in range(len(units) + offsets[-1]):
        for number, (k, h) in enumerate(units):
            if wave - number in offsets:
                stages[offsets.index(wave - number)](k, h)
    for k, h in units:
        settle(k, h)


def reduce_grads(mesh_shape, pairs, bias_rows, number):
    dp_size, pair_size = mesh_shape
    shard_count = dp_size * pair_size
    line = dp_size // 4
    lead = (line, 2, 2, pair_size)
    low = jnp.bfloat16
    operands = [side for pair in pairs for side in pair]
    shapes = [(left.shape[1] // shard_count, right.shape[1]) for left, right in pairs]
    scratch = [pltpu.VMEM(lead + shape, low) for shape in shapes]
    if bias_rows is not None:
        operands.append(bias_rows.reshape(lead + BIAS_TILE))
        shapes.append(BIAS_TILE)
    count = len(shapes)
    for space in ((line, 2, 2), (line, 2), (line,), (line,), (line,)):
        scratch += [pltpu.VMEM(space + shape, low) for shape in shapes]
    dma = pltpu.SemaphoreType.DMA
    scratch += [dma((count, line))] * 10
    vmem = pl.BlockSpec(memory_space=pltpu.VMEM)
    return pl.pallas_call(
        functools.partial(reduce_kernel, count, len(pairs)),
        out_shape=[jax.ShapeDtypeStruct(shape, jnp.float32) for shape in shapes],
        in_specs=[vmem] * len(operands),
        out_specs=[vmem] * count,
        scratch_shapes=scratch,
        compiler_params=pltpu.CompilerParams(
            collective_id=LAYERS + number, has_side_effects=True, vmem_limit_bytes=VMEM_LIMIT
        ),
        cost_estimate=pl.CostEstimate(flops=0, bytes_accessed=150_000_000, transcendentals=0),
        name="reduce_grads_%d" % number,
    )(*operands)


def spread(values):
    count = lax.axis_size(AXES)
    copies = jnp.broadcast_to(values[None], (count,) + values.shape)
    copies = lax.all_to_all(copies, AXES, split_axis=0, concat_axis=0, tiled=True)
    return copies.reshape((-1,) + values.shape[1:])


def plain_gather(shards, bias_block, layer):
    weights = [lax.all_gather(shard[layer], AXES, axis=0, tiled=True) for shard in shards]
    if bias_block is None:
        return weights, None
    return weights, lax.all_gather(bias_block.reshape(1, -1), AXES, axis=0, tiled=True)


def plain_reduce(pairs, bias_rows, number):
    grads = []
    for left, right in pairs:
        product = jnp.einsum("tk,tn->kn", left, right, preferred_element_type=jnp.float32)
        grads.append(product.astype(GRAD_DTYPE))
    if bias_rows is not None:
        grads.append(bias_rows)
    return [
        lax.psum_scatter(grad, AXES, scatter_dimension=0, tiled=True).astype(jnp.float32)
        for grad in grads
    ]


TOKENS_NT = (((1,), (1,)), ((), ()))
TOKENS_TN = (((0,), (0,)), ((), ()))
WIDE = 2 * HEAD
STEP = 768


def dot32(left, right, dims=(((1,), (0,)), ((), ()))):
    return lax.dot_general(left, right, dims, preferred_element_type=jnp.float32)


def standardize(values):
    centre = values - jnp.mean(values, axis=-1, keepdims=True)
    inverse = lax.rsqrt(jnp.mean(centre * centre, axis=-1, keepdims=True) + EPSILON)
    return centre * inverse, inverse


def head_masks():
    lane = lax.broadcasted_iota(jnp.int32, (1, WIDE), 1)
    first = (lane < HEAD).astype(jnp.float32)
    return lane < HEAD, (first.astype(jnp.bfloat16), (1.0 - first).astype(jnp.bfloat16))


def softmax_parts(query, keys):
    scores = dot32(query, keys, TOKENS_NT) * HEAD ** (-0.5)
    weights = jnp.exp(scores - jnp.max(scores, axis=-1, keepdims=True))
    return weights * (1.0 / jnp.sum(weights, axis=-1, keepdims=True))


def forward_steps(seq, refs):
    (stream, mod, qkv_w, qkv_b, proj_w, proj_b, expand_w, expand_b, reduce_w, reduce_b) = refs[:10]
    (normed_in, qkv, attended, attn_out, middle, normed_mid, pre_act, activated, mlp_out, out) = refs[
        10:
    ]
    tokens, width = stream.shape
    latents = tokens // seq
    hidden = pre_act.shape[1]
    groups = width // WIDE

    def row(b, number):
        return mod[b * 6 + number : b * 6 + number + 1, :]

    def rows(b):
        return slice(b * seq, (b + 1) * seq)

    def enter(b):
        values, _ = standardize(stream[rows(b), :])
        values = values * (1.0 + row(b, 1)) + row(b, 0)
        normed_in[rows(b), :] = values.astype(jnp.bfloat16)

    def project(j):
        at = slice(j * STEP, (j + 1) * STEP)
        qkv[:, at] = (dot32(normed_in[...], qkv_w[:, at]) + qkv_b[:, at]).astype(jnp.bfloat16)

    def attend(b, low, high):
        is_first, masks = head_masks()

        def one(p, carry):
            here = rows(b)
            query = qkv[here, pl.ds(pl.multiple_of(p * WIDE, WIDE), WIDE)]
            keys = qkv[here, pl.ds(pl.multiple_of(width + p * WIDE, WIDE), WIDE)]
            values = qkv[here, pl.ds(pl.multiple_of(2 * width + p * WIDE, WIDE), WIDE)]
            parts = [
                dot32(softmax_parts(query * mask, keys).astype(jnp.bfloat16), values)
                for mask in masks
            ]
            attended[here, pl.ds(pl.multiple_of(p * WIDE, WIDE), WIDE)] = jnp.where(
                is_first, parts[0], parts[1]
            ).astype(jnp.bfloat16)
            return carry

        lax.fori_loop(low, high, one, 0)

    def leave(b):
        result = dot32(attended[rows(b), :], proj_w[...]) + proj_b[...]
        attn_out[rows(b), :] = result
        state = stream[rows(b), :] + row(b, 2) * result
        middle[rows(b), :] = state
        values, _ = standardize(state)
        values = values * (1.0 + row(b, 4)) + row(b, 3)
        normed_mid[rows(b), :] = values.astype(jnp.bfloat16)

    def expand(j):
        at = slice(j * STEP, (j + 1) * STEP)
        before = dot32(normed_mid[...], expand_w[:, at]) + expand_b[:, at]
        pre_act[:, at] = before
        activated[:, at] = gelu_tanh(before).astype(jnp.bfloat16)

    def contract(b):
        result = dot32(activated[rows(b), :], reduce_w[...]) + reduce_b[...]
        mlp_out[rows(b), :] = result
        out[rows(b), :] = middle[rows(b), :] + row(b, 5) * result

    steps = [functools.partial(enter, b) for b in range(latents)]
    steps += [functools.partial(project, j) for j in range(3 * width // STEP)]
    third = groups // 3
    for b in range(latents):
        for low in range(0, groups, third):
            steps.append(functools.partial(attend, b, low, low + third))
    steps += [functools.partial(leave, b) for b in range(latents)]
    steps += [functools.partial(expand, j) for j in range(hidden // STEP)]
    steps += [functools.partial(contract, b) for b in range(latents)]
    return steps


def forward_operands(stream, modulation, gathered):
    (qkv_w, query_b, value_b, proj_w, proj_b, expand_w, expand_b, reduce_w, reduce_b) = gathered
    latents, seq, width = stream.shape
    qkv_b = jnp.concatenate([query_b, jnp.zeros_like(query_b), value_b])
    flat = [bias.astype(jnp.float32)[None] for bias in (qkv_b, proj_b, expand_b, reduce_b)]
    operands = [stream.reshape(-1, width), modulation.reshape(latents * 6, width)]
    for weight, bias in zip((qkv_w, proj_w, expand_w, reduce_w), flat):
        operands += [weight, bias]
    return operands


def forward_shapes(tokens, width, hidden):
    low, high = jnp.bfloat16, jnp.float32
    kinds = [(width, low), (3 * width, low), (width, low), (width, high), (width, high)]
    kinds += [(width, low), (hidden, high), (hidden, low), (width, high), (width, high)]
    return [jax.ShapeDtypeStruct((tokens, columns), kind) for columns, kind in kinds]


def forward_layer(stream, modulation, gathered):
    latents, seq, width = stream.shape
    operands = forward_operands(stream, modulation, gathered)

    def kernel(*refs):
        for step in forward_steps(seq, refs):
            step()

    vmem = pl.BlockSpec(memory_space=pltpu.VMEM)
    shapes = forward_shapes(latents * seq, width, operands[6].shape[1])
    saved = pl.pallas_call(
        kernel,
        out_shape=shapes,
        in_specs=[vmem] * len(operands),
        out_specs=[vmem] * len(shapes),
        compiler_params=pltpu.CompilerParams(vmem_limit_bytes=VMEM_LIMIT),
        name="forward_layer",
    )(*operands)
    return saved[-1].reshape(stream.shape), (operands[0], operands[1], *saved[:-1])


def backward_kernel(seq, *refs):
    (upstream, mod, stream, qkv, attn_out, middle, pre_act, mlp_out) = refs[:8]
    (qkv_w, proj_w, expand_w, reduce_w) = refs[8:12]
    (d_mlp, d_pre, d_attn, d_qkv, d_stream, d_mod) = refs[12:18]
    (g_reduce_b, g_expand_b, g_proj_b, g_qkv_b) = refs[18:22]
    (d_normed, d_middle, d_attended) = refs[22:]
    tokens, width = stream.shape
    latents = tokens // seq
    hidden = pre_act.shape[1]
    groups = width // WIDE
    low = jnp.bfloat16

    def row(b, number):
        return mod[b * 6 + number : b * 6 + number + 1, :]

    def put(b, number, value):
        d_mod[b * 6 + number : b * 6 + number + 1, :] = jnp.sum(value, axis=0, keepdims=True)

    def rows(b):
        return slice(b * seq, (b + 1) * seq)

    def total(value):
        return jnp.sum(value.astype(jnp.float32), axis=0, keepdims=True)

    g_reduce_b[...] = jnp.zeros_like(g_reduce_b)
    g_proj_b[...] = jnp.zeros_like(g_proj_b)
    for b in range(latents):
        above = upstream[rows(b), :]
        put(b, 5, above * mlp_out[rows(b), :])
        value = (row(b, 5) * above).astype(low)
        d_mlp[rows(b), :] = value
        g_reduce_b[...] += total(value)

    d_normed[...] = jnp.zeros_like(d_normed)

    def through(j, carry):
        at = pl.ds(pl.multiple_of(j * STEP, STEP), STEP)
        inner = dot32(d_mlp[...], reduce_w[at, :], TOKENS_NT)
        u = pre_act[:, at]
        rate = (2.0 / jnp.pi) ** 0.5
        bend = jnp.tanh(rate * (u + 0.044715 * (u * u * u)))
        slope = 0.5 * (1.0 + bend) + 0.5 * u * (1.0 - bend * bend) * rate * (
            1.0 + 3.0 * 0.044715 * (u * u)
        )
        value = (inner * slope).astype(low)
        d_pre[:, at] = value
        g_expand_b[:, at] = total(value)
        d_normed[...] += dot32(value, expand_w[:, at], TOKENS_NT)
        return carry

    lax.fori_loop(0, hidden // STEP, through, 0)

    def norm_back(b, source, scale_row, shift_row):
        unit, inverse = standardize(source[rows(b), :])
        flow = d_normed[rows(b), :]
        put(b, shift_row, flow)
        put(b, scale_row, flow * unit)
        flow = flow * (1.0 + row(b, scale_row))
        mean = jnp.mean(flow, axis=-1, keepdims=True)
        along = jnp.mean(flow * unit, axis=-1, keepdims=True)
        return inverse * (flow - mean - unit * along)

    for b in range(latents):
        value = norm_back(b, middle, 4, 3) + upstream[rows(b), :]
        d_middle[rows(b), :] = value
        put(b, 2, value * attn_out[rows(b), :])
        value = (row(b, 2) * value).astype(low)
        d_attn[rows(b), :] = value
        g_proj_b[...] += total(value)
    d_attended[...] = dot32(d_attn[...], proj_w[...], TOKENS_NT).astype(low)

    is_first, masks = head_masks()
    root = HEAD ** (-0.5)
    for b in range(latents):

        def one(p, carry, b=b):
            here = rows(b)
            at_q = pl.ds(pl.multiple_of(p * WIDE, WIDE), WIDE)
            at_k = pl.ds(pl.multiple_of(width + p * WIDE, WIDE), WIDE)
            at_v = pl.ds(pl.multiple_of(2 * width + p * WIDE, WIDE), WIDE)
            query, keys, values = qkv[here, at_q], qkv[here, at_k], qkv[here, at_v]
            flow = d_attended[here, at_q]
            parts = []
            for mask in masks:
                probs = softmax_parts(query * mask, keys)
                d_probs = dot32(flow * mask, values, TOKENS_NT)
                mixed = probs * d_probs
                d_scores = (mixed - probs * jnp.sum(mixed, axis=-1, keepdims=True)).astype(low)
                parts.append(
                    (
                        dot32(d_scores, keys) * root,
                        dot32(d_scores, query, TOKENS_TN) * root,
                        dot32(probs.astype(low), flow, TOKENS_TN),
                    )
                )
            for at, first, second in zip((at_q, at_k, at_v), *parts):
                d_qkv[here, at] = jnp.where(is_first, first, second).astype(low)
            return carry

        lax.fori_loop(0, groups, one, 0)

    for j in range(3):
        at = slice(j * width, (j + 1) * width)
        g_qkv_b[:, at] = total(d_qkv[:, at])
    d_normed[...] = dot32(d_qkv[...], qkv_w[...], TOKENS_NT)
    for b in range(latents):
        d_stream[rows(b), :] = d_middle[rows(b), :] + norm_back(b, stream, 1, 0)


def backward_layer(upstream, gathered, stored):
    (qkv_w, query_b, value_b, proj_w, proj_b, expand_w, expand_b, reduce_w, reduce_b) = gathered
    (stream, mod, normed_in, qkv, attended, attn_out, middle, normed_mid, pre_act) = stored[:9]
    activated, mlp_out = stored[9:]
    latents, seq, width = upstream.shape
    tokens, hidden = pre_act.shape
    low, high = jnp.bfloat16, jnp.float32
    shapes = [(tokens, width, low), (tokens, hidden, low), (tokens, width, low)]
    shapes += [(tokens, 3 * width, low), (tokens, width, high), (latents * 6, width, high)]
    shapes += [(1, width, high), (1, hidden, high), (1, width, high), (1, 3 * width, high)]
    operands = [upstream.reshape(tokens, width), mod, stream, qkv, attn_out, middle, pre_act]
    operands += [mlp_out, qkv_w, proj_w, expand_w, reduce_w]
    vmem = pl.BlockSpec(memory_space=pltpu.VMEM)
    found = pl.pallas_call(
        functools.partial(backward_kernel, seq),
        out_shape=[jax.ShapeDtypeStruct((m, n), kind) for m, n, kind in shapes],
        in_specs=[vmem] * len(operands),
        out_specs=[vmem] * len(shapes),
        scratch_shapes=[
            pltpu.VMEM((tokens, width), high),
            pltpu.VMEM((tokens, width), high),
            pltpu.VMEM((tokens, width), low),
        ],
        compiler_params=pltpu.CompilerParams(vmem_limit_bytes=VMEM_LIMIT),
        name="backward_layer",
    )(*operands)
    (d_mlp, d_pre, d_attn, d_qkv, d_stream, d_mod, g_reduce_b, g_expand_b, g_proj_b, g_qkv_b) = found
    pairs = [(normed_in, d_qkv), (attended, d_attn), (normed_mid, d_pre), (activated, d_mlp)]
    bias_grads = (g_qkv_b[:, :width], g_qkv_b[:, 2 * width :], g_proj_b, g_expand_b, g_reduce_b)
    d_modulation = d_mod.reshape(latents, 6 * width).astype(low)
    return d_stream.reshape(upstream.shape), d_modulation, pairs, bias_grads


def on_device(
    latents,
    conditioning,
    cotangent,
    adaln_weight,
    adaln_bias,
    qkv_weight,
    query_bias,
    value_bias,
    proj_weight,
    proj_bias,
    expand_weight,
    expand_bias,
    reduce_weight,
    reduce_bias,
):
    shard_count = lax.axis_size(AXES)
    mesh_shape = (lax.axis_size("dp"), lax.axis_size("pair"))
    rows = qkv_weight.shape[1]
    in_kernels = rows % 8 == 0 and CHUNK % rows == 0
    here = lax.axis_index(AXES)
    stream = latents.astype(jnp.float32)
    cond_part = conditioning.astype(jnp.float32)
    adaln_size = adaln_bias.shape[1]
    adaln_columns = adaln_weight.reshape(LAYERS * rows, shard_count, adaln_size)
    adaln_columns = adaln_columns.transpose(1, 0, 2)
    own = conditioning.reshape(-1)
    more = -(-own.shape[0] // (8 * adaln_size)) * 8
    own = jnp.pad(own, (0, more * adaln_size - own.shape[0])).reshape(1, more, adaln_size)
    own = jnp.broadcast_to(own, (shard_count, more, adaln_size))
    adaln_columns = jnp.concatenate([adaln_columns, own], axis=1)
    adaln_columns = lax.all_to_all(adaln_columns, AXES, split_axis=0, concat_axis=0, tiled=True)
    conditioning_all = adaln_columns[:, LAYERS * rows :].reshape(shard_count, -1)
    conditioning_all = conditioning_all[:, : conditioning.size].reshape(-1, conditioning.shape[1])
    silu_low = jax.nn.silu(conditioning_all.astype(jnp.float32)).astype(jnp.bfloat16)
    silu_mine = lax.dynamic_slice_in_dim(silu_low, here * rows, rows, axis=1)
    modulation = []
    for layer in range(LAYERS):
        columns = adaln_columns[:, layer * rows : (layer + 1) * rows].reshape(-1, adaln_size)
        modulation.append(
            jnp.dot(silu_low, columns, preferred_element_type=jnp.float32)
            + adaln_bias[layer].astype(jnp.float32)
        )
    modulation = jnp.stack(modulation)
    modulation = lax.all_to_all(modulation, AXES, split_axis=1, concat_axis=2, tiled=True)
    shards = (qkv_weight, proj_weight, expand_weight, reduce_weight)
    bias_members = (query_bias, value_bias, proj_bias, expand_bias, reduce_bias)
    bias_sizes = [member.shape[1] for member in bias_members]
    room = BIAS_TILE[0] * BIAS_TILE[1]
    bias_row = jnp.concatenate(bias_members, axis=1).reshape(-1)
    bias_row = jnp.pad(bias_row, (0, room - bias_row.shape[0])).reshape(BIAS_TILE)
    weights = []
    for layer in range(LAYERS):
        block = bias_row if layer == 0 else None
        if in_kernels:
            found = gather_weights(mesh_shape, shards, block, layer)
        else:
            found = plain_gather(shards, block, layer)
        weights.append(found[0])
        if layer == 0:
            bias_rows = found[1]
    gathered = []
    at = 0
    for layer in range(LAYERS):
        biases = []
        for size in bias_sizes:
            biases.append(bias_rows[:, at : at + size].reshape(-1))
            at += size
        query_b, value_b, proj_b, expand_b, reduce_b = biases
        qkv_w, proj_w, expand_w, reduce_w = weights[layer]
        gathered.append(
            (qkv_w, query_b, value_b, proj_w, proj_b, expand_w, expand_b, reduce_w, reduce_b)
        )
    stored = [None] * LAYERS
    for layer in range(LAYERS):
        stream, stored[layer] = forward_layer(stream, modulation[layer], gathered[layer])
    outputs = stream.astype(jnp.bfloat16)
    upstream = cotangent.astype(jnp.float32)
    d_mods = [None] * LAYERS
    terms = [None] * LAYERS
    reduce = functools.partial(reduce_grads, mesh_shape) if in_kernels else plain_reduce
    for layer in reversed(range(LAYERS)):
        upstream, d_mods[layer], pairs, bias_grads = backward_layer(
            upstream, gathered[layer], stored[layer]
        )
        flat = jnp.concatenate([grad.reshape(shard_count, -1) for grad in bias_grads], axis=1)
        flat = jnp.pad(flat, ((0, 0), (0, room - flat.shape[1]))).astype(GRAD_DTYPE)
        terms[layer] = (pairs, flat)
    terms[1], d_modulation = lax.optimization_barrier((terms[1], jnp.stack(d_mods)))
    d_mods = spread(d_modulation.transpose(1, 0, 2))
    summed = [None, reduce(*terms[1], number=0)]
    d_mods, summed[1] = lax.optimization_barrier((d_mods, summed[1]))
    g_adaln_w = []
    g_adaln_b = []
    d_silu = 0.0
    for layer in range(LAYERS):
        part = d_mods[:, layer]
        g_adaln_w.append(
            jnp.einsum("bd,bf->df", silu_mine, part, preferred_element_type=jnp.float32)
        )
        mine = lax.dynamic_slice_in_dim(part, here * adaln_size, adaln_size, axis=1)
        g_adaln_b.append(jnp.sum(mine, axis=0, dtype=jnp.float32))
        d_silu = d_silu + jnp.einsum(
            "bf,df->bd", part, adaln_weight[layer], preferred_element_type=jnp.float32
        )
    terms[0], d_silu = lax.optimization_barrier((terms[0], d_silu))
    summed[0] = reduce(*terms[0], number=1)
    d_silu = lax.all_to_all(d_silu, AXES, split_axis=0, concat_axis=1, tiled=True)
    _, pull_silu = jax.vjp(jax.nn.silu, cond_part)
    grad_conditioning = pull_silu(d_silu)[0]
    small = [[] for _ in bias_sizes]
    for layer in range(LAYERS):
        flat = summed[layer][4].reshape(-1)
        at = 0
        for number, size in enumerate(bias_sizes):
            small[number].append(flat[at : at + size])
            at += size
    large = [[summed[layer][member] for layer in range(LAYERS)] for member in range(4)]
    stacked = [
        g_adaln_w,
        g_adaln_b,
        large[0],
        small[0],
        small[1],
        large[1],
        small[2],
        large[2],
        small[3],
        large[3],
        small[4],
    ]
    stacked = [jnp.stack(member) for member in stacked]
    return tuple([outputs, upstream, grad_conditioning] + stacked)


def solution(mesh):
    in_specs = (
        P(("dp", "pair"), None, None),
        P(("dp", "pair"), None),
        P(("dp", "pair"), None, None),
        P(None, ("dp", "pair"), None),
        P(None, ("dp", "pair")),
        P(None, ("dp", "pair"), None),
        P(None, ("dp", "pair")),
        P(None, ("dp", "pair")),
        P(None, ("dp", "pair"), None),
        P(None, ("dp", "pair")),
        P(None, ("dp", "pair"), None),
        P(None, ("dp", "pair")),
        P(None, ("dp", "pair"), None),
        P(None, ("dp", "pair")),
    )
    out_specs = (
        P(("dp", "pair"), None, None),
        P(("dp", "pair"), None, None),
        P(("dp", "pair"), None),
        P(None, ("dp", "pair"), None),
        P(None, ("dp", "pair")),
        P(None, ("dp", "pair"), None),
        P(None, ("dp", "pair")),
        P(None, ("dp", "pair")),
        P(None, ("dp", "pair"), None),
        P(None, ("dp", "pair")),
        P(None, ("dp", "pair"), None),
        P(None, ("dp", "pair")),
        P(None, ("dp", "pair"), None),
        P(None, ("dp", "pair")),
    )
    return jax.shard_map(
        on_device, mesh=mesh, in_specs=in_specs, out_specs=out_specs, check_vma=False
    )
```

```python
import functools

import jax
import jax.numpy as jnp
from jax import lax
from jax.experimental import pallas as pl
from jax.experimental.pallas import tpu as pltpu
from jax.sharding import PartitionSpec as P

HEADS = 12
HEAD = 64
LAYERS = 2


EPSILON = 1e-06


def gelu_tanh(values):
    return jax.nn.gelu(values, approximate=True)


AXES = ("dp", "pair")
LANES = 128
GRAD_DTYPE = jnp.bfloat16


MESH_ID = pl.DeviceIdType.MESH
BIAS_TILE = (16, 128)
CHUNK = 384
SIDE_LAG = 1
CORNER_LAG = 2
OFFSETS = (0, 1, 2, 3, 4)
ORDERS = ((1, 3, 2, 0, 4), (8, 7, 5, 6, 9))
VMEM_LIMIT = 60 * 1024 * 1024


class Place:
    def __init__(self):
        self.line = lax.axis_size("dp") // 4
        spot = lax.axis_index("dp")
        self.z, self.y, self.c = spot // 4, (spot // 2) % 2, spot % 2
        self.x = lax.axis_index("pair")

    def device(self, z=None, y=None, c=None, x=None):
        z = self.z if z is None else z
        y = self.y if y is None else y
        c = self.c if c is None else c
        x = self.x if x is None else x
        return ((z * 2 + y) * 2 + c, x)

    def partner(self, axis):
        return self.device(**{axis: 1 - getattr(self, axis)})

    def greet(self):
        barrier = pltpu.get_barrier_semaphore()
        for axis in ("y", "c", "x"):
            pl.semaphore_signal(
                barrier, inc=1, device_id=self.partner(axis), device_id_type=MESH_ID
            )

        @pl.when(self.z > 0)
        def _():
            pl.semaphore_signal(
                barrier, inc=1, device_id=self.device(z=self.z - 1), device_id_type=MESH_ID
            )

        @pl.when(self.z < self.line - 1)
        def _():
            pl.semaphore_signal(
                barrier, inc=1, device_id=self.device(z=self.z + 1), device_id_type=MESH_ID
            )

        ends = (self.z > 0).astype(jnp.int32) + (self.z < self.line - 1).astype(jnp.int32)
        pl.semaphore_wait(barrier, 3 + ends)


def remote(src, dst, send, recv, device):
    return pltpu.make_async_remote_copy(
        src_ref=src,
        dst_ref=dst,
        send_sem=send,
        recv_sem=recv,
        device_id=device,
        device_id_type=MESH_ID,
    )


def gather_kernel(members, *refs):
    count = len(members)
    input_count = len(refs) - 9 - count
    ins, outs = refs[:input_count], refs[input_count : input_count + count]
    (local, zs, as_, bs, cs, zr, ar, br, cr) = refs[input_count + count :]
    place = Place()
    line, z, y, c, x = place.line, place.z, place.y, place.c, place.x
    place.greet()

    def source(k):
        number, layer = members[k]
        return ins[number] if layer is None else ins[number].at[layer]

    def at(k, zz, flip_y=False, flip_x=False):
        return outs[k].at[zz, 1 - y if flip_y else y, c, 1 - x if flip_x else x]

    def z_copy(k, src, zz, up):
        to = place.device(z=z + 1 if up else z - 1)
        return remote(src, at(k, zz), zs.at[k, 0 if up else 1, zz], zr.at[k, zz], to)

    def y_copy(k, src, dst, step, zz):
        return remote(src, dst, as_.at[k, step], ar.at[k, step, zz], place.partner("y"))

    def x_copy(k, src, dst, step, zz):
        return remote(src, dst, bs.at[k, step], br.at[k, step, zz], place.partner("x"))

    def c_copy(k, src, dst):
        return remote(src, dst, cs.at[k], cr.at[k], place.partner("c"))

    def spread(k, src, zz):
        dst = at(k, zz)
        y_copy(k, src, dst, 0, zz).start()
        x_copy(k, src, dst, 0, zz).start()
        c_copy(k, src, dst).start()

    def line_step(k, d):
        if d == 0:
            src = source(k)

            @pl.when(z < line - 1)
            def _():
                z_copy(k, src, z, True).start()

            @pl.when(z > 0)
            def _():
                z_copy(k, src, z, False).start()

            spread(k, src, z)
            pltpu.make_async_copy(src, at(k, z), local.at[k]).start()
            return

        @pl.when(z >= d)
        def _():
            zz = z - d
            z_copy(k, at(k, zz), zz, True).wait_recv()

            @pl.when(z < line - 1)
            def _():
                z_copy(k, at(k, zz), zz, True).start()

            spread(k, at(k, zz), zz)

        @pl.when(z + d < line)
        def _():
            zz = z + d
            z_copy(k, at(k, zz), zz, False).wait_recv()

            @pl.when(z > 0)
            def _():
                z_copy(k, at(k, zz), zz, False).start()

            spread(k, at(k, zz), zz)

    def at_distance(d, use):
        if d == 0:
            use(z)
            return

        @pl.when(z >= d)
        def _():
            use(z - d)

        @pl.when(z + d < line)
        def _():
            use(z + d)

    def y_first(zz):
        return zz % 2 == 0

    def side_step(k, d):
        def use(zz):
            over_y, over_x = at(k, zz, flip_y=True), at(k, zz, flip_x=True)
            y_copy(k, over_y, over_y, 0, zz).wait_recv()

            @pl.when(y_first(zz))
            def _():
                x_copy(k, over_y, over_y, 1, zz).start()

            c_copy(k, over_y, over_y).start()
            x_copy(k, over_x, over_x, 0, zz).wait_recv()

            @pl.when(jnp.logical_not(y_first(zz)))
            def _():
                y_copy(k, over_x, over_x, 1, zz).start()

            c_copy(k, over_x, over_x).start()

        at_distance(d, use)

    def corner_step(k, d):
        def use(zz):
            corner = at(k, zz, flip_y=True, flip_x=True)

            @pl.when(y_first(zz))
            def _():
                x_copy(k, corner, corner, 1, zz).wait_recv()

            @pl.when(jnp.logical_not(y_first(zz)))
            def _():
                y_copy(k, corner, corner, 1, zz).wait_recv()

            c_copy(k, corner, corner).start()

        at_distance(d, use)

    for wave in range(count + line + CORNER_LAG):
        for k in range(count):
            step = wave - k
            if 0 <= step < line:
                line_step(k, step)
            if 0 <= step - SIDE_LAG < line:
                side_step(k, step - SIDE_LAG)
            if 0 <= step - CORNER_LAG < line:
                corner_step(k, step - CORNER_LAG)

    for k in range(count):
        pltpu.make_async_copy(source(k), at(k, z), local.at[k]).wait()
        theirs = outs[k].at[:, :, 1 - c]
        own = outs[k].at[:, :, c]
        c_copy(k, theirs, theirs).wait_recv()
        c_copy(k, own, own).wait_send()
        column = outs[k].at[:, y, c, x]
        y_copy(k, column, column, 0, 0).wait_send()
        x_copy(k, column, column, 0, 0).wait_send()
        part = outs[k].at[pl.ds(0, line // 2), y, c, x]
        y_copy(k, part, part, 1, 0).wait_send()
        x_copy(k, part, part, 1, 0).wait_send()
        for zz in range(line):

            @pl.when((z < line - 1) & (zz <= z))
            def _():
                z_copy(k, at(k, zz), zz, True).wait_send()

            @pl.when((z > 0) & (zz >= z))
            def _():
                z_copy(k, at(k, zz), zz, False).wait_send()


def gather_weights(mesh_shape, shards, bias_block, layer):
    dp_size, pair_size = mesh_shape
    line = dp_size // 4
    members = []
    outs = []
    operands = list(shards)
    if bias_block is not None:
        members.append((len(shards), None))
        outs.append(bias_block)
        operands.append(bias_block)
    for number, shard in enumerate(shards):
        members.append((number, layer))
        outs.append(shard[layer])
    count = len(members)
    shapes = [
        jax.ShapeDtypeStruct((line, 2, 2, pair_size) + out.shape, out.dtype) for out in outs
    ]
    dma = pltpu.SemaphoreType.DMA
    full = pl.pallas_call(
        functools.partial(gather_kernel, members),
        out_shape=shapes,
        in_specs=[pl.BlockSpec(memory_space=pl.ANY)] * len(operands),
        out_specs=[pl.BlockSpec(memory_space=pl.ANY)] * count,
        scratch_shapes=[
            dma((count,)),
            dma((count, 2, line)),
            dma((count, 2)),
            dma((count, 2)),
            dma((count,)),
            dma((count, line)),
            dma((count, 2, line)),
            dma((count, 2, line)),
            dma((count,)),
        ],
        compiler_params=pltpu.CompilerParams(collective_id=layer, has_side_effects=True),
        cost_estimate=pl.CostEstimate(flops=0, bytes_accessed=200_000_000, transcendentals=0),
        name="gather_weights_%d" % layer,
    )(*operands)
    weights = [weight.reshape(-1, weight.shape[-1]) for weight in full[-len(shards) :]]
    biases = None if bias_block is None else full[0].reshape(dp_size * pair_size, -1)
    return weights, biases


def reduce_kernel(*refs):
    count, each = 10, 5
    operands = [refs[8 * slot : 8 * slot + 8] for slot in range(2)]
    given = refs[16:18]
    outs = refs[18 : 18 + each]
    full = refs[18 + each : 22 + each]
    at = 22 + each
    from_c, from_b, from_a, from_low, from_high = [
        refs[at + count * j : at + count * (j + 1)] for j in range(5)
    ]
    at += 5 * count
    wide, narrow, load = refs[at : at + 3]
    c_send, c_recv, b_send, b_recv, a_send, a_recv, up_send, up_recv, down_send, down_recv = refs[
        at + 3 :
    ]
    full = list(full) + [given[0]] + list(full) + [given[1]]
    place = Place()
    line, z, y, c, x = place.line, place.z, place.y, place.c, place.x
    half = line // 2
    place.greet()

    def axes(zz):
        return ("x", "y") if zz % 2 == 0 else ("y", "x")

    def add(total_ref, total_at, more_ref, more_at):
        total_ref[total_at] = (
            total_ref[total_at].astype(jnp.float32) + more_ref[more_at].astype(jnp.float32)
        ).astype(total_ref.dtype)

    def c_copy(k, zz):
        return remote(
            full[k].at[zz, :, 1 - c],
            from_c[k].at[zz],
            c_send.at[k, zz],
            c_recv.at[k, zz],
            place.partner("c"),
        )

    def b_copy(k, zz):
        first = axes(zz)[0]
        src = from_c[k].at[zz, :, 1 - x] if first == "x" else from_c[k].at[zz, 1 - y]
        return remote(
            src, from_b[k].at[zz], b_send.at[k, zz], b_recv.at[k, zz], place.partner(first)
        )

    def a_copy(k, zz):
        second = axes(zz)[1]
        other = 1 - getattr(place, second)
        return remote(
            from_b[k].at[zz, other],
            from_a[k].at[zz],
            a_send.at[k, zz],
            a_recv.at[k, zz],
            place.partner(second),
        )

    def up_copy(k, t, src):
        return remote(
            src, from_low[k].at[t], up_send.at[k, t], up_recv.at[k, t], place.device(z=z + 1)
        )

    def down_copy(k, t, src):
        return remote(
            src, from_high[k].at[t], down_send.at[k, t], down_recv.at[k, t], place.device(z=z - 1)
        )

    def zs_of(h):
        return range(h * half, (h + 1) * half)

    sequence = [k for k in ORDERS[0] + ORDERS[1] if k % each < 4]

    def sides(k):
        number = sequence.index(k) % 2
        left, right = operands[k // each][2 * (k % each) : 2 * (k % each) + 2]
        if left.shape[1] > right.shape[1]:
            left_at, right_at = wide, narrow
        else:
            left_at, right_at = narrow, wide
        left_at = left_at.at[number, :, pl.ds(0, left.shape[1])]
        right_at = right_at.at[number, :, pl.ds(0, right.shape[1])]
        return (left, left_at, load.at[number, 0]), (right, right_at, load.at[number, 1])

    for k in sequence[:2]:
        for side in sides(k):
            pltpu.make_async_copy(*side).start()

    def compute(k, h):
        if k % each < 4:
            (_, left, _), (_, right, _) = sides(k)
            if h == 0:
                for side in sides(k):
                    pltpu.make_async_copy(*side).wait()
            if k >= each:
                for zz in zs_of(h):
                    c_copy(k - each, zz).wait_send()
            rows = full[k].shape[4]
            height = full[k].shape[0] * 8 * rows // 2
            blocks = CHUNK // rows
            for chunk in range(height // CHUNK):
                base = h * half * 8 + chunk * blocks
                first = h * height + chunk * CHUNK

                def tile(j, carry, base=base, first=first):
                    columns = pl.ds(pl.multiple_of(j * 768, 768), 768)
                    product = lax.dot_general(
                        left[:, first : first + CHUNK],
                        right[:, columns],
                        (((0,), (0,)), ((), ())),
                        preferred_element_type=jnp.float32,
                    )
                    for block in range(blocks):
                        n = base + block
                        full[k][n // 8, (n // 4) % 2, (n // 2) % 2, n % 2, :, columns] = product[
                            block * rows : (block + 1) * rows
                        ].astype(jnp.bfloat16)
                    return carry

                lax.fori_loop(0, right.shape[1] // 768, tile, 0)
            number = sequence.index(k) + 2
            if h == 1 and number < len(sequence):
                for side in sides(sequence[number]):
                    pltpu.make_async_copy(*side).start()
        for zz in zs_of(h):
            c_copy(k, zz).start()

    def after_c(k, h):
        def sweep(zz, other):
            for side in range(2):
                yy, xx = (side, other) if axes(zz)[0] == "x" else (other, side)
                add(from_c[k], (zz, yy, xx), full[k], (zz, yy, c, xx))

        for zz in zs_of(h):
            mine = getattr(place, axes(zz)[0])
            c_copy(k, zz).wait_recv()
            sweep(zz, 1 - mine)
            b_copy(k, zz).start()
        for zz in zs_of(h):
            sweep(zz, getattr(place, axes(zz)[0]))

    def after_b(k, h):
        def sweep(zz, side):
            yy, xx = (side, x) if axes(zz)[0] == "x" else (y, side)
            add(from_b[k], (zz, side), from_c[k], (zz, yy, xx))

        for zz in zs_of(h):
            mine = getattr(place, axes(zz)[1])
            b_copy(k, zz).wait_recv()
            sweep(zz, 1 - mine)
            a_copy(k, zz).start()
        for zz in zs_of(h):
            sweep(zz, getattr(place, axes(zz)[1]))

    def after_a(k, h):
        for zz in zs_of(h):
            a_copy(k, zz).wait_recv()
            add(from_a[k], (zz,), from_b[k], (zz, getattr(place, axes(zz)[1])))

    def hop(k, h, step):
        for t in reversed(range(h * half, (h + 1) * half)):

            @pl.when((z == step) & (z < t))
            def _():
                if step == 0:
                    up_copy(k, t, from_a[k].at[t]).start()
                else:
                    up_copy(k, t, from_low[k].at[t]).wait_recv()
                    add(from_low[k], (t,), from_a[k], (t,))
                    up_copy(k, t, from_low[k].at[t]).start()

        for t in range(h * half, (h + 1) * half):

            @pl.when((z == line - 1 - step) & (z > t))
            def _():
                if step == 0:
                    down_copy(k, t, from_a[k].at[t]).start()
                else:
                    down_copy(k, t, from_high[k].at[t]).wait_recv()
                    add(from_high[k], (t,), from_a[k], (t,))
                    down_copy(k, t, from_high[k].at[t]).start()

    def finish(k, h):
        for t in range(h * half, (h + 1) * half):

            @pl.when(z == t)
            def _():
                total = from_a[k][t].astype(jnp.float32)
                if t > 0:
                    up_copy(k, t, from_low[k].at[t]).wait_recv()
                    total = total + from_low[k][t].astype(jnp.float32)
                if t < line - 1:
                    down_copy(k, t, from_high[k].at[t]).wait_recv()
                    total = total + from_high[k][t].astype(jnp.float32)
                outs[k % each][1 - k // each] = total

    def settle(k, h):
        for t in zs_of(h):
            if k % each == 4 or k >= each:
                c_copy(k, t).wait_send()
            b_copy(k, t).wait_send()
            a_copy(k, t).wait_send()

            @pl.when(z < t)
            def _():
                up_copy(k, t, from_a[k].at[t]).wait_send()

            @pl.when(z > t)
            def _():
                down_copy(k, t, from_a[k].at[t]).wait_send()

    units = [(k, h) for k in ORDERS[0] + ORDERS[1] for h in range(2)]
    stages = [compute, after_c, after_b, after_a]
    stages += [functools.partial(hop, step=step) for step in range(line)]
    stages += [finish]
    offsets = list(OFFSETS) + [OFFSETS[-1] + 1 + step for step in range(line)]
    for wave in range(len(units) + offsets[-1]):
        for number, (k, h) in enumerate(units):
            if wave - number in offsets:
                stages[offsets.index(wave - number)](k, h)
    for k, h in units:
        settle(k, h)


def reduce_grads(mesh_shape, terms):
    dp_size, pair_size = mesh_shape
    shard_count = dp_size * pair_size
    line = dp_size // 4
    lead = (line, 2, 2, pair_size)
    low = jnp.bfloat16
    pairs = terms[0][0]
    tokens = pairs[0][0].shape[0]
    shapes = [(left.shape[1] // shard_count, right.shape[1]) for left, right in pairs]
    scratch = [pltpu.VMEM(lead + shape, low) for shape in shapes]
    shapes.append(BIAS_TILE)
    for space in ((line, 2, 2), (line, 2), (line,), (line,), (line,)):
        scratch += [pltpu.VMEM(space + shape, low) for shape in shapes * 2]
    dma = pltpu.SemaphoreType.DMA
    widest = max(side.shape[1] for pair in pairs for side in pair)
    scratch += [pltpu.VMEM((2, tokens, widest), low)]
    scratch += [pltpu.VMEM((2, tokens, min(pairs[0][0].shape[1], widest)), low), dma((2, 2))]
    scratch += [dma((2 * len(shapes), line))] * 10
    operands = [side for layer in (1, 0) for pair in terms[layer][0] for side in pair]
    operands += [terms[layer][1].reshape(lead + BIAS_TILE) for layer in (1, 0)]
    vmem = pl.BlockSpec(memory_space=pltpu.VMEM)
    return pl.pallas_call(
        reduce_kernel,
        out_shape=[jax.ShapeDtypeStruct((LAYERS,) + shape, jnp.float32) for shape in shapes],
        in_specs=[pl.BlockSpec(memory_space=pl.ANY)] * 16 + [vmem] * 2,
        out_specs=[vmem] * len(shapes),
        scratch_shapes=scratch,
        compiler_params=pltpu.CompilerParams(
            collective_id=LAYERS, has_side_effects=True, vmem_limit_bytes=VMEM_LIMIT
        ),
        cost_estimate=pl.CostEstimate(flops=0, bytes_accessed=400_000_000, transcendentals=0),
        name="reduce_grads",
    )(*operands)


def spread(values):
    count = lax.axis_size(AXES)
    copies = jnp.broadcast_to(values[None], (count,) + values.shape)
    copies = lax.all_to_all(copies, AXES, split_axis=0, concat_axis=0, tiled=True)
    return copies.reshape((-1,) + values.shape[1:])


def plain_gather(shards, bias_block, layer):
    weights = [lax.all_gather(shard[layer], AXES, axis=0, tiled=True) for shard in shards]
    if bias_block is None:
        return weights, None
    return weights, lax.all_gather(bias_block.reshape(1, -1), AXES, axis=0, tiled=True)


def plain_reduce(mesh_shape, terms):
    layers = []
    for pairs, bias_rows in terms:
        grads = []
        for left, right in pairs:
            product = jnp.einsum("tk,tn->kn", left, right, preferred_element_type=jnp.float32)
            grads.append(product.astype(GRAD_DTYPE))
        grads.append(bias_rows)
        layers.append(
            [
                lax.psum_scatter(grad, AXES, scatter_dimension=0, tiled=True).astype(jnp.float32)
                for grad in grads
            ]
        )
    return [jnp.stack(member) for member in zip(*layers)]


TOKENS_NT = (((1,), (1,)), ((), ()))
TOKENS_TN = (((0,), (0,)), ((), ()))
WIDE = 2 * HEAD
STEP = 768


def dot32(left, right, dims=(((1,), (0,)), ((), ()))):
    return lax.dot_general(left, right, dims, preferred_element_type=jnp.float32)


def standardize(values):
    centre = values - jnp.mean(values, axis=-1, keepdims=True)
    inverse = lax.rsqrt(jnp.mean(centre * centre, axis=-1, keepdims=True) + EPSILON)
    return centre * inverse, inverse


def head_masks():
    lane = lax.broadcasted_iota(jnp.int32, (1, WIDE), 1)
    first = (lane < HEAD).astype(jnp.float32)
    return lane < HEAD, (first.astype(jnp.bfloat16), (1.0 - first).astype(jnp.bfloat16))


def softmax_parts(query, keys):
    scores = dot32(query, keys, TOKENS_NT) * HEAD ** (-0.5)
    weights = jnp.exp(scores - jnp.max(scores, axis=-1, keepdims=True))
    return weights * (1.0 / jnp.sum(weights, axis=-1, keepdims=True))


def forward_steps(seq, refs):
    (stream, mod, qkv_w, qkv_b, proj_w, proj_b, expand_w, expand_b, reduce_w, reduce_b) = refs[:10]
    (normed_in, qkv, attended, attn_out, middle, normed_mid, pre_act, activated, mlp_out, out) = refs[
        10:
    ]
    tokens, width = stream.shape
    latents = tokens // seq
    hidden = pre_act.shape[1]
    groups = width // WIDE

    def row(b, number):
        return mod[b * 6 + number : b * 6 + number + 1, :]

    def rows(b):
        return slice(b * seq, (b + 1) * seq)

    def enter(b):
        values, _ = standardize(stream[rows(b), :])
        values = values * (1.0 + row(b, 1)) + row(b, 0)
        normed_in[rows(b), :] = values.astype(jnp.bfloat16)

    def project(j):
        at = slice(j * STEP, (j + 1) * STEP)
        qkv[:, at] = (dot32(normed_in[...], qkv_w[:, at]) + qkv_b[:, at]).astype(jnp.bfloat16)

    def attend(b, low, high):
        is_first, masks = head_masks()

        def one(p, carry):
            here = rows(b)
            query = qkv[here, pl.ds(pl.multiple_of(p * WIDE, WIDE), WIDE)]
            keys = qkv[here, pl.ds(pl.multiple_of(width + p * WIDE, WIDE), WIDE)]
            values = qkv[here, pl.ds(pl.multiple_of(2 * width + p * WIDE, WIDE), WIDE)]
            parts = [
                dot32(softmax_parts(query * mask, keys).astype(jnp.bfloat16), values)
                for mask in masks
            ]
            attended[here, pl.ds(pl.multiple_of(p * WIDE, WIDE), WIDE)] = jnp.where(
                is_first, parts[0], parts[1]
            ).astype(jnp.bfloat16)
            return carry

        lax.fori_loop(low, high, one, 0)

    def leave(b):
        result = dot32(attended[rows(b), :], proj_w[...]) + proj_b[...]
        attn_out[rows(b), :] = result
        state = stream[rows(b), :] + row(b, 2) * result
        middle[rows(b), :] = state
        values, _ = standardize(state)
        values = values * (1.0 + row(b, 4)) + row(b, 3)
        normed_mid[rows(b), :] = values.astype(jnp.bfloat16)

    def expand(j):
        at = slice(j * STEP, (j + 1) * STEP)
        before = dot32(normed_mid[...], expand_w[:, at]) + expand_b[:, at]
        pre_act[:, at] = before
        activated[:, at] = gelu_tanh(before).astype(jnp.bfloat16)

    def contract(b):
        result = dot32(activated[rows(b), :], reduce_w[...]) + reduce_b[...]
        mlp_out[rows(b), :] = result
        out[rows(b), :] = middle[rows(b), :] + row(b, 5) * result

    steps = [functools.partial(enter, b) for b in range(latents)]
    steps += [functools.partial(project, j) for j in range(3 * width // STEP)]
    third = groups // 3
    for b in range(latents):
        for low in range(0, groups, third):
            steps.append(functools.partial(attend, b, low, low + third))
    steps += [functools.partial(leave, b) for b in range(latents)]
    steps += [functools.partial(expand, j) for j in range(hidden // STEP)]
    steps += [functools.partial(contract, b) for b in range(latents)]
    return steps


def forward_operands(stream, modulation, gathered):
    (qkv_w, query_b, value_b, proj_w, proj_b, expand_w, expand_b, reduce_w, reduce_b) = gathered
    latents, seq, width = stream.shape
    qkv_b = jnp.concatenate([query_b, jnp.zeros_like(query_b), value_b])
    flat = [bias.astype(jnp.float32)[None] for bias in (qkv_b, proj_b, expand_b, reduce_b)]
    operands = [stream.reshape(-1, width), modulation.reshape(latents * 6, width)]
    for weight, bias in zip((qkv_w, proj_w, expand_w, reduce_w), flat):
        operands += [weight, bias]
    return operands


def forward_shapes(tokens, width, hidden):
    low, high = jnp.bfloat16, jnp.float32
    kinds = [(width, low), (3 * width, low), (width, low), (width, high), (width, high)]
    kinds += [(width, low), (hidden, high), (hidden, low), (width, high), (width, high)]
    return [jax.ShapeDtypeStruct((tokens, columns), kind) for columns, kind in kinds]


def forward_layer(stream, modulation, gathered):
    latents, seq, width = stream.shape
    operands = forward_operands(stream, modulation, gathered)

    def kernel(*refs):
        for step in forward_steps(seq, refs):
            step()

    vmem = pl.BlockSpec(memory_space=pltpu.VMEM)
    shapes = forward_shapes(latents * seq, width, operands[6].shape[1])
    saved = pl.pallas_call(
        kernel,
        out_shape=shapes,
        in_specs=[vmem] * len(operands),
        out_specs=[vmem] * len(shapes),
        compiler_params=pltpu.CompilerParams(vmem_limit_bytes=VMEM_LIMIT),
        name="forward_layer",
    )(*operands)
    return saved[-1].reshape(stream.shape), (operands[0], operands[1], *saved[:-1])


def backward_kernel(seq, *refs):
    (upstream, mod, stream, qkv, attn_out, middle, pre_act, mlp_out) = refs[:8]
    (qkv_w, proj_w, expand_w, reduce_w) = refs[8:12]
    (d_mlp, d_pre, d_attn, d_qkv, d_stream, d_mod) = refs[12:18]
    (g_reduce_b, g_expand_b, g_proj_b, g_qkv_b) = refs[18:22]
    (d_normed, d_middle, d_attended) = refs[22:]
    tokens, width = stream.shape
    latents = tokens // seq
    hidden = pre_act.shape[1]
    groups = width // WIDE
    low = jnp.bfloat16

    def row(b, number):
        return mod[b * 6 + number : b * 6 + number + 1, :]

    def put(b, number, value):
        d_mod[b * 6 + number : b * 6 + number + 1, :] = jnp.sum(value, axis=0, keepdims=True)

    def rows(b):
        return slice(b * seq, (b + 1) * seq)

    def total(value):
        return jnp.sum(value.astype(jnp.float32), axis=0, keepdims=True)

    g_reduce_b[...] = jnp.zeros_like(g_reduce_b)
    g_proj_b[...] = jnp.zeros_like(g_proj_b)
    for b in range(latents):
        above = upstream[rows(b), :]
        put(b, 5, above * mlp_out[rows(b), :])
        value = (row(b, 5) * above).astype(low)
        d_mlp[rows(b), :] = value
        g_reduce_b[...] += total(value)

    d_normed[...] = jnp.zeros_like(d_normed)

    def through(j, carry):
        at = pl.ds(pl.multiple_of(j * STEP, STEP), STEP)
        inner = dot32(d_mlp[...], reduce_w[at, :], TOKENS_NT)
        u = pre_act[:, at]
        rate = (2.0 / jnp.pi) ** 0.5
        bend = jnp.tanh(rate * (u + 0.044715 * (u * u * u)))
        slope = 0.5 * (1.0 + bend) + 0.5 * u * (1.0 - bend * bend) * rate * (
            1.0 + 3.0 * 0.044715 * (u * u)
        )
        value = (inner * slope).astype(low)
        d_pre[:, at] = value
        g_expand_b[:, at] = total(value)
        d_normed[...] += dot32(value, expand_w[:, at], TOKENS_NT)
        return carry

    lax.fori_loop(0, hidden // STEP, through, 0)

    def norm_back(b, source, scale_row, shift_row):
        unit, inverse = standardize(source[rows(b), :])
        flow = d_normed[rows(b), :]
        put(b, shift_row, flow)
        put(b, scale_row, flow * unit)
        flow = flow * (1.0 + row(b, scale_row))
        mean = jnp.mean(flow, axis=-1, keepdims=True)
        along = jnp.mean(flow * unit, axis=-1, keepdims=True)
        return inverse * (flow - mean - unit * along)

    for b in range(latents):
        value = norm_back(b, middle, 4, 3) + upstream[rows(b), :]
        d_middle[rows(b), :] = value
        put(b, 2, value * attn_out[rows(b), :])
        value = (row(b, 2) * value).astype(low)
        d_attn[rows(b), :] = value
        g_proj_b[...] += total(value)
    d_attended[...] = dot32(d_attn[...], proj_w[...], TOKENS_NT).astype(low)

    is_first, masks = head_masks()
    root = HEAD ** (-0.5)
    for b in range(latents):

        def one(p, carry, b=b):
            here = rows(b)
            at_q = pl.ds(pl.multiple_of(p * WIDE, WIDE), WIDE)
            at_k = pl.ds(pl.multiple_of(width + p * WIDE, WIDE), WIDE)
            at_v = pl.ds(pl.multiple_of(2 * width + p * WIDE, WIDE), WIDE)
            query, keys, values = qkv[here, at_q], qkv[here, at_k], qkv[here, at_v]
            flow = d_attended[here, at_q]
            parts = []
            for mask in masks:
                probs = softmax_parts(query * mask, keys)
                d_probs = dot32(flow * mask, values, TOKENS_NT)
                mixed = probs * d_probs
                d_scores = (mixed - probs * jnp.sum(mixed, axis=-1, keepdims=True)).astype(low)
                parts.append(
                    (
                        dot32(d_scores, keys) * root,
                        dot32(d_scores, query, TOKENS_TN) * root,
                        dot32(probs.astype(low), flow, TOKENS_TN),
                    )
                )
            for at, first, second in zip((at_q, at_k, at_v), *parts):
                d_qkv[here, at] = jnp.where(is_first, first, second).astype(low)
            return carry

        lax.fori_loop(0, groups, one, 0)

    for j in range(3):
        at = slice(j * width, (j + 1) * width)
        g_qkv_b[:, at] = total(d_qkv[:, at])
    d_normed[...] = dot32(d_qkv[...], qkv_w[...], TOKENS_NT)
    for b in range(latents):
        d_stream[rows(b), :] = d_middle[rows(b), :] + norm_back(b, stream, 1, 0)


def backward_layer(upstream, gathered, stored):
    (qkv_w, query_b, value_b, proj_w, proj_b, expand_w, expand_b, reduce_w, reduce_b) = gathered
    (stream, mod, normed_in, qkv, attended, attn_out, middle, normed_mid, pre_act) = stored[:9]
    activated, mlp_out = stored[9:]
    latents, seq, width = upstream.shape
    tokens, hidden = pre_act.shape
    low, high = jnp.bfloat16, jnp.float32
    shapes = [(tokens, width, low), (tokens, hidden, low), (tokens, width, low)]
    shapes += [(tokens, 3 * width, low), (tokens, width, high), (latents * 6, width, high)]
    shapes += [(1, width, high), (1, hidden, high), (1, width, high), (1, 3 * width, high)]
    operands = [upstream.reshape(tokens, width), mod, stream, qkv, attn_out, middle, pre_act]
    operands += [mlp_out, qkv_w, proj_w, expand_w, reduce_w]
    vmem = pl.BlockSpec(memory_space=pltpu.VMEM)
    found = pl.pallas_call(
        functools.partial(backward_kernel, seq),
        out_shape=[jax.ShapeDtypeStruct((m, n), kind) for m, n, kind in shapes],
        in_specs=[vmem] * len(operands),
        out_specs=[vmem] * len(shapes),
        scratch_shapes=[
            pltpu.VMEM((tokens, width), high),
            pltpu.VMEM((tokens, width), high),
            pltpu.VMEM((tokens, width), low),
        ],
        compiler_params=pltpu.CompilerParams(vmem_limit_bytes=VMEM_LIMIT),
        name="backward_layer",
    )(*operands)
    (d_mlp, d_pre, d_attn, d_qkv, d_stream, d_mod, g_reduce_b, g_expand_b, g_proj_b, g_qkv_b) = found
    pairs = [(normed_in, d_qkv), (attended, d_attn), (normed_mid, d_pre), (activated, d_mlp)]
    bias_grads = (g_qkv_b[:, :width], g_qkv_b[:, 2 * width :], g_proj_b, g_expand_b, g_reduce_b)
    d_modulation = d_mod.reshape(latents, 6 * width).astype(low)
    return d_stream.reshape(upstream.shape), d_modulation, pairs, bias_grads


def on_device(
    latents,
    conditioning,
    cotangent,
    adaln_weight,
    adaln_bias,
    qkv_weight,
    query_bias,
    value_bias,
    proj_weight,
    proj_bias,
    expand_weight,
    expand_bias,
    reduce_weight,
    reduce_bias,
):
    shard_count = lax.axis_size(AXES)
    mesh_shape = (lax.axis_size("dp"), lax.axis_size("pair"))
    rows = qkv_weight.shape[1]
    in_kernels = rows % 8 == 0 and CHUNK % rows == 0
    here = lax.axis_index(AXES)
    stream = latents.astype(jnp.float32)
    cond_part = conditioning.astype(jnp.float32)
    adaln_size = adaln_bias.shape[1]
    adaln_columns = adaln_weight.reshape(LAYERS * rows, shard_count, adaln_size)
    adaln_columns = adaln_columns.transpose(1, 0, 2)
    own = conditioning.reshape(-1)
    more = -(-own.shape[0] // (8 * adaln_size)) * 8
    own = jnp.pad(own, (0, more * adaln_size - own.shape[0])).reshape(1, more, adaln_size)
    own = jnp.broadcast_to(own, (shard_count, more, adaln_size))
    adaln_columns = jnp.concatenate([adaln_columns, own], axis=1)
    adaln_columns = lax.all_to_all(adaln_columns, AXES, split_axis=0, concat_axis=0, tiled=True)
    conditioning_all = adaln_columns[:, LAYERS * rows :].reshape(shard_count, -1)
    conditioning_all = conditioning_all[:, : conditioning.size].reshape(-1, conditioning.shape[1])
    silu_low = jax.nn.silu(conditioning_all.astype(jnp.float32)).astype(jnp.bfloat16)
    silu_mine = lax.dynamic_slice_in_dim(silu_low, here * rows, rows, axis=1)
    modulation = []
    for layer in range(LAYERS):
        columns = adaln_columns[:, layer * rows : (layer + 1) * rows].reshape(-1, adaln_size)
        modulation.append(
            jnp.dot(silu_low, columns, preferred_element_type=jnp.float32)
            + adaln_bias[layer].astype(jnp.float32)
        )
    modulation = jnp.stack(modulation)
    shards = (qkv_weight, proj_weight, expand_weight, reduce_weight)
    bias_members = (query_bias, value_bias, proj_bias, expand_bias, reduce_bias)
    bias_sizes = [member.shape[1] for member in bias_members]
    room = BIAS_TILE[0] * BIAS_TILE[1]
    bias_row = jnp.concatenate(bias_members, axis=1).reshape(-1)
    bias_row = jnp.pad(bias_row, (0, room - bias_row.shape[0])).reshape(BIAS_TILE)
    weights = []
    for layer in range(LAYERS):
        block = bias_row if layer == 0 else None
        if layer == 1:
            shards, modulation = lax.optimization_barrier((shards, modulation))
            modulation = lax.all_to_all(modulation, AXES, split_axis=1, concat_axis=2, tiled=True)
        if in_kernels:
            found = gather_weights(mesh_shape, shards, block, layer)
        else:
            found = plain_gather(shards, block, layer)
        weights.append(found[0])
        if layer == 0:
            bias_rows = found[1]
    gathered = []
    at = 0
    for layer in range(LAYERS):
        biases = []
        for size in bias_sizes:
            biases.append(bias_rows[:, at : at + size].reshape(-1))
            at += size
        query_b, value_b, proj_b, expand_b, reduce_b = biases
        qkv_w, proj_w, expand_w, reduce_w = weights[layer]
        gathered.append(
            (qkv_w, query_b, value_b, proj_w, proj_b, expand_w, expand_b, reduce_w, reduce_b)
        )
    stored = [None] * LAYERS
    for layer in range(LAYERS):
        stream, stored[layer] = forward_layer(stream, modulation[layer], gathered[layer])
    outputs = stream.astype(jnp.bfloat16)
    upstream = cotangent.astype(jnp.float32)
    d_mods = [None] * LAYERS
    terms = [None] * LAYERS
    for layer in reversed(range(LAYERS)):
        upstream, d_mods[layer], pairs, bias_grads = backward_layer(
            upstream, gathered[layer], stored[layer]
        )
        flat = jnp.concatenate([grad.reshape(shard_count, -1) for grad in bias_grads], axis=1)
        flat = jnp.pad(flat, ((0, 0), (0, room - flat.shape[1]))).astype(GRAD_DTYPE)
        terms[layer] = (pairs, flat)
    terms, d_modulation = lax.optimization_barrier((terms, jnp.stack(d_mods)))
    d_mods = spread(d_modulation.transpose(1, 0, 2))
    summed = (reduce_grads if in_kernels else plain_reduce)(mesh_shape, terms)
    g_adaln_w = []
    g_adaln_b = []
    d_silu = 0.0
    for layer in range(LAYERS):
        part = d_mods[:, layer]
        g_adaln_w.append(
            jnp.einsum("bd,bf->df", silu_mine, part, preferred_element_type=jnp.float32)
        )
        mine = lax.dynamic_slice_in_dim(part, here * adaln_size, adaln_size, axis=1)
        g_adaln_b.append(jnp.sum(mine, axis=0, dtype=jnp.float32))
        d_silu = d_silu + jnp.einsum(
            "bf,df->bd", part, adaln_weight[layer], preferred_element_type=jnp.float32
        )
    d_silu = lax.all_to_all(d_silu, AXES, split_axis=0, concat_axis=1, tiled=True)
    _, pull_silu = jax.vjp(jax.nn.silu, cond_part)
    grad_conditioning = pull_silu(d_silu)[0]
    flat = summed[4].reshape(LAYERS, -1)
    small = []
    at = 0
    for size in bias_sizes:
        small.append(flat[:, at : at + size])
        at += size
    return (
        outputs,
        upstream,
        grad_conditioning,
        jnp.stack(g_adaln_w),
        jnp.stack(g_adaln_b),
        summed[0],
        small[0],
        small[1],
        summed[1],
        small[2],
        summed[2],
        small[3],
        summed[3],
        small[4],
    )


def solution(mesh):
    in_specs = (
        P(("dp", "pair"), None, None),
        P(("dp", "pair"), None),
        P(("dp", "pair"), None, None),
        P(None, ("dp", "pair"), None),
        P(None, ("dp", "pair")),
        P(None, ("dp", "pair"), None),
        P(None, ("dp", "pair")),
        P(None, ("dp", "pair")),
        P(None, ("dp", "pair"), None),
        P(None, ("dp", "pair")),
        P(None, ("dp", "pair"), None),
        P(None, ("dp", "pair")),
        P(None, ("dp", "pair"), None),
        P(None, ("dp", "pair")),
    )
    out_specs = (
        P(("dp", "pair"), None, None),
        P(("dp", "pair"), None, None),
        P(("dp", "pair"), None),
        P(None, ("dp", "pair"), None),
        P(None, ("dp", "pair")),
        P(None, ("dp", "pair"), None),
        P(None, ("dp", "pair")),
        P(None, ("dp", "pair")),
        P(None, ("dp", "pair"), None),
        P(None, ("dp", "pair")),
        P(None, ("dp", "pair"), None),
        P(None, ("dp", "pair")),
        P(None, ("dp", "pair"), None),
        P(None, ("dp", "pair")),
    )
    return jax.shard_map(
        on_device, mesh=mesh, in_specs=in_specs, out_specs=out_specs, check_vma=False
    )
```

```python
import functools

import jax
import jax.numpy as jnp
from jax import lax
from jax.experimental import pallas as pl
from jax.experimental.pallas import tpu as pltpu
from jax.sharding import PartitionSpec as P

HEADS = 12
HEAD = 64
LAYERS = 2


EPSILON = 1e-06


def gelu_tanh(values):
    return jax.nn.gelu(values, approximate=True)


AXES = ("dp", "pair")
LANES = 128
GRAD_DTYPE = jnp.bfloat16


MESH_ID = pl.DeviceIdType.MESH
BIAS_TILE = (16, 128)
CHUNK = 384
SIDE_LAG = 1
CORNER_LAG = 2
OFFSETS = (0, 1, 2, 3, 4)
ORDERS = ((1, 3, 2, 0, 4), (8, 7, 5, 6, 9))
VMEM_LIMIT = 60 * 1024 * 1024


class Place:
    def __init__(self):
        self.line = lax.axis_size("dp") // 4
        spot = lax.axis_index("dp")
        self.z, self.y, self.c = spot // 4, (spot // 2) % 2, spot % 2
        self.x = lax.axis_index("pair")

    def device(self, z=None, y=None, c=None, x=None):
        z = self.z if z is None else z
        y = self.y if y is None else y
        c = self.c if c is None else c
        x = self.x if x is None else x
        return ((z * 2 + y) * 2 + c, x)

    def partner(self, axis):
        return self.device(**{axis: 1 - getattr(self, axis)})

    def greet(self):
        barrier = pltpu.get_barrier_semaphore()
        for axis in ("y", "c", "x"):
            pl.semaphore_signal(
                barrier, inc=1, device_id=self.partner(axis), device_id_type=MESH_ID
            )

        @pl.when(self.z > 0)
        def _():
            pl.semaphore_signal(
                barrier, inc=1, device_id=self.device(z=self.z - 1), device_id_type=MESH_ID
            )

        @pl.when(self.z < self.line - 1)
        def _():
            pl.semaphore_signal(
                barrier, inc=1, device_id=self.device(z=self.z + 1), device_id_type=MESH_ID
            )

        ends = (self.z > 0).astype(jnp.int32) + (self.z < self.line - 1).astype(jnp.int32)
        pl.semaphore_wait(barrier, 3 + ends)


def remote(src, dst, send, recv, device):
    return pltpu.make_async_remote_copy(
        src_ref=src,
        dst_ref=dst,
        send_sem=send,
        recv_sem=recv,
        device_id=device,
        device_id_type=MESH_ID,
    )


def gather_kernel(members, *refs):
    count = len(members)
    input_count = len(refs) - 9 - count
    ins, outs = refs[:input_count], refs[input_count : input_count + count]
    (local, zs, as_, bs, cs, zr, ar, br, cr) = refs[input_count + count :]
    place = Place()
    line, z, y, c, x = place.line, place.z, place.y, place.c, place.x
    place.greet()

    def source(k):
        number, layer = members[k]
        return ins[number] if layer is None else ins[number].at[layer]

    def at(k, zz, flip_y=False, flip_x=False):
        return outs[k].at[zz, 1 - y if flip_y else y, c, 1 - x if flip_x else x]

    def z_copy(k, src, zz, up):
        to = place.device(z=z + 1 if up else z - 1)
        return remote(src, at(k, zz), zs.at[k, 0 if up else 1, zz], zr.at[k, zz], to)

    def y_copy(k, src, dst, step, zz):
        return remote(src, dst, as_.at[k, step], ar.at[k, step, zz], place.partner("y"))

    def x_copy(k, src, dst, step, zz):
        return remote(src, dst, bs.at[k, step], br.at[k, step, zz], place.partner("x"))

    def c_copy(k, src, dst):
        return remote(src, dst, cs.at[k], cr.at[k], place.partner("c"))

    def spread(k, src, zz):
        dst = at(k, zz)
        y_copy(k, src, dst, 0, zz).start()
        x_copy(k, src, dst, 0, zz).start()
        c_copy(k, src, dst).start()

    def line_step(k, d):
        if d == 0:
            src = source(k)

            @pl.when(z < line - 1)
            def _():
                z_copy(k, src, z, True).start()

            @pl.when(z > 0)
            def _():
                z_copy(k, src, z, False).start()

            spread(k, src, z)
            pltpu.make_async_copy(src, at(k, z), local.at[k]).start()
            return

        @pl.when(z >= d)
        def _():
            zz = z - d
            z_copy(k, at(k, zz), zz, True).wait_recv()

            @pl.when(z < line - 1)
            def _():
                z_copy(k, at(k, zz), zz, True).start()

            spread(k, at(k, zz), zz)

        @pl.when(z + d < line)
        def _():
            zz = z + d
            z_copy(k, at(k, zz), zz, False).wait_recv()

            @pl.when(z > 0)
            def _():
                z_copy(k, at(k, zz), zz, False).start()

            spread(k, at(k, zz), zz)

    def at_distance(d, use):
        if d == 0:
            use(z)
            return

        @pl.when(z >= d)
        def _():
            use(z - d)

        @pl.when(z + d < line)
        def _():
            use(z + d)

    def y_first(zz):
        return zz % 2 == 0

    def side_step(k, d):
        def use(zz):
            over_y, over_x = at(k, zz, flip_y=True), at(k, zz, flip_x=True)
            y_copy(k, over_y, over_y, 0, zz).wait_recv()

            @pl.when(y_first(zz))
            def _():
                x_copy(k, over_y, over_y, 1, zz).start()

            c_copy(k, over_y, over_y).start()
            x_copy(k, over_x, over_x, 0, zz).wait_recv()

            @pl.when(jnp.logical_not(y_first(zz)))
            def _():
                y_copy(k, over_x, over_x, 1, zz).start()

            c_copy(k, over_x, over_x).start()

        at_distance(d, use)

    def corner_step(k, d):
        def use(zz):
            corner = at(k, zz, flip_y=True, flip_x=True)

            @pl.when(y_first(zz))
            def _():
                x_copy(k, corner, corner, 1, zz).wait_recv()

            @pl.when(jnp.logical_not(y_first(zz)))
            def _():
                y_copy(k, corner, corner, 1, zz).wait_recv()

            c_copy(k, corner, corner).start()

        at_distance(d, use)

    for wave in range(count + line + CORNER_LAG):
        for k in range(count):
            step = wave - k
            if 0 <= step < line:
                line_step(k, step)
            if 0 <= step - SIDE_LAG < line:
                side_step(k, step - SIDE_LAG)
            if 0 <= step - CORNER_LAG < line:
                corner_step(k, step - CORNER_LAG)

    for k in range(count):
        pltpu.make_async_copy(source(k), at(k, z), local.at[k]).wait()
        theirs = outs[k].at[:, :, 1 - c]
        own = outs[k].at[:, :, c]
        c_copy(k, theirs, theirs).wait_recv()
        c_copy(k, own, own).wait_send()
        column = outs[k].at[:, y, c, x]
        y_copy(k, column, column, 0, 0).wait_send()
        x_copy(k, column, column, 0, 0).wait_send()
        part = outs[k].at[pl.ds(0, line // 2), y, c, x]
        y_copy(k, part, part, 1, 0).wait_send()
        x_copy(k, part, part, 1, 0).wait_send()
        for zz in range(line):

            @pl.when((z < line - 1) & (zz <= z))
            def _():
                z_copy(k, at(k, zz), zz, True).wait_send()

            @pl.when((z > 0) & (zz >= z))
            def _():
                z_copy(k, at(k, zz), zz, False).wait_send()


def gather_weights(mesh_shape, shards, bias_block, layer):
    dp_size, pair_size = mesh_shape
    line = dp_size // 4
    members = []
    outs = []
    operands = list(shards)
    if bias_block is not None:
        members.append((len(shards), None))
        outs.append(bias_block)
        operands.append(bias_block)
    for number, shard in enumerate(shards):
        members.append((number, layer))
        outs.append(shard[layer])
    count = len(members)
    shapes = [
        jax.ShapeDtypeStruct((line, 2, 2, pair_size) + out.shape, out.dtype) for out in outs
    ]
    dma = pltpu.SemaphoreType.DMA
    full = pl.pallas_call(
        functools.partial(gather_kernel, members),
        out_shape=shapes,
        in_specs=[pl.BlockSpec(memory_space=pl.ANY)] * len(operands),
        out_specs=[pl.BlockSpec(memory_space=pl.ANY)] * count,
        scratch_shapes=[
            dma((count,)),
            dma((count, 2, line)),
            dma((count, 2)),
            dma((count, 2)),
            dma((count,)),
            dma((count, line)),
            dma((count, 2, line)),
            dma((count, 2, line)),
            dma((count,)),
        ],
        compiler_params=pltpu.CompilerParams(collective_id=layer, has_side_effects=True),
        cost_estimate=pl.CostEstimate(flops=0, bytes_accessed=200_000_000, transcendentals=0),
        name="gather_weights_%d" % layer,
    )(*operands)
    weights = [weight.reshape(-1, weight.shape[-1]) for weight in full[-len(shards) :]]
    biases = None if bias_block is None else full[0].reshape(dp_size * pair_size, -1)
    return weights, biases


def reduce_kernel(*refs):
    count, each = 10, 5
    operands = [refs[8 * slot : 8 * slot + 8] for slot in range(2)]
    given = refs[16:18]
    outs = refs[18 : 18 + each]
    full = refs[18 + each : 22 + each]
    at = 22 + each
    from_c, from_b, from_a, from_low, from_high = [
        refs[at + count * j : at + count * (j + 1)] for j in range(5)
    ]
    at += 5 * count
    wide, narrow, load = refs[at : at + 3]
    c_send, c_recv, b_send, b_recv, a_send, a_recv, up_send, up_recv, down_send, down_recv = refs[
        at + 3 :
    ]
    full = list(full) + [given[0]] + list(full) + [given[1]]
    place = Place()
    line, z, y, c, x = place.line, place.z, place.y, place.c, place.x
    half = line // 2
    place.greet()

    def axes(zz):
        return ("x", "y") if zz % 2 == 0 else ("y", "x")

    def add(total_ref, total_at, more_ref, more_at):
        total_ref[total_at] = (
            total_ref[total_at].astype(jnp.float32) + more_ref[more_at].astype(jnp.float32)
        ).astype(total_ref.dtype)

    def c_copy(k, zz):
        return remote(
            full[k].at[zz, :, 1 - c],
            from_c[k].at[zz],
            c_send.at[k, zz],
            c_recv.at[k, zz],
            place.partner("c"),
        )

    def b_copy(k, zz):
        first = axes(zz)[0]
        src = from_c[k].at[zz, :, 1 - x] if first == "x" else from_c[k].at[zz, 1 - y]
        return remote(
            src, from_b[k].at[zz], b_send.at[k, zz], b_recv.at[k, zz], place.partner(first)
        )

    def a_copy(k, zz):
        second = axes(zz)[1]
        other = 1 - getattr(place, second)
        return remote(
            from_b[k].at[zz, other],
            from_a[k].at[zz],
            a_send.at[k, zz],
            a_recv.at[k, zz],
            place.partner(second),
        )

    def up_copy(k, t, src):
        return remote(
            src, from_low[k].at[t], up_send.at[k, t], up_recv.at[k, t], place.device(z=z + 1)
        )

    def down_copy(k, t, src):
        return remote(
            src, from_high[k].at[t], down_send.at[k, t], down_recv.at[k, t], place.device(z=z - 1)
        )

    def zs_of(h):
        return range(h * half, (h + 1) * half)

    sequence = [k for k in ORDERS[0] + ORDERS[1] if k % each < 4]

    def sides(k):
        number = sequence.index(k) % 2
        left, right = operands[k // each][2 * (k % each) : 2 * (k % each) + 2]
        if left.shape[1] > right.shape[1]:
            left_at, right_at = wide, narrow
        else:
            left_at, right_at = narrow, wide
        left_at = left_at.at[number, :, pl.ds(0, left.shape[1])]
        right_at = right_at.at[number, :, pl.ds(0, right.shape[1])]
        return (left, left_at, load.at[number, 0]), (right, right_at, load.at[number, 1])

    for k in sequence[:2]:
        for side in sides(k):
            pltpu.make_async_copy(*side).start()

    def compute(k, h):
        if k % each < 4:
            (_, left, _), (_, right, _) = sides(k)
            if h == 0:
                for side in sides(k):
                    pltpu.make_async_copy(*side).wait()
            if k >= each:
                for zz in zs_of(h):
                    c_copy(k - each, zz).wait_send()
            rows = full[k].shape[4]
            height = full[k].shape[0] * 8 * rows // 2
            blocks = CHUNK // rows
            for chunk in range(height // CHUNK):
                base = h * half * 8 + chunk * blocks
                first = h * height + chunk * CHUNK

                def tile(j, carry, base=base, first=first):
                    columns = pl.ds(pl.multiple_of(j * 768, 768), 768)
                    product = lax.dot_general(
                        left[:, first : first + CHUNK],
                        right[:, columns],
                        (((0,), (0,)), ((), ())),
                        preferred_element_type=jnp.float32,
                    )
                    for block in range(blocks):
                        n = base + block
                        full[k][n // 8, (n // 4) % 2, (n // 2) % 2, n % 2, :, columns] = product[
                            block * rows : (block + 1) * rows
                        ].astype(jnp.bfloat16)
                    return carry

                lax.fori_loop(0, right.shape[1] // 768, tile, 0)
            number = sequence.index(k) + 2
            if h == 1 and number < len(sequence):
                for side in sides(sequence[number]):
                    pltpu.make_async_copy(*side).start()
        for zz in zs_of(h):
            c_copy(k, zz).start()

    def after_c(k, h):
        def sweep(zz, other):
            for side in range(2):
                yy, xx = (side, other) if axes(zz)[0] == "x" else (other, side)
                add(from_c[k], (zz, yy, xx), full[k], (zz, yy, c, xx))

        for zz in zs_of(h):
            mine = getattr(place, axes(zz)[0])
            c_copy(k, zz).wait_recv()
            sweep(zz, 1 - mine)
            b_copy(k, zz).start()
        for zz in zs_of(h):
            sweep(zz, getattr(place, axes(zz)[0]))

    def after_b(k, h):
        def sweep(zz, side):
            yy, xx = (side, x) if axes(zz)[0] == "x" else (y, side)
            add(from_b[k], (zz, side), from_c[k], (zz, yy, xx))

        for zz in zs_of(h):
            mine = getattr(place, axes(zz)[1])
            b_copy(k, zz).wait_recv()
            sweep(zz, 1 - mine)
            a_copy(k, zz).start()
        for zz in zs_of(h):
            sweep(zz, getattr(place, axes(zz)[1]))

    def after_a(k, h):
        for zz in zs_of(h):
            a_copy(k, zz).wait_recv()
            add(from_a[k], (zz,), from_b[k], (zz, getattr(place, axes(zz)[1])))

    def hop(k, h, step):
        for t in reversed(range(h * half, (h + 1) * half)):

            @pl.when((z == step) & (z < t))
            def _():
                if step == 0:
                    up_copy(k, t, from_a[k].at[t]).start()
                else:
                    up_copy(k, t, from_low[k].at[t]).wait_recv()
                    add(from_low[k], (t,), from_a[k], (t,))
                    up_copy(k, t, from_low[k].at[t]).start()

        for t in range(h * half, (h + 1) * half):

            @pl.when((z == line - 1 - step) & (z > t))
            def _():
                if step == 0:
                    down_copy(k, t, from_a[k].at[t]).start()
                else:
                    down_copy(k, t, from_high[k].at[t]).wait_recv()
                    add(from_high[k], (t,), from_a[k], (t,))
                    down_copy(k, t, from_high[k].at[t]).start()

    def finish(k, h):
        for t in range(h * half, (h + 1) * half):

            @pl.when(z == t)
            def _():
                total = from_a[k][t].astype(jnp.float32)
                if t > 0:
                    up_copy(k, t, from_low[k].at[t]).wait_recv()
                    total = total + from_low[k][t].astype(jnp.float32)
                if t < line - 1:
                    down_copy(k, t, from_high[k].at[t]).wait_recv()
                    total = total + from_high[k][t].astype(jnp.float32)
                outs[k % each][1 - k // each] = total

    def settle(k, h):
        for t in zs_of(h):
            if k % each == 4 or k >= each:
                c_copy(k, t).wait_send()
            b_copy(k, t).wait_send()
            a_copy(k, t).wait_send()

            @pl.when(z < t)
            def _():
                up_copy(k, t, from_a[k].at[t]).wait_send()

            @pl.when(z > t)
            def _():
                down_copy(k, t, from_a[k].at[t]).wait_send()

    units = [(k, h) for k in ORDERS[0] + ORDERS[1] for h in range(2)]
    stages = [compute, after_c, after_b, after_a]
    stages += [functools.partial(hop, step=step) for step in range(line)]
    stages += [finish]
    offsets = list(OFFSETS) + [OFFSETS[-1] + 1 + step for step in range(line)]
    for wave in range(len(units) + offsets[-1]):
        for number, (k, h) in enumerate(units):
            if wave - number in offsets:
                stages[offsets.index(wave - number)](k, h)
    for k, h in units:
        settle(k, h)


def reduce_grads(mesh_shape, terms):
    dp_size, pair_size = mesh_shape
    shard_count = dp_size * pair_size
    line = dp_size // 4
    lead = (line, 2, 2, pair_size)
    low = jnp.bfloat16
    pairs = terms[0][0]
    tokens = pairs[0][0].shape[0]
    shapes = [(left.shape[1] // shard_count, right.shape[1]) for left, right in pairs]
    scratch = [pltpu.VMEM(lead + shape, low) for shape in shapes]
    shapes.append(BIAS_TILE)
    for space in ((line, 2, 2), (line, 2), (line,), (line,), (line,)):
        scratch += [pltpu.VMEM(space + shape, low) for shape in shapes * 2]
    dma = pltpu.SemaphoreType.DMA
    widest = max(side.shape[1] for pair in pairs for side in pair)
    scratch += [pltpu.VMEM((2, tokens, widest), low)]
    scratch += [pltpu.VMEM((2, tokens, min(pairs[0][0].shape[1], widest)), low), dma((2, 2))]
    scratch += [dma((2 * len(shapes), line))] * 10
    operands = [side for layer in (1, 0) for pair in terms[layer][0] for side in pair]
    operands += [terms[layer][1].reshape(lead + BIAS_TILE) for layer in (1, 0)]
    vmem = pl.BlockSpec(memory_space=pltpu.VMEM)
    return pl.pallas_call(
        reduce_kernel,
        out_shape=[jax.ShapeDtypeStruct((LAYERS,) + shape, jnp.float32) for shape in shapes],
        in_specs=[pl.BlockSpec(memory_space=pl.ANY)] * 16 + [vmem] * 2,
        out_specs=[vmem] * len(shapes),
        scratch_shapes=scratch,
        compiler_params=pltpu.CompilerParams(
            collective_id=LAYERS, has_side_effects=True, vmem_limit_bytes=VMEM_LIMIT
        ),
        cost_estimate=pl.CostEstimate(flops=0, bytes_accessed=400_000_000, transcendentals=0),
        name="reduce_grads",
    )(*operands)


def spread(values):
    count = lax.axis_size(AXES)
    copies = jnp.broadcast_to(values[None], (count,) + values.shape)
    copies = lax.all_to_all(copies, AXES, split_axis=0, concat_axis=0, tiled=True)
    return copies.reshape((-1,) + values.shape[1:])


def plain_gather(shards, bias_block, layer):
    weights = [lax.all_gather(shard[layer], AXES, axis=0, tiled=True) for shard in shards]
    if bias_block is None:
        return weights, None
    return weights, lax.all_gather(bias_block.reshape(1, -1), AXES, axis=0, tiled=True)


def plain_reduce(mesh_shape, terms):
    layers = []
    for pairs, bias_rows in terms:
        grads = []
        for left, right in pairs:
            product = jnp.einsum("tk,tn->kn", left, right, preferred_element_type=jnp.float32)
            grads.append(product.astype(GRAD_DTYPE))
        grads.append(bias_rows)
        layers.append(
            [
                lax.psum_scatter(grad, AXES, scatter_dimension=0, tiled=True).astype(jnp.float32)
                for grad in grads
            ]
        )
    return [jnp.stack(member) for member in zip(*layers)]


TOKENS_NT = (((1,), (1,)), ((), ()))
TOKENS_TN = (((0,), (0,)), ((), ()))
WIDE = 2 * HEAD
STEP = 768
UNROLL = 2
UNROLL_BACK = 2


def dot32(left, right, dims=(((1,), (0,)), ((), ()))):
    return lax.dot_general(left, right, dims, preferred_element_type=jnp.float32)


def standardize(values):
    centre = values - jnp.mean(values, axis=-1, keepdims=True)
    inverse = lax.rsqrt(jnp.mean(centre * centre, axis=-1, keepdims=True) + EPSILON)
    return centre * inverse, inverse


def head_masks():
    lane = lax.broadcasted_iota(jnp.int32, (1, WIDE), 1)
    first = (lane < HEAD).astype(jnp.float32)
    return lane < HEAD, (first.astype(jnp.bfloat16), (1.0 - first).astype(jnp.bfloat16))


def scaled(query):
    return query * jnp.bfloat16(HEAD ** (-0.5))


def softmax_parts(query, keys):
    scores = dot32(query, keys, TOKENS_NT)
    weights = jnp.exp(scores - jnp.max(scores, axis=-1, keepdims=True))
    return weights * (1.0 / jnp.sum(weights, axis=-1, keepdims=True))


def forward_steps(seq, refs):
    (stream, mod, qkv_w, qkv_b, proj_w, proj_b, expand_w, expand_b, reduce_w, reduce_b) = refs[:10]
    (normed_in, qkv, attended, attn_out, middle, normed_mid, pre_act, activated, mlp_out, out) = refs[
        10:
    ]
    tokens, width = stream.shape
    latents = tokens // seq
    hidden = pre_act.shape[1]
    groups = width // WIDE

    def row(b, number):
        return mod[b * 6 + number : b * 6 + number + 1, :]

    def rows(b):
        return slice(b * seq, (b + 1) * seq)

    def enter(b):
        values, _ = standardize(stream[rows(b), :])
        values = values * (1.0 + row(b, 1)) + row(b, 0)
        normed_in[rows(b), :] = values.astype(jnp.bfloat16)

    def project(j):
        at = slice(j * STEP, (j + 1) * STEP)
        qkv[:, at] = (dot32(normed_in[...], qkv_w[:, at]) + qkv_b[:, at]).astype(jnp.bfloat16)

    def attend(b, low, high):
        is_first, masks = head_masks()

        def one(p, carry):
            here = rows(b)
            query = qkv[here, pl.ds(pl.multiple_of(p * WIDE, WIDE), WIDE)]
            keys = qkv[here, pl.ds(pl.multiple_of(width + p * WIDE, WIDE), WIDE)]
            values = qkv[here, pl.ds(pl.multiple_of(2 * width + p * WIDE, WIDE), WIDE)]
            query = scaled(query)
            parts = [
                dot32(softmax_parts(query * mask, keys).astype(jnp.bfloat16), values)
                for mask in masks
            ]
            attended[here, pl.ds(pl.multiple_of(p * WIDE, WIDE), WIDE)] = jnp.where(
                is_first, parts[0], parts[1]
            ).astype(jnp.bfloat16)
            return carry

        lax.fori_loop(low, high, one, 0, unroll=UNROLL)

    def leave(b):
        result = dot32(attended[rows(b), :], proj_w[...]) + proj_b[...]
        attn_out[rows(b), :] = result
        state = stream[rows(b), :] + row(b, 2) * result
        middle[rows(b), :] = state
        values, _ = standardize(state)
        values = values * (1.0 + row(b, 4)) + row(b, 3)
        normed_mid[rows(b), :] = values.astype(jnp.bfloat16)

    def expand(j):
        at = slice(j * STEP, (j + 1) * STEP)
        before = dot32(normed_mid[...], expand_w[:, at]) + expand_b[:, at]
        pre_act[:, at] = before
        activated[:, at] = gelu_tanh(before).astype(jnp.bfloat16)

    def contract(b):
        result = dot32(activated[rows(b), :], reduce_w[...]) + reduce_b[...]
        mlp_out[rows(b), :] = result
        out[rows(b), :] = middle[rows(b), :] + row(b, 5) * result

    steps = [functools.partial(enter, b) for b in range(latents)]
    steps += [functools.partial(project, j) for j in range(3 * width // STEP)]
    third = groups // 3
    for b in range(latents):
        for low in range(0, groups, third):
            steps.append(functools.partial(attend, b, low, low + third))
    steps += [functools.partial(leave, b) for b in range(latents)]
    steps += [functools.partial(expand, j) for j in range(hidden // STEP)]
    steps += [functools.partial(contract, b) for b in range(latents)]
    return steps


def forward_operands(stream, modulation, gathered):
    (qkv_w, query_b, value_b, proj_w, proj_b, expand_w, expand_b, reduce_w, reduce_b) = gathered
    latents, seq, width = stream.shape
    qkv_b = jnp.concatenate([query_b, jnp.zeros_like(query_b), value_b])
    flat = [bias.astype(jnp.float32)[None] for bias in (qkv_b, proj_b, expand_b, reduce_b)]
    operands = [stream.reshape(-1, width), modulation.reshape(latents * 6, width)]
    for weight, bias in zip((qkv_w, proj_w, expand_w, reduce_w), flat):
        operands += [weight, bias]
    return operands


def forward_shapes(tokens, width, hidden):
    low, high = jnp.bfloat16, jnp.float32
    kinds = [(width, low), (3 * width, low), (width, low), (width, high), (width, high)]
    kinds += [(width, low), (hidden, high), (hidden, low), (width, high), (width, high)]
    return [jax.ShapeDtypeStruct((tokens, columns), kind) for columns, kind in kinds]


def forward_layer(stream, modulation, gathered):
    latents, seq, width = stream.shape
    operands = forward_operands(stream, modulation, gathered)

    shapes = forward_shapes(latents * seq, width, operands[6].shape[1])
    large = (0, 2, 4, 6, 8)
    hidden_tiles = operands[6].shape[1] // STEP
    needs = {"enter": 0, "project": 2, "leave": 4, "expand": 6, "contract": 8}
    gives = {"enter": (0,), "project": (1,), "attend": (2,), "leave": (3, 4, 5)}
    gives.update({"contract": (8, 9)})

    def kernel(*refs):
        ins, outs = refs[:10], refs[10:20]
        held, made = refs[20:25], refs[25:35]
        in_sem, out_sem, tile_sem = refs[35:]
        local = list(ins)
        for number, which in enumerate(large):
            local[which] = held[number]

        def fetch(which):
            number = large.index(which)
            return pltpu.make_async_copy(ins[which], held[number], in_sem.at[number])

        def store(which):
            return pltpu.make_async_copy(made[which], outs[which], out_sem.at[which])

        def store_tile(which, j):
            at = pl.ds(j * STEP, STEP)
            return pltpu.make_async_copy(
                made[which].at[:, at], outs[which].at[:, at], tile_sem.at[which - 6, j]
            )

        for which in large:
            fetch(which).start()
        steps = forward_steps(seq, (*local, *made))
        names = [step.func.__name__ for step in steps]
        for number, (name, step) in enumerate(zip(names, steps)):
            if name in needs and name not in names[:number]:
                fetch(needs[name]).wait()
            step()
            if name == "expand":
                for which in (6, 7):
                    store_tile(which, step.args[0]).start()
            elif name not in names[number + 1 :]:
                for which in gives[name]:
                    store(which).start()
        for which in range(10):
            if which in (6, 7):
                for j in range(hidden_tiles):
                    store_tile(which, j).wait()
            else:
                store(which).wait()

    vmem = pl.BlockSpec(memory_space=pltpu.VMEM)
    anywhere = pl.BlockSpec(memory_space=pl.ANY)
    dma = pltpu.SemaphoreType.DMA
    saved = pl.pallas_call(
        kernel,
        out_shape=shapes,
        in_specs=[anywhere if number in large else vmem for number in range(len(operands))],
        out_specs=[anywhere] * len(shapes),
        scratch_shapes=[pltpu.VMEM(operands[which].shape, operands[which].dtype) for which in large]
        + [pltpu.VMEM(shape.shape, shape.dtype) for shape in shapes]
        + [dma((len(large),)), dma((len(shapes),)), dma((2, hidden_tiles))],
        compiler_params=pltpu.CompilerParams(vmem_limit_bytes=VMEM_LIMIT),
        name="forward_layer",
    )(*operands)
    return saved[-1].reshape(stream.shape), (operands[0], operands[1], *saved[:-1])


def backward_kernel(seq, *refs):
    given, results = refs[:12], refs[12:17]
    mod = given[1]
    (d_mod, g_reduce_b, g_expand_b, g_proj_b, g_qkv_b) = refs[17:22]
    held, made = refs[22:33], refs[33:38]
    (upstream, stream, qkv, attn_out, middle, pre_act, mlp_out) = held[:7]
    (qkv_w, proj_w, expand_w, reduce_w) = held[7:]
    (d_mlp, d_pre, d_attn, d_qkv, d_stream) = made
    (d_normed, d_middle, d_attended, in_sem, tile_sem, out_sem) = refs[38:]
    tokens, width = stream.shape
    latents = tokens // seq
    hidden = pre_act.shape[1]
    groups = width // WIDE
    low = jnp.bfloat16

    def row(b, number):
        return mod[b * 6 + number : b * 6 + number + 1, :]

    def put(b, number, value):
        d_mod[b * 6 + number : b * 6 + number + 1, :] = jnp.sum(value, axis=0, keepdims=True)

    def rows(b):
        return slice(b * seq, (b + 1) * seq)

    def total(value):
        return jnp.sum(value.astype(jnp.float32), axis=0, keepdims=True)

    outside = given[:1] + given[2:]

    def fetch(number):
        return pltpu.make_async_copy(outside[number], held[number], in_sem.at[number])

    def fetch_tiles(j):
        at = pl.ds(pl.multiple_of(j * STEP, STEP), STEP)
        return (
            pltpu.make_async_copy(outside[10].at[at], reduce_w.at[at], tile_sem.at[0, j]),
            pltpu.make_async_copy(outside[5].at[:, at], pre_act.at[:, at], tile_sem.at[1, j]),
            pltpu.make_async_copy(outside[9].at[:, at], expand_w.at[:, at], tile_sem.at[2, j]),
        )

    def store(number):
        return pltpu.make_async_copy(made[number], results[number], out_sem.at[number])

    fetch(0).start()
    fetch(6).start()
    for j in range(hidden // STEP):
        for copy in fetch_tiles(j):
            copy.start()
    for number in (4, 3, 8, 2, 7, 1):
        fetch(number).start()
    fetch(0).wait()
    fetch(6).wait()
    g_reduce_b[...] = jnp.zeros_like(g_reduce_b)
    g_proj_b[...] = jnp.zeros_like(g_proj_b)
    for b in range(latents):
        above = upstream[rows(b), :]
        put(b, 5, above * mlp_out[rows(b), :])
        value = (row(b, 5) * above).astype(low)
        d_mlp[rows(b), :] = value
        g_reduce_b[...] += total(value)

    store(0).start()
    d_normed[...] = jnp.zeros_like(d_normed)

    def through(j, carry):
        for copy in fetch_tiles(j):
            copy.wait()
        at = pl.ds(pl.multiple_of(j * STEP, STEP), STEP)
        inner = dot32(d_mlp[...], reduce_w[at, :], TOKENS_NT)
        u = pre_act[:, at]
        rate = (2.0 / jnp.pi) ** 0.5
        bend = jnp.tanh(rate * (u + 0.044715 * (u * u * u)))
        slope = 0.5 * (1.0 + bend) + 0.5 * u * (1.0 - bend * bend) * rate * (
            1.0 + 3.0 * 0.044715 * (u * u)
        )
        value = (inner * slope).astype(low)
        d_pre[:, at] = value
        g_expand_b[:, at] = total(value)
        d_normed[...] += dot32(value, expand_w[:, at], TOKENS_NT)
        return carry

    lax.fori_loop(0, hidden // STEP, through, 0)
    store(1).start()
    for number in (4, 3, 8):
        fetch(number).wait()

    def norm_back(b, source, scale_row, shift_row):
        unit, inverse = standardize(source[rows(b), :])
        flow = d_normed[rows(b), :]
        put(b, shift_row, flow)
        put(b, scale_row, flow * unit)
        flow = flow * (1.0 + row(b, scale_row))
        mean = jnp.mean(flow, axis=-1, keepdims=True)
        along = jnp.mean(flow * unit, axis=-1, keepdims=True)
        return inverse * (flow - mean - unit * along)

    for b in range(latents):
        value = norm_back(b, middle, 4, 3) + upstream[rows(b), :]
        d_middle[rows(b), :] = value
        put(b, 2, value * attn_out[rows(b), :])
        value = (row(b, 2) * value).astype(low)
        d_attn[rows(b), :] = value
        g_proj_b[...] += total(value)
    store(2).start()
    d_attended[...] = dot32(d_attn[...], proj_w[...], TOKENS_NT).astype(low)
    fetch(2).wait()

    is_first, masks = head_masks()
    root = HEAD ** (-0.5)
    for b in range(latents):

        def one(p, carry, b=b):
            here = rows(b)
            at_q = pl.ds(pl.multiple_of(p * WIDE, WIDE), WIDE)
            at_k = pl.ds(pl.multiple_of(width + p * WIDE, WIDE), WIDE)
            at_v = pl.ds(pl.multiple_of(2 * width + p * WIDE, WIDE), WIDE)
            query, keys, values = qkv[here, at_q], qkv[here, at_k], qkv[here, at_v]
            flow = d_attended[here, at_q]
            parts = []
            for mask in masks:
                scores = dot32(keys, scaled(query) * mask, TOKENS_NT)
                weights = jnp.exp(scores - jnp.max(scores, axis=0, keepdims=True))
                probs = weights * (1.0 / jnp.sum(weights, axis=0, keepdims=True))
                d_probs = dot32(values, flow * mask, TOKENS_NT)
                mixed = probs * d_probs
                d_scores = (mixed - probs * jnp.sum(mixed, axis=0, keepdims=True)).astype(low)
                parts.append(
                    (
                        dot32(d_scores, keys, TOKENS_TN) * root,
                        dot32(d_scores, query) * root,
                        dot32(probs.astype(low), flow),
                    )
                )
            for at, first, second in zip((at_q, at_k, at_v), *parts):
                d_qkv[here, at] = jnp.where(is_first, first, second).astype(low)
            return carry

        lax.fori_loop(0, groups, one, 0, unroll=UNROLL_BACK)

    store(3).start()
    fetch(7).wait()
    fetch(1).wait()
    for j in range(3):
        at = slice(j * width, (j + 1) * width)
        g_qkv_b[:, at] = total(d_qkv[:, at])
    d_normed[...] = dot32(d_qkv[...], qkv_w[...], TOKENS_NT)
    for b in range(latents):
        d_stream[rows(b), :] = d_middle[rows(b), :] + norm_back(b, stream, 1, 0)
    store(4).start()
    for number in range(5):
        store(number).wait()


def backward_layer(upstream, gathered, stored):
    (qkv_w, query_b, value_b, proj_w, proj_b, expand_w, expand_b, reduce_w, reduce_b) = gathered
    (stream, mod, normed_in, qkv, attended, attn_out, middle, normed_mid, pre_act) = stored[:9]
    activated, mlp_out = stored[9:]
    latents, seq, width = upstream.shape
    tokens, hidden = pre_act.shape
    low, high = jnp.bfloat16, jnp.float32
    shapes = [(tokens, width, low), (tokens, hidden, low), (tokens, width, low)]
    shapes += [(tokens, 3 * width, low), (tokens, width, high), (latents * 6, width, high)]
    shapes += [(1, width, high), (1, hidden, high), (1, width, high), (1, 3 * width, high)]
    operands = [upstream.reshape(tokens, width), mod, stream, qkv, attn_out, middle, pre_act]
    operands += [mlp_out, qkv_w, proj_w, expand_w, reduce_w]
    vmem = pl.BlockSpec(memory_space=pltpu.VMEM)
    anywhere = pl.BlockSpec(memory_space=pl.ANY)
    dma = pltpu.SemaphoreType.DMA
    held = [operand for number, operand in enumerate(operands) if number != 1]
    found = pl.pallas_call(
        functools.partial(backward_kernel, seq),
        out_shape=[jax.ShapeDtypeStruct((m, n), kind) for m, n, kind in shapes],
        in_specs=[vmem if number == 1 else anywhere for number in range(len(operands))],
        out_specs=[anywhere] * 5 + [vmem] * 5,
        scratch_shapes=[pltpu.VMEM(operand.shape, operand.dtype) for operand in held]
        + [pltpu.VMEM((m, n), kind) for m, n, kind in shapes[:5]]
        + [
            pltpu.VMEM((tokens, width), high),
            pltpu.VMEM((tokens, width), high),
            pltpu.VMEM((tokens, width), low),
            dma((len(held),)),
            dma((3, hidden // STEP)),
            dma((5,)),
        ],
        compiler_params=pltpu.CompilerParams(vmem_limit_bytes=VMEM_LIMIT),
        name="backward_layer",
    )(*operands)
    (d_mlp, d_pre, d_attn, d_qkv, d_stream, d_mod, g_reduce_b, g_expand_b, g_proj_b, g_qkv_b) = found
    pairs = [(normed_in, d_qkv), (attended, d_attn), (normed_mid, d_pre), (activated, d_mlp)]
    bias_grads = (g_qkv_b[:, :width], g_qkv_b[:, 2 * width :], g_proj_b, g_expand_b, g_reduce_b)
    d_modulation = d_mod.reshape(latents, 6 * width).astype(low)
    return d_stream.reshape(upstream.shape), d_modulation, pairs, bias_grads


def on_device(
    latents,
    conditioning,
    cotangent,
    adaln_weight,
    adaln_bias,
    qkv_weight,
    query_bias,
    value_bias,
    proj_weight,
    proj_bias,
    expand_weight,
    expand_bias,
    reduce_weight,
    reduce_bias,
):
    shard_count = lax.axis_size(AXES)
    mesh_shape = (lax.axis_size("dp"), lax.axis_size("pair"))
    rows = qkv_weight.shape[1]
    in_kernels = rows % 8 == 0 and CHUNK % rows == 0
    here = lax.axis_index(AXES)
    stream = latents.astype(jnp.float32)
    cond_part = conditioning.astype(jnp.float32)
    adaln_size = adaln_bias.shape[1]
    adaln_columns = adaln_weight.reshape(LAYERS * rows, shard_count, adaln_size)
    adaln_columns = adaln_columns.transpose(1, 0, 2)
    own = conditioning.reshape(-1)
    more = -(-own.shape[0] // (8 * adaln_size)) * 8
    own = jnp.pad(own, (0, more * adaln_size - own.shape[0])).reshape(1, more, adaln_size)
    own = jnp.broadcast_to(own, (shard_count, more, adaln_size))
    adaln_columns = jnp.concatenate([adaln_columns, own], axis=1)
    adaln_columns = lax.all_to_all(adaln_columns, AXES, split_axis=0, concat_axis=0, tiled=True)
    conditioning_all = adaln_columns[:, LAYERS * rows :].reshape(shard_count, -1)
    conditioning_all = conditioning_all[:, : conditioning.size].reshape(-1, conditioning.shape[1])
    silu_low = jax.nn.silu(conditioning_all.astype(jnp.float32)).astype(jnp.bfloat16)
    silu_mine = lax.dynamic_slice_in_dim(silu_low, here * rows, rows, axis=1)
    modulation = []
    for layer in range(LAYERS):
        columns = adaln_columns[:, layer * rows : (layer + 1) * rows].reshape(-1, adaln_size)
        modulation.append(
            jnp.dot(silu_low, columns, preferred_element_type=jnp.float32)
            + adaln_bias[layer].astype(jnp.float32)
        )
    modulation = jnp.stack(modulation)
    shards = (qkv_weight, proj_weight, expand_weight, reduce_weight)
    bias_members = (query_bias, value_bias, proj_bias, expand_bias, reduce_bias)
    bias_sizes = [member.shape[1] for member in bias_members]
    room = BIAS_TILE[0] * BIAS_TILE[1]
    bias_row = jnp.concatenate(bias_members, axis=1).reshape(-1)
    bias_row = jnp.pad(bias_row, (0, room - bias_row.shape[0])).reshape(BIAS_TILE)
    weights = []
    for layer in range(LAYERS):
        block = bias_row if layer == 0 else None
        if layer == 1:
            shards, modulation = lax.optimization_barrier((shards, modulation))
            modulation = lax.all_to_all(modulation, AXES, split_axis=1, concat_axis=2, tiled=True)
        if in_kernels:
            found = gather_weights(mesh_shape, shards, block, layer)
        else:
            found = plain_gather(shards, block, layer)
        weights.append(found[0])
        if layer == 0:
            bias_rows = found[1]
    gathered = []
    at = 0
    for layer in range(LAYERS):
        biases = []
        for size in bias_sizes:
            biases.append(bias_rows[:, at : at + size].reshape(-1))
            at += size
        query_b, value_b, proj_b, expand_b, reduce_b = biases
        qkv_w, proj_w, expand_w, reduce_w = weights[layer]
        gathered.append(
            (qkv_w, query_b, value_b, proj_w, proj_b, expand_w, expand_b, reduce_w, reduce_b)
        )
    stored = [None] * LAYERS
    for layer in range(LAYERS):
        stream, stored[layer] = forward_layer(stream, modulation[layer], gathered[layer])
    outputs = stream.astype(jnp.bfloat16)
    upstream = cotangent.astype(jnp.float32)
    d_mods = [None] * LAYERS
    terms = [None] * LAYERS
    for layer in reversed(range(LAYERS)):
        upstream, d_mods[layer], pairs, bias_grads = backward_layer(
            upstream, gathered[layer], stored[layer]
        )
        flat = jnp.concatenate([grad.reshape(shard_count, -1) for grad in bias_grads], axis=1)
        flat = jnp.pad(flat, ((0, 0), (0, room - flat.shape[1]))).astype(GRAD_DTYPE)
        terms[layer] = (pairs, flat)
    terms, d_modulation = lax.optimization_barrier((terms, jnp.stack(d_mods)))
    d_mods = spread(d_modulation.transpose(1, 0, 2))
    summed = (reduce_grads if in_kernels else plain_reduce)(mesh_shape, terms)
    g_adaln_w = []
    g_adaln_b = []
    d_silu = 0.0
    for layer in range(LAYERS):
        part = d_mods[:, layer]
        g_adaln_w.append(
            jnp.einsum("bd,bf->df", silu_mine, part, preferred_element_type=jnp.float32)
        )
        mine = lax.dynamic_slice_in_dim(part, here * adaln_size, adaln_size, axis=1)
        g_adaln_b.append(jnp.sum(mine, axis=0, dtype=jnp.float32))
        d_silu = d_silu + jnp.einsum(
            "bf,df->bd", part, adaln_weight[layer], preferred_element_type=jnp.float32
        )
    d_silu = lax.all_to_all(d_silu, AXES, split_axis=0, concat_axis=1, tiled=True)
    _, pull_silu = jax.vjp(jax.nn.silu, cond_part)
    grad_conditioning = pull_silu(d_silu)[0]
    flat = summed[4].reshape(LAYERS, -1)
    small = []
    at = 0
    for size in bias_sizes:
        small.append(flat[:, at : at + size])
        at += size
    return (
        outputs,
        upstream,
        grad_conditioning,
        jnp.stack(g_adaln_w),
        jnp.stack(g_adaln_b),
        summed[0],
        small[0],
        small[1],
        summed[1],
        small[2],
        summed[2],
        small[3],
        summed[3],
        small[4],
    )


def solution(mesh):
    in_specs = (
        P(("dp", "pair"), None, None),
        P(("dp", "pair"), None),
        P(("dp", "pair"), None, None),
        P(None, ("dp", "pair"), None),
        P(None, ("dp", "pair")),
        P(None, ("dp", "pair"), None),
        P(None, ("dp", "pair")),
        P(None, ("dp", "pair")),
        P(None, ("dp", "pair"), None),
        P(None, ("dp", "pair")),
        P(None, ("dp", "pair"), None),
        P(None, ("dp", "pair")),
        P(None, ("dp", "pair"), None),
        P(None, ("dp", "pair")),
    )
    out_specs = (
        P(("dp", "pair"), None, None),
        P(("dp", "pair"), None, None),
        P(("dp", "pair"), None),
        P(None, ("dp", "pair"), None),
        P(None, ("dp", "pair")),
        P(None, ("dp", "pair"), None),
        P(None, ("dp", "pair")),
        P(None, ("dp", "pair")),
        P(None, ("dp", "pair"), None),
        P(None, ("dp", "pair")),
        P(None, ("dp", "pair"), None),
        P(None, ("dp", "pair")),
        P(None, ("dp", "pair"), None),
        P(None, ("dp", "pair")),
    )
    return jax.shard_map(
        on_device, mesh=mesh, in_specs=in_specs, out_specs=out_specs, check_vma=False
    )
```

```python
import functools

import jax
import jax.numpy as jnp
from jax import lax
from jax.experimental import pallas as pl
from jax.experimental.pallas import tpu as pltpu
from jax.sharding import PartitionSpec as P

HEADS = 12
HEAD = 64
LAYERS = 2


EPSILON = 1e-06


def gelu_tanh(values):
    return jax.nn.gelu(values, approximate=True)


AXES = ("dp", "pair")
LANES = 128
GRAD_DTYPE = jnp.bfloat16


MESH_ID = pl.DeviceIdType.MESH
BIAS_TILE = (16, 128)
CHUNK = 384
GATHER_ORDER = (0, 1, 2, 3)
SIDE_LAG = 1
CORNER_LAG = 2
OFFSETS = (0, 1, 3, 5, 6)
ORDERS = ((1, 3, 2, 0, 4), (8, 7, 5, 6, 9))
VMEM_LIMIT = 60 * 1024 * 1024


class Place:
    def __init__(self):
        self.line = lax.axis_size("dp") // 4
        spot = lax.axis_index("dp")
        self.z, self.y, self.c = spot // 4, (spot // 2) % 2, spot % 2
        self.x = lax.axis_index("pair")

    def device(self, z=None, y=None, c=None, x=None):
        z = self.z if z is None else z
        y = self.y if y is None else y
        c = self.c if c is None else c
        x = self.x if x is None else x
        return ((z * 2 + y) * 2 + c, x)

    def partner(self, axis):
        return self.device(**{axis: 1 - getattr(self, axis)})

    def greet(self):
        barrier = pltpu.get_barrier_semaphore()
        for axis in ("y", "c", "x"):
            pl.semaphore_signal(
                barrier, inc=1, device_id=self.partner(axis), device_id_type=MESH_ID
            )

        @pl.when(self.z > 0)
        def _():
            pl.semaphore_signal(
                barrier, inc=1, device_id=self.device(z=self.z - 1), device_id_type=MESH_ID
            )

        @pl.when(self.z < self.line - 1)
        def _():
            pl.semaphore_signal(
                barrier, inc=1, device_id=self.device(z=self.z + 1), device_id_type=MESH_ID
            )

        ends = (self.z > 0).astype(jnp.int32) + (self.z < self.line - 1).astype(jnp.int32)
        pl.semaphore_wait(barrier, 3 + ends)


def remote(src, dst, send, recv, device):
    return pltpu.make_async_remote_copy(
        src_ref=src,
        dst_ref=dst,
        send_sem=send,
        recv_sem=recv,
        device_id=device,
        device_id_type=MESH_ID,
    )


def gather_kernel(members, *refs):
    count = len(members)
    input_count = len(refs) - 9 - count
    ins, outs = refs[:input_count], refs[input_count : input_count + count]
    (local, zs, as_, bs, cs, zr, ar, br, cr) = refs[input_count + count :]
    place = Place()
    line, z, y, c, x = place.line, place.z, place.y, place.c, place.x
    place.greet()

    def source(k):
        number, layer = members[k]
        return ins[number] if layer is None else ins[number].at[layer]

    def at(k, zz, flip_y=False, flip_x=False):
        return outs[k].at[zz, 1 - y if flip_y else y, c, 1 - x if flip_x else x]

    def z_copy(k, src, zz, up):
        to = place.device(z=z + 1 if up else z - 1)
        return remote(src, at(k, zz), zs.at[k, 0 if up else 1, zz], zr.at[k, zz], to)

    def y_copy(k, src, dst, step, zz):
        return remote(src, dst, as_.at[k, step], ar.at[k, step, zz], place.partner("y"))

    def x_copy(k, src, dst, step, zz):
        return remote(src, dst, bs.at[k, step], br.at[k, step, zz], place.partner("x"))

    def c_copy(k, src, dst):
        return remote(src, dst, cs.at[k], cr.at[k], place.partner("c"))

    def spread(k, src, zz):
        dst = at(k, zz)
        y_copy(k, src, dst, 0, zz).start()
        x_copy(k, src, dst, 0, zz).start()
        c_copy(k, src, dst).start()

    def line_step(k, d):
        if d == 0:
            src = source(k)

            @pl.when(z < line - 1)
            def _():
                z_copy(k, src, z, True).start()

            @pl.when(z > 0)
            def _():
                z_copy(k, src, z, False).start()

            spread(k, src, z)
            pltpu.make_async_copy(src, at(k, z), local.at[k]).start()
            return

        @pl.when(z >= d)
        def _():
            zz = z - d
            z_copy(k, at(k, zz), zz, True).wait_recv()

            @pl.when(z < line - 1)
            def _():
                z_copy(k, at(k, zz), zz, True).start()

            spread(k, at(k, zz), zz)

        @pl.when(z + d < line)
        def _():
            zz = z + d
            z_copy(k, at(k, zz), zz, False).wait_recv()

            @pl.when(z > 0)
            def _():
                z_copy(k, at(k, zz), zz, False).start()

            spread(k, at(k, zz), zz)

    def at_distance(d, use):
        if d == 0:
            use(z)
            return

        @pl.when(z >= d)
        def _():
            use(z - d)

        @pl.when(z + d < line)
        def _():
            use(z + d)

    def y_first(zz):
        return zz % 2 == 0

    def side_step(k, d):
        def use(zz):
            over_y, over_x = at(k, zz, flip_y=True), at(k, zz, flip_x=True)
            y_copy(k, over_y, over_y, 0, zz).wait_recv()

            @pl.when(y_first(zz))
            def _():
                x_copy(k, over_y, over_y, 1, zz).start()

            c_copy(k, over_y, over_y).start()
            x_copy(k, over_x, over_x, 0, zz).wait_recv()

            @pl.when(jnp.logical_not(y_first(zz)))
            def _():
                y_copy(k, over_x, over_x, 1, zz).start()

            c_copy(k, over_x, over_x).start()

        at_distance(d, use)

    def corner_step(k, d):
        def use(zz):
            corner = at(k, zz, flip_y=True, flip_x=True)

            @pl.when(y_first(zz))
            def _():
                x_copy(k, corner, corner, 1, zz).wait_recv()

            @pl.when(jnp.logical_not(y_first(zz)))
            def _():
                y_copy(k, corner, corner, 1, zz).wait_recv()

            c_copy(k, corner, corner).start()

        at_distance(d, use)

    turns = [k + count - 4 for k in GATHER_ORDER]
    turns = turns[:1] + list(range(count - 4)) + turns[1:]
    for wave in range(count + line + CORNER_LAG):
        for turn, k in enumerate(turns):
            step = wave - turn
            if 0 <= step < line:
                line_step(k, step)
            if 0 <= step - SIDE_LAG < line:
                side_step(k, step - SIDE_LAG)
            if 0 <= step - CORNER_LAG < line:
                corner_step(k, step - CORNER_LAG)

    for k in range(count):
        pltpu.make_async_copy(source(k), at(k, z), local.at[k]).wait()
        theirs = outs[k].at[:, :, 1 - c]
        own = outs[k].at[:, :, c]
        c_copy(k, theirs, theirs).wait_recv()
        c_copy(k, own, own).wait_send()
        column = outs[k].at[:, y, c, x]
        y_copy(k, column, column, 0, 0).wait_send()
        x_copy(k, column, column, 0, 0).wait_send()
        part = outs[k].at[pl.ds(0, line // 2), y, c, x]
        y_copy(k, part, part, 1, 0).wait_send()
        x_copy(k, part, part, 1, 0).wait_send()
        for zz in range(line):

            @pl.when((z < line - 1) & (zz <= z))
            def _():
                z_copy(k, at(k, zz), zz, True).wait_send()

            @pl.when((z > 0) & (zz >= z))
            def _():
                z_copy(k, at(k, zz), zz, False).wait_send()


def gather_weights(mesh_shape, shards, bias_block, layer):
    dp_size, pair_size = mesh_shape
    line = dp_size // 4
    members = []
    outs = []
    operands = list(shards)
    if bias_block is not None:
        members.append((len(shards), None))
        outs.append(bias_block)
        operands.append(bias_block)
    for number, shard in enumerate(shards):
        members.append((number, layer))
        outs.append(shard[layer])
    count = len(members)
    shapes = [
        jax.ShapeDtypeStruct((line, 2, 2, pair_size) + out.shape, out.dtype) for out in outs
    ]
    dma = pltpu.SemaphoreType.DMA
    full = pl.pallas_call(
        functools.partial(gather_kernel, members),
        out_shape=shapes,
        in_specs=[pl.BlockSpec(memory_space=pl.ANY)] * len(operands),
        out_specs=[pl.BlockSpec(memory_space=pl.ANY)] * count,
        scratch_shapes=[
            dma((count,)),
            dma((count, 2, line)),
            dma((count, 2)),
            dma((count, 2)),
            dma((count,)),
            dma((count, line)),
            dma((count, 2, line)),
            dma((count, 2, line)),
            dma((count,)),
        ],
        compiler_params=pltpu.CompilerParams(collective_id=layer, has_side_effects=True),
        cost_estimate=pl.CostEstimate(flops=0, bytes_accessed=200_000_000, transcendentals=0),
        name="gather_weights_%d" % layer,
    )(*operands)
    weights = [weight.reshape(-1, weight.shape[-1]) for weight in full[-len(shards) :]]
    biases = None if bias_block is None else full[0].reshape(dp_size * pair_size, -1)
    return weights, biases


def reduce_kernel(*refs):
    count, each = 10, 5
    operands = [refs[8 * slot : 8 * slot + 8] for slot in range(2)]
    given = refs[16:18]
    outs = refs[18 : 18 + each]
    full = refs[18 + each : 22 + each]
    at = 22 + each
    from_c, from_b, from_a, from_low, from_high = [
        refs[at + count * j : at + count * (j + 1)] for j in range(5)
    ]
    at += 5 * count
    wide, narrow, load = refs[at : at + 3]
    c_send, c_recv, b_send, b_recv, a_send, a_recv, up_send, up_recv, down_send, down_recv = refs[
        at + 3 :
    ]
    full = list(full) + [given[0]] + list(full) + [given[1]]
    place = Place()
    line, z, y, c, x = place.line, place.z, place.y, place.c, place.x
    half = line // 2
    place.greet()

    def axes(zz):
        return ("x", "y") if zz % 2 == 0 else ("y", "x")

    def add(total_ref, total_at, more_ref, more_at):
        total_ref[total_at] = (
            total_ref[total_at].astype(jnp.float32) + more_ref[more_at].astype(jnp.float32)
        ).astype(total_ref.dtype)

    def c_copy(k, zz):
        return remote(
            full[k].at[zz, :, 1 - c],
            from_c[k].at[zz],
            c_send.at[k, zz],
            c_recv.at[k, zz],
            place.partner("c"),
        )

    def b_copy(k, zz):
        first = axes(zz)[0]
        src = from_c[k].at[zz, :, 1 - x] if first == "x" else from_c[k].at[zz, 1 - y]
        return remote(
            src, from_b[k].at[zz], b_send.at[k, zz], b_recv.at[k, zz], place.partner(first)
        )

    def a_copy(k, zz):
        second = axes(zz)[1]
        other = 1 - getattr(place, second)
        return remote(
            from_b[k].at[zz, other],
            from_a[k].at[zz],
            a_send.at[k, zz],
            a_recv.at[k, zz],
            place.partner(second),
        )

    def up_copy(k, t, src):
        return remote(
            src, from_low[k].at[t], up_send.at[k, t], up_recv.at[k, t], place.device(z=z + 1)
        )

    def down_copy(k, t, src):
        return remote(
            src, from_high[k].at[t], down_send.at[k, t], down_recv.at[k, t], place.device(z=z - 1)
        )

    def zs_of(h):
        return range(h * half, (h + 1) * half)

    sequence = [k for k in ORDERS[0] + ORDERS[1] if k % each < 4]

    def sides(k):
        number = sequence.index(k) % 2
        left, right = operands[k // each][2 * (k % each) : 2 * (k % each) + 2]
        if left.shape[1] > right.shape[1]:
            left_at, right_at = wide, narrow
        else:
            left_at, right_at = narrow, wide
        left_at = left_at.at[number, :, pl.ds(0, left.shape[1])]
        right_at = right_at.at[number, :, pl.ds(0, right.shape[1])]
        return (left, left_at, load.at[number, 0]), (right, right_at, load.at[number, 1])

    for k in sequence[:2]:
        for side in sides(k):
            pltpu.make_async_copy(*side).start()

    def compute(k, h):
        if k % each < 4:
            (_, left, _), (_, right, _) = sides(k)
            if h == 0:
                for side in sides(k):
                    pltpu.make_async_copy(*side).wait()
            if k >= each:
                for zz in zs_of(h):
                    c_copy(k - each, zz).wait_send()
            rows = full[k].shape[4]
            height = full[k].shape[0] * 8 * rows // 2
            blocks = CHUNK // rows
            for chunk in range(height // CHUNK):
                base = h * half * 8 + chunk * blocks
                first = h * height + chunk * CHUNK

                def tile(j, carry, base=base, first=first):
                    columns = pl.ds(pl.multiple_of(j * 768, 768), 768)
                    product = lax.dot_general(
                        left[:, first : first + CHUNK],
                        right[:, columns],
                        (((0,), (0,)), ((), ())),
                        preferred_element_type=jnp.float32,
                    )
                    for block in range(blocks):
                        n = base + block
                        full[k][n // 8, (n // 4) % 2, (n // 2) % 2, n % 2, :, columns] = product[
                            block * rows : (block + 1) * rows
                        ].astype(jnp.bfloat16)
                    return carry

                lax.fori_loop(0, right.shape[1] // 768, tile, 0)
            number = sequence.index(k) + 2
            if h == 1 and number < len(sequence):
                for side in sides(sequence[number]):
                    pltpu.make_async_copy(*side).start()
        for zz in zs_of(h):
            c_copy(k, zz).start()

    def after_c(k, h):
        def sweep(zz, other):
            for side in range(2):
                yy, xx = (side, other) if axes(zz)[0] == "x" else (other, side)
                add(from_c[k], (zz, yy, xx), full[k], (zz, yy, c, xx))

        for zz in zs_of(h):
            mine = getattr(place, axes(zz)[0])
            c_copy(k, zz).wait_recv()
            sweep(zz, 1 - mine)
            b_copy(k, zz).start()
        for zz in zs_of(h):
            sweep(zz, getattr(place, axes(zz)[0]))

    def after_b(k, h):
        def sweep(zz, side):
            yy, xx = (side, x) if axes(zz)[0] == "x" else (y, side)
            add(from_b[k], (zz, side), from_c[k], (zz, yy, xx))

        for zz in zs_of(h):
            mine = getattr(place, axes(zz)[1])
            b_copy(k, zz).wait_recv()
            sweep(zz, 1 - mine)
            a_copy(k, zz).start()
        for zz in zs_of(h):
            sweep(zz, getattr(place, axes(zz)[1]))

    def after_a(k, h):
        for zz in zs_of(h):
            a_copy(k, zz).wait_recv()
            add(from_a[k], (zz,), from_b[k], (zz, getattr(place, axes(zz)[1])))

    def hop(k, h, step):
        for t in reversed(range(h * half, (h + 1) * half)):

            @pl.when((z == step) & (z < t))
            def _():
                if step == 0:
                    up_copy(k, t, from_a[k].at[t]).start()
                else:
                    up_copy(k, t, from_low[k].at[t]).wait_recv()
                    add(from_low[k], (t,), from_a[k], (t,))
                    up_copy(k, t, from_low[k].at[t]).start()

        for t in range(h * half, (h + 1) * half):

            @pl.when((z == line - 1 - step) & (z > t))
            def _():
                if step == 0:
                    down_copy(k, t, from_a[k].at[t]).start()
                else:
                    down_copy(k, t, from_high[k].at[t]).wait_recv()
                    add(from_high[k], (t,), from_a[k], (t,))
                    down_copy(k, t, from_high[k].at[t]).start()

    def finish(k, h):
        for t in range(h * half, (h + 1) * half):

            @pl.when(z == t)
            def _():
                total = from_a[k][t].astype(jnp.float32)
                if t > 0:
                    up_copy(k, t, from_low[k].at[t]).wait_recv()
                    total = total + from_low[k][t].astype(jnp.float32)
                if t < line - 1:
                    down_copy(k, t, from_high[k].at[t]).wait_recv()
                    total = total + from_high[k][t].astype(jnp.float32)
                outs[k % each][1 - k // each] = total

    def settle(k, h):
        for t in zs_of(h):
            if k % each == 4 or k >= each:
                c_copy(k, t).wait_send()
            b_copy(k, t).wait_send()
            a_copy(k, t).wait_send()

            @pl.when(z < t)
            def _():
                up_copy(k, t, from_a[k].at[t]).wait_send()

            @pl.when(z > t)
            def _():
                down_copy(k, t, from_a[k].at[t]).wait_send()

    units = [(k, h) for k in ORDERS[0] + ORDERS[1] for h in range(2)]
    stages = [compute, after_c, after_b, after_a]
    stages += [functools.partial(hop, step=step) for step in range(line)]
    stages += [finish]
    offsets = list(OFFSETS) + [OFFSETS[-1] + 1 + step for step in range(line)]
    for wave in range(len(units) + offsets[-1]):
        for number, (k, h) in enumerate(units):
            if wave - number in offsets:
                stages[offsets.index(wave - number)](k, h)
    for k, h in units:
        settle(k, h)


def reduce_grads(mesh_shape, terms):
    dp_size, pair_size = mesh_shape
    shard_count = dp_size * pair_size
    line = dp_size // 4
    lead = (line, 2, 2, pair_size)
    low = jnp.bfloat16
    pairs = terms[0][0]
    tokens = pairs[0][0].shape[0]
    shapes = [(left.shape[1] // shard_count, right.shape[1]) for left, right in pairs]
    scratch = [pltpu.VMEM(lead + shape, low) for shape in shapes]
    shapes.append(BIAS_TILE)
    for space in ((line, 2, 2), (line, 2), (line,), (line,), (line,)):
        scratch += [pltpu.VMEM(space + shape, low) for shape in shapes * 2]
    dma = pltpu.SemaphoreType.DMA
    widest = max(side.shape[1] for pair in pairs for side in pair)
    scratch += [pltpu.VMEM((2, tokens, widest), low)]
    scratch += [pltpu.VMEM((2, tokens, min(pairs[0][0].shape[1], widest)), low), dma((2, 2))]
    scratch += [dma((2 * len(shapes), line))] * 10
    operands = [side for layer in (1, 0) for pair in terms[layer][0] for side in pair]
    operands += [terms[layer][1].reshape(lead + BIAS_TILE) for layer in (1, 0)]
    vmem = pl.BlockSpec(memory_space=pltpu.VMEM)
    return pl.pallas_call(
        reduce_kernel,
        out_shape=[jax.ShapeDtypeStruct((LAYERS,) + shape, jnp.float32) for shape in shapes],
        in_specs=[pl.BlockSpec(memory_space=pl.ANY)] * 16 + [vmem] * 2,
        out_specs=[vmem] * len(shapes),
        scratch_shapes=scratch,
        compiler_params=pltpu.CompilerParams(
            collective_id=LAYERS, has_side_effects=True, vmem_limit_bytes=VMEM_LIMIT
        ),
        cost_estimate=pl.CostEstimate(flops=0, bytes_accessed=400_000_000, transcendentals=0),
        name="reduce_grads",
    )(*operands)


def spread(values):
    count = lax.axis_size(AXES)
    copies = jnp.broadcast_to(values[None], (count,) + values.shape)
    copies = lax.all_to_all(copies, AXES, split_axis=0, concat_axis=0, tiled=True)
    return copies.reshape((-1,) + values.shape[1:])


def plain_gather(shards, bias_block, layer):
    weights = [lax.all_gather(shard[layer], AXES, axis=0, tiled=True) for shard in shards]
    if bias_block is None:
        return weights, None
    return weights, lax.all_gather(bias_block.reshape(1, -1), AXES, axis=0, tiled=True)


def plain_reduce(mesh_shape, terms):
    layers = []
    for pairs, bias_rows in terms:
        grads = []
        for left, right in pairs:
            product = jnp.einsum("tk,tn->kn", left, right, preferred_element_type=jnp.float32)
            grads.append(product.astype(GRAD_DTYPE))
        grads.append(bias_rows)
        layers.append(
            [
                lax.psum_scatter(grad, AXES, scatter_dimension=0, tiled=True).astype(jnp.float32)
                for grad in grads
            ]
        )
    return [jnp.stack(member) for member in zip(*layers)]


TOKENS_NT = (((1,), (1,)), ((), ()))
TOKENS_TN = (((0,), (0,)), ((), ()))
WIDE = 2 * HEAD
STEP = 768
UNROLL = 2
UNROLL_BACK = 2


def dot32(left, right, dims=(((1,), (0,)), ((), ()))):
    return lax.dot_general(left, right, dims, preferred_element_type=jnp.float32)


def standardize(values):
    centre = values - jnp.mean(values, axis=-1, keepdims=True)
    inverse = lax.rsqrt(jnp.mean(centre * centre, axis=-1, keepdims=True) + EPSILON)
    return centre * inverse, inverse


def head_masks():
    lane = lax.broadcasted_iota(jnp.int32, (1, WIDE), 1)
    first = (lane < HEAD).astype(jnp.float32)
    return lane < HEAD, (first.astype(jnp.bfloat16), (1.0 - first).astype(jnp.bfloat16))


def scaled(query):
    return query * jnp.bfloat16(HEAD ** (-0.5))


def softmax_parts(query, keys):
    scores = dot32(query, keys, TOKENS_NT)
    weights = jnp.exp(scores - jnp.max(scores, axis=-1, keepdims=True))
    return weights * (1.0 / jnp.sum(weights, axis=-1, keepdims=True))


def forward_steps(seq, refs):
    (stream, mod, qkv_w, qkv_b, proj_w, proj_b, expand_w, expand_b, reduce_w, reduce_b) = refs[:10]
    (normed_in, qkv, attended, attn_out, middle, normed_mid, pre_act, activated, mlp_out, out) = refs[
        10:
    ]
    tokens, width = stream.shape
    latents = tokens // seq
    hidden = pre_act.shape[1]
    groups = width // WIDE

    def row(b, number):
        return mod[b * 6 + number : b * 6 + number + 1, :]

    def rows(b):
        return slice(b * seq, (b + 1) * seq)

    def enter(b):
        values, _ = standardize(stream[rows(b), :])
        values = values * (1.0 + row(b, 1)) + row(b, 0)
        normed_in[rows(b), :] = values.astype(jnp.bfloat16)

    def project(j):
        at = slice(j * STEP, (j + 1) * STEP)
        qkv[:, at] = (dot32(normed_in[...], qkv_w[:, at]) + qkv_b[:, at]).astype(jnp.bfloat16)

    def attend(b, low, high):
        is_first, masks = head_masks()

        def one(p, carry):
            here = rows(b)
            query = qkv[here, pl.ds(pl.multiple_of(p * WIDE, WIDE), WIDE)]
            keys = qkv[here, pl.ds(pl.multiple_of(width + p * WIDE, WIDE), WIDE)]
            values = qkv[here, pl.ds(pl.multiple_of(2 * width + p * WIDE, WIDE), WIDE)]
            query = scaled(query)
            parts = [
                dot32(softmax_parts(query * mask, keys).astype(jnp.bfloat16), values)
                for mask in masks
            ]
            attended[here, pl.ds(pl.multiple_of(p * WIDE, WIDE), WIDE)] = jnp.where(
                is_first, parts[0], parts[1]
            ).astype(jnp.bfloat16)
            return carry

        lax.fori_loop(low, high, one, 0, unroll=UNROLL)

    def leave(b):
        result = dot32(attended[rows(b), :], proj_w[...]) + proj_b[...]
        attn_out[rows(b), :] = result
        state = stream[rows(b), :] + row(b, 2) * result
        middle[rows(b), :] = state
        values, _ = standardize(state)
        values = values * (1.0 + row(b, 4)) + row(b, 3)
        normed_mid[rows(b), :] = values.astype(jnp.bfloat16)

    def expand(j):
        at = slice(j * STEP, (j + 1) * STEP)
        before = dot32(normed_mid[...], expand_w[:, at]) + expand_b[:, at]
        pre_act[:, at] = before
        activated[:, at] = gelu_tanh(before).astype(jnp.bfloat16)

    def contract(b):
        result = dot32(activated[rows(b), :], reduce_w[...]) + reduce_b[...]
        mlp_out[rows(b), :] = result
        out[rows(b), :] = middle[rows(b), :] + row(b, 5) * result

    steps = [functools.partial(enter, b) for b in range(latents)]
    steps += [functools.partial(project, j) for j in range(3 * width // STEP)]
    third = groups // 3
    for b in range(latents):
        for low in range(0, groups, third):
            steps.append(functools.partial(attend, b, low, low + third))
    steps += [functools.partial(leave, b) for b in range(latents)]
    steps += [functools.partial(expand, j) for j in range(hidden // STEP)]
    steps += [functools.partial(contract, b) for b in range(latents)]
    return steps


def forward_operands(stream, modulation, gathered):
    (qkv_w, query_b, value_b, proj_w, proj_b, expand_w, expand_b, reduce_w, reduce_b) = gathered
    latents, seq, width = stream.shape
    qkv_b = jnp.concatenate([query_b, jnp.zeros_like(query_b), value_b])
    flat = [bias.astype(jnp.float32)[None] for bias in (qkv_b, proj_b, expand_b, reduce_b)]
    operands = [stream.reshape(-1, width), modulation.reshape(latents * 6, width)]
    for weight, bias in zip((qkv_w, proj_w, expand_w, reduce_w), flat):
        operands += [weight, bias]
    return operands


def forward_shapes(tokens, width, hidden):
    low, high = jnp.bfloat16, jnp.float32
    kinds = [(width, low), (3 * width, low), (width, low), (width, high), (width, high)]
    kinds += [(width, low), (hidden, high), (hidden, low), (width, high), (width, high)]
    return [jax.ShapeDtypeStruct((tokens, columns), kind) for columns, kind in kinds]


def forward_layer(stream, modulation, gathered):
    latents, seq, width = stream.shape
    operands = forward_operands(stream, modulation, gathered)

    shapes = forward_shapes(latents * seq, width, operands[6].shape[1])
    large = (0, 2, 4, 6, 8)
    hidden_tiles = operands[6].shape[1] // STEP
    needs = {"enter": 0, "project": 2, "leave": 4, "expand": 6, "contract": 8}
    gives = {"enter": (0,), "project": (1,), "attend": (2,), "leave": (3, 4, 5)}
    gives.update({"contract": (8, 9)})

    def kernel(*refs):
        ins, outs = refs[:10], refs[10:20]
        held, made = refs[20:25], refs[25:35]
        in_sem, out_sem, tile_sem = refs[35:]
        local = list(ins)
        for number, which in enumerate(large):
            local[which] = held[number]

        def fetch(which):
            number = large.index(which)
            return pltpu.make_async_copy(ins[which], held[number], in_sem.at[number])

        def store(which):
            return pltpu.make_async_copy(made[which], outs[which], out_sem.at[which])

        def store_tile(which, j):
            at = pl.ds(j * STEP, STEP)
            return pltpu.make_async_copy(
                made[which].at[:, at], outs[which].at[:, at], tile_sem.at[which - 6, j]
            )

        for which in large:
            fetch(which).start()
        steps = forward_steps(seq, (*local, *made))
        names = [step.func.__name__ for step in steps]
        for number, (name, step) in enumerate(zip(names, steps)):
            if name in needs and name not in names[:number]:
                fetch(needs[name]).wait()
            step()
            if name == "expand":
                for which in (6, 7):
                    store_tile(which, step.args[0]).start()
            elif name not in names[number + 1 :]:
                for which in gives[name]:
                    store(which).start()
        for which in range(10):
            if which in (6, 7):
                for j in range(hidden_tiles):
                    store_tile(which, j).wait()
            else:
                store(which).wait()

    vmem = pl.BlockSpec(memory_space=pltpu.VMEM)
    anywhere = pl.BlockSpec(memory_space=pl.ANY)
    dma = pltpu.SemaphoreType.DMA
    saved = pl.pallas_call(
        kernel,
        out_shape=shapes,
        in_specs=[anywhere if number in large else vmem for number in range(len(operands))],
        out_specs=[anywhere] * len(shapes),
        scratch_shapes=[pltpu.VMEM(operands[which].shape, operands[which].dtype) for which in large]
        + [pltpu.VMEM(shape.shape, shape.dtype) for shape in shapes]
        + [dma((len(large),)), dma((len(shapes),)), dma((2, hidden_tiles))],
        compiler_params=pltpu.CompilerParams(vmem_limit_bytes=VMEM_LIMIT),
        name="forward_layer",
    )(*operands)
    return saved[-1].reshape(stream.shape), (operands[0], operands[1], *saved[:-1])


def backward_kernel(seq, *refs):
    given, results = refs[:12], refs[12:17]
    mod = given[1]
    (d_mod, g_reduce_b, g_expand_b, g_proj_b, g_qkv_b) = refs[17:22]
    held, made = refs[22:33], refs[33:38]
    (upstream, stream, qkv, attn_out, middle, pre_act, mlp_out) = held[:7]
    (qkv_w, proj_w, expand_w, reduce_w) = held[7:]
    (d_mlp, d_pre, d_attn, d_qkv, d_stream) = made
    (d_normed, d_middle, d_attended, in_sem, tile_sem, out_sem) = refs[38:]
    tokens, width = stream.shape
    latents = tokens // seq
    hidden = pre_act.shape[1]
    groups = width // WIDE
    low = jnp.bfloat16

    def row(b, number):
        return mod[b * 6 + number : b * 6 + number + 1, :]

    def put(b, number, value):
        d_mod[b * 6 + number : b * 6 + number + 1, :] = jnp.sum(value, axis=0, keepdims=True)

    def rows(b):
        return slice(b * seq, (b + 1) * seq)

    def total(value):
        return jnp.sum(value.astype(jnp.float32), axis=0, keepdims=True)

    outside = given[:1] + given[2:]

    def fetch(number):
        return pltpu.make_async_copy(outside[number], held[number], in_sem.at[number])

    def fetch_tiles(j):
        at = pl.ds(pl.multiple_of(j * STEP, STEP), STEP)
        return (
            pltpu.make_async_copy(outside[10].at[at], reduce_w.at[at], tile_sem.at[0, j]),
            pltpu.make_async_copy(outside[5].at[:, at], pre_act.at[:, at], tile_sem.at[1, j]),
            pltpu.make_async_copy(outside[9].at[:, at], expand_w.at[:, at], tile_sem.at[2, j]),
        )

    def store(number):
        return pltpu.make_async_copy(made[number], results[number], out_sem.at[number])

    fetch(0).start()
    fetch(6).start()
    for j in range(hidden // STEP):
        for copy in fetch_tiles(j):
            copy.start()
    for number in (4, 3, 8, 2, 7, 1):
        fetch(number).start()
    fetch(0).wait()
    fetch(6).wait()
    g_reduce_b[...] = jnp.zeros_like(g_reduce_b)
    g_proj_b[...] = jnp.zeros_like(g_proj_b)
    for b in range(latents):
        above = upstream[rows(b), :]
        put(b, 5, above * mlp_out[rows(b), :])
        value = (row(b, 5) * above).astype(low)
        d_mlp[rows(b), :] = value
        g_reduce_b[...] += total(value)

    store(0).start()
    d_normed[...] = jnp.zeros_like(d_normed)

    def through(j, carry):
        for copy in fetch_tiles(j):
            copy.wait()
        at = pl.ds(pl.multiple_of(j * STEP, STEP), STEP)
        inner = dot32(d_mlp[...], reduce_w[at, :], TOKENS_NT)
        u = pre_act[:, at]
        rate = (2.0 / jnp.pi) ** 0.5
        bend = jnp.tanh(rate * (u + 0.044715 * (u * u * u)))
        slope = 0.5 * (1.0 + bend) + 0.5 * u * (1.0 - bend * bend) * rate * (
            1.0 + 3.0 * 0.044715 * (u * u)
        )
        value = (inner * slope).astype(low)
        d_pre[:, at] = value
        g_expand_b[:, at] = total(value)
        d_normed[...] += dot32(value, expand_w[:, at], TOKENS_NT)
        return carry

    lax.fori_loop(0, hidden // STEP, through, 0)
    store(1).start()
    for number in (4, 3, 8):
        fetch(number).wait()

    def norm_back(b, source, scale_row, shift_row):
        unit, inverse = standardize(source[rows(b), :])
        flow = d_normed[rows(b), :]
        put(b, shift_row, flow)
        put(b, scale_row, flow * unit)
        flow = flow * (1.0 + row(b, scale_row))
        mean = jnp.mean(flow, axis=-1, keepdims=True)
        along = jnp.mean(flow * unit, axis=-1, keepdims=True)
        return inverse * (flow - mean - unit * along)

    for b in range(latents):
        value = norm_back(b, middle, 4, 3) + upstream[rows(b), :]
        d_middle[rows(b), :] = value
        put(b, 2, value * attn_out[rows(b), :])
        value = (row(b, 2) * value).astype(low)
        d_attn[rows(b), :] = value
        g_proj_b[...] += total(value)
    store(2).start()
    d_attended[...] = dot32(d_attn[...], proj_w[...], TOKENS_NT).astype(low)
    fetch(2).wait()

    is_first, masks = head_masks()
    root = HEAD ** (-0.5)
    for b in range(latents):

        def one(p, carry, b=b):
            here = rows(b)
            at_q = pl.ds(pl.multiple_of(p * WIDE, WIDE), WIDE)
            at_k = pl.ds(pl.multiple_of(width + p * WIDE, WIDE), WIDE)
            at_v = pl.ds(pl.multiple_of(2 * width + p * WIDE, WIDE), WIDE)
            query, keys, values = qkv[here, at_q], qkv[here, at_k], qkv[here, at_v]
            flow = d_attended[here, at_q]
            parts = []
            for mask in masks:
                scores = dot32(keys, scaled(query) * mask, TOKENS_NT)
                weights = jnp.exp(scores - jnp.max(scores, axis=0, keepdims=True))
                probs = weights * (1.0 / jnp.sum(weights, axis=0, keepdims=True))
                d_probs = dot32(values, flow * mask, TOKENS_NT)
                mixed = probs * d_probs
                d_scores = (mixed - probs * jnp.sum(mixed, axis=0, keepdims=True)).astype(low)
                parts.append(
                    (
                        dot32(d_scores, keys, TOKENS_TN) * root,
                        dot32(d_scores, query) * root,
                        dot32(probs.astype(low), flow),
                    )
                )
            for at, first, second in zip((at_q, at_k, at_v), *parts):
                d_qkv[here, at] = jnp.where(is_first, first, second).astype(low)
            return carry

        lax.fori_loop(0, groups, one, 0, unroll=UNROLL_BACK)

    store(3).start()
    fetch(7).wait()
    fetch(1).wait()
    for j in range(3):
        at = slice(j * width, (j + 1) * width)
        g_qkv_b[:, at] = total(d_qkv[:, at])
    d_normed[...] = dot32(d_qkv[...], qkv_w[...], TOKENS_NT)
    for b in range(latents):
        d_stream[rows(b), :] = d_middle[rows(b), :] + norm_back(b, stream, 1, 0)
    store(4).start()
    for number in range(5):
        store(number).wait()


def backward_layer(upstream, gathered, stored):
    (qkv_w, query_b, value_b, proj_w, proj_b, expand_w, expand_b, reduce_w, reduce_b) = gathered
    (stream, mod, normed_in, qkv, attended, attn_out, middle, normed_mid, pre_act) = stored[:9]
    activated, mlp_out = stored[9:]
    latents, seq, width = upstream.shape
    tokens, hidden = pre_act.shape
    low, high = jnp.bfloat16, jnp.float32
    shapes = [(tokens, width, low), (tokens, hidden, low), (tokens, width, low)]
    shapes += [(tokens, 3 * width, low), (tokens, width, high), (latents * 6, width, high)]
    shapes += [(1, width, high), (1, hidden, high), (1, width, high), (1, 3 * width, high)]
    operands = [upstream.reshape(tokens, width), mod, stream, qkv, attn_out, middle, pre_act]
    operands += [mlp_out, qkv_w, proj_w, expand_w, reduce_w]
    vmem = pl.BlockSpec(memory_space=pltpu.VMEM)
    anywhere = pl.BlockSpec(memory_space=pl.ANY)
    dma = pltpu.SemaphoreType.DMA
    held = [operand for number, operand in enumerate(operands) if number != 1]
    found = pl.pallas_call(
        functools.partial(backward_kernel, seq),
        out_shape=[jax.ShapeDtypeStruct((m, n), kind) for m, n, kind in shapes],
        in_specs=[vmem if number == 1 else anywhere for number in range(len(operands))],
        out_specs=[anywhere] * 5 + [vmem] * 5,
        scratch_shapes=[pltpu.VMEM(operand.shape, operand.dtype) for operand in held]
        + [pltpu.VMEM((m, n), kind) for m, n, kind in shapes[:5]]
        + [
            pltpu.VMEM((tokens, width), high),
            pltpu.VMEM((tokens, width), high),
            pltpu.VMEM((tokens, width), low),
            dma((len(held),)),
            dma((3, hidden // STEP)),
            dma((5,)),
        ],
        compiler_params=pltpu.CompilerParams(vmem_limit_bytes=VMEM_LIMIT),
        name="backward_layer",
    )(*operands)
    (d_mlp, d_pre, d_attn, d_qkv, d_stream, d_mod, g_reduce_b, g_expand_b, g_proj_b, g_qkv_b) = found
    pairs = [(normed_in, d_qkv), (attended, d_attn), (normed_mid, d_pre), (activated, d_mlp)]
    bias_grads = (g_qkv_b[:, :width], g_qkv_b[:, 2 * width :], g_proj_b, g_expand_b, g_reduce_b)
    d_modulation = d_mod.reshape(latents, 6 * width).astype(low)
    return d_stream.reshape(upstream.shape), d_modulation, pairs, bias_grads


def on_device(
    latents,
    conditioning,
    cotangent,
    adaln_weight,
    adaln_bias,
    qkv_weight,
    query_bias,
    value_bias,
    proj_weight,
    proj_bias,
    expand_weight,
    expand_bias,
    reduce_weight,
    reduce_bias,
):
    shard_count = lax.axis_size(AXES)
    mesh_shape = (lax.axis_size("dp"), lax.axis_size("pair"))
    rows = qkv_weight.shape[1]
    in_kernels = rows % 8 == 0 and CHUNK % rows == 0
    here = lax.axis_index(AXES)
    stream = latents.astype(jnp.float32)
    cond_part = conditioning.astype(jnp.float32)
    adaln_size = adaln_bias.shape[1]
    adaln_columns = adaln_weight.reshape(LAYERS * rows, shard_count, adaln_size)
    adaln_columns = adaln_columns.transpose(1, 0, 2)
    own = conditioning.reshape(-1)
    more = -(-own.shape[0] // (8 * adaln_size)) * 8
    own = jnp.pad(own, (0, more * adaln_size - own.shape[0])).reshape(1, more, adaln_size)
    own = jnp.broadcast_to(own, (shard_count, more, adaln_size))
    adaln_columns = jnp.concatenate([adaln_columns, own], axis=1)
    adaln_columns = lax.all_to_all(adaln_columns, AXES, split_axis=0, concat_axis=0, tiled=True)
    conditioning_all = adaln_columns[:, LAYERS * rows :].reshape(shard_count, -1)
    conditioning_all = conditioning_all[:, : conditioning.size].reshape(-1, conditioning.shape[1])
    silu_low = jax.nn.silu(conditioning_all.astype(jnp.float32)).astype(jnp.bfloat16)
    silu_mine = lax.dynamic_slice_in_dim(silu_low, here * rows, rows, axis=1)
    modulation = []
    for layer in range(LAYERS):
        columns = adaln_columns[:, layer * rows : (layer + 1) * rows].reshape(-1, adaln_size)
        modulation.append(
            jnp.dot(silu_low, columns, preferred_element_type=jnp.float32)
            + adaln_bias[layer].astype(jnp.float32)
        )
    modulation = jnp.stack(modulation)
    shards = (qkv_weight, proj_weight, expand_weight, reduce_weight)
    bias_members = (query_bias, value_bias, proj_bias, expand_bias, reduce_bias)
    bias_sizes = [member.shape[1] for member in bias_members]
    room = BIAS_TILE[0] * BIAS_TILE[1]
    bias_row = jnp.concatenate(bias_members, axis=1).reshape(-1)
    bias_row = jnp.pad(bias_row, (0, room - bias_row.shape[0])).reshape(BIAS_TILE)
    weights = []
    for layer in range(LAYERS):
        block = bias_row if layer == 0 else None
        if layer == 1:
            shards, modulation = lax.optimization_barrier((shards, modulation))
            modulation = lax.all_to_all(modulation, AXES, split_axis=1, concat_axis=2, tiled=True)
        if in_kernels:
            found = gather_weights(mesh_shape, shards, block, layer)
        else:
            found = plain_gather(shards, block, layer)
        weights.append(found[0])
        if layer == 0:
            bias_rows = found[1]
    gathered = []
    at = 0
    for layer in range(LAYERS):
        biases = []
        for size in bias_sizes:
            biases.append(bias_rows[:, at : at + size].reshape(-1))
            at += size
        query_b, value_b, proj_b, expand_b, reduce_b = biases
        qkv_w, proj_w, expand_w, reduce_w = weights[layer]
        gathered.append(
            (qkv_w, query_b, value_b, proj_w, proj_b, expand_w, expand_b, reduce_w, reduce_b)
        )
    stored = [None] * LAYERS
    for layer in range(LAYERS):
        stream, stored[layer] = forward_layer(stream, modulation[layer], gathered[layer])
    outputs = stream.astype(jnp.bfloat16)
    upstream = cotangent.astype(jnp.float32)
    d_mods = [None] * LAYERS
    terms = [None] * LAYERS
    for layer in reversed(range(LAYERS)):
        upstream, d_mods[layer], pairs, bias_grads = backward_layer(
            upstream, gathered[layer], stored[layer]
        )
        flat = jnp.concatenate([grad.reshape(shard_count, -1) for grad in bias_grads], axis=1)
        flat = jnp.pad(flat, ((0, 0), (0, room - flat.shape[1]))).astype(GRAD_DTYPE)
        terms[layer] = (pairs, flat)
    terms, d_modulation = lax.optimization_barrier((terms, jnp.stack(d_mods)))
    d_mods = spread(d_modulation.transpose(1, 0, 2))
    summed = (reduce_grads if in_kernels else plain_reduce)(mesh_shape, terms)
    g_adaln_w = []
    g_adaln_b = []
    d_silu = 0.0
    for layer in range(LAYERS):
        part = d_mods[:, layer]
        g_adaln_w.append(
            jnp.einsum("bd,bf->df", silu_mine, part, preferred_element_type=jnp.float32)
        )
        mine = lax.dynamic_slice_in_dim(part, here * adaln_size, adaln_size, axis=1)
        g_adaln_b.append(jnp.sum(mine, axis=0, dtype=jnp.float32))
        d_silu = d_silu + jnp.einsum(
            "bf,df->bd", part, adaln_weight[layer], preferred_element_type=jnp.float32
        )
    d_silu = lax.all_to_all(d_silu, AXES, split_axis=0, concat_axis=1, tiled=True)
    _, pull_silu = jax.vjp(jax.nn.silu, cond_part)
    grad_conditioning = pull_silu(d_silu)[0]
    flat = summed[4].reshape(LAYERS, -1)
    small = []
    at = 0
    for size in bias_sizes:
        small.append(flat[:, at : at + size])
        at += size
    return (
        outputs,
        upstream,
        grad_conditioning,
        jnp.stack(g_adaln_w),
        jnp.stack(g_adaln_b),
        summed[0],
        small[0],
        small[1],
        summed[1],
        small[2],
        summed[2],
        small[3],
        summed[3],
        small[4],
    )


def solution(mesh):
    in_specs = (
        P(("dp", "pair"), None, None),
        P(("dp", "pair"), None),
        P(("dp", "pair"), None, None),
        P(None, ("dp", "pair"), None),
        P(None, ("dp", "pair")),
        P(None, ("dp", "pair"), None),
        P(None, ("dp", "pair")),
        P(None, ("dp", "pair")),
        P(None, ("dp", "pair"), None),
        P(None, ("dp", "pair")),
        P(None, ("dp", "pair"), None),
        P(None, ("dp", "pair")),
        P(None, ("dp", "pair"), None),
        P(None, ("dp", "pair")),
    )
    out_specs = (
        P(("dp", "pair"), None, None),
        P(("dp", "pair"), None, None),
        P(("dp", "pair"), None),
        P(None, ("dp", "pair"), None),
        P(None, ("dp", "pair")),
        P(None, ("dp", "pair"), None),
        P(None, ("dp", "pair")),
        P(None, ("dp", "pair")),
        P(None, ("dp", "pair"), None),
        P(None, ("dp", "pair")),
        P(None, ("dp", "pair"), None),
        P(None, ("dp", "pair")),
        P(None, ("dp", "pair"), None),
        P(None, ("dp", "pair")),
    )
    return jax.shard_map(
        on_device, mesh=mesh, in_specs=in_specs, out_specs=out_specs, check_vma=False
    )
```
